256 devices in a mesh: depth: 16 (over z, y_hi), lat: 16 (over y_lo, x, core).
Axes of the slice: x: 4, y: 4 (y_hi: 2, y_lo: 2; y = y_hi * 2 + y_lo), z: 8, core: 2. Of those that a mesh axis runs over, the one named last changes fastest.
Arguments:
- object_slices: float32 [16, 2, 2048, 2048], P('depth', None, 'lat'), as said below
- probe: float32 [2, 2, 256, 256], replicated, may hold values from -2.7 to 2.7
- positions: int32 [64, 2], P('lat'), may hold values from 0 to 2047, as said below
- measured: float32 [64, 256, 256], P('lat'), may hold values from 0 to 0.8
Outputs:
- object_grad: float32 [16, 2, 2048, 2048], P('depth', None, 'lat')
The draws below stay inside these ranges and needn't reach their ends.
Inputs may be any that keep to these rules, and one draw needn't show every extreme that they name: Rows 4 l ... 4 l + 3 are the positions of lat index l: their row offset lies in [l * 128, (l + 1) * 128) and their column offset in [0, 1792]. `object_slices`: each cell's magnitude, sqrt(real part squared plus imaginary part squared), lies between 0.9 and 1.
All inputs are finite; a program needn't handle non-finite values.
Results may differ from the reference program's by a relative error of at most 0.039.
Values may be sent and summed in bfloat16 or wider, within the bound.
No kernel may reach another device: no remote copies, remote signals or barrier semaphores. Data moves between devices by JAX's collectives and lax.ppermute only.
A program may use at most 64 MiB of HBM per device.

```python
import math
import jax
import jax.numpy as jnp
from jax import lax

PROBE = 256
MODES = 2
POS_DEV = 4
COLS = 2048
TILE = 128
NX = 2048
SLICES = 16
POS_TOTAL = 64


def draw_object_slices(key, part):
    mag_key, phase_key = jax.random.split(key)
    shape = (SLICES, NX, COLS)
    magnitude = jax.random.uniform(mag_key, shape, jnp.float32, 0.9, 1.0)
    phase_angle = jax.random.uniform(phase_key, shape, jnp.float32, -0.6, 0.6)
    return jnp.stack([magnitude * jnp.cos(phase_angle), magnitude * jnp.sin(phase_angle)], axis=1)


def draw_positions(key, part):
    row_key, col_key = jax.random.split(key)
    slots = jnp.arange(POS_TOTAL, dtype=jnp.int32)
    owner = slots // POS_DEV
    within = slots % POS_DEV
    spacing = (COLS - PROBE) // POS_DEV
    row_jitter = jax.random.randint(row_key, (POS_TOTAL,), 0, TILE, dtype=jnp.int32)
    col_jitter = jax.random.randint(col_key, (POS_TOTAL,), 0, spacing + 1, dtype=jnp.int32)
    row_offset = owner * TILE + row_jitter
    col_offset = within * spacing + col_jitter
    row_offset = row_offset.at[0].set(0).at[POS_TOTAL - 1].set(NX - 1)
    col_offset = col_offset.at[0].set(0).at[POS_TOTAL - 1].set(COLS - PROBE)
    return jnp.stack([row_offset, col_offset], axis=1).astype(jnp.int32)


def level_of(stream_key, dims, shards, smallest, largest):
    def one(position, parts):
        draws = jax.random.uniform(jax.random.fold_in(jax.random.fold_in(stream_key, 6), position), (parts,), jnp.float32, smallest / len(shards), largest / len(shards))
        return jnp.repeat(jnp.exp(draws), dims[position] // parts).reshape((-1,) + (1,) * (len(dims) - position - 1))

    gain = one(*shards[0])
    for cut in shards[1:]:
        gain = gain * one(*cut)
    return gain


def scatter_about(own_key, dims, deviation, limit, kind=jnp.bfloat16):
    return jnp.clip(deviation * jax.random.normal(own_key, dims, jnp.float32), -limit, limit).astype(kind)


def setup_inputs(seed: int = 0) -> dict:
    keys = jax.random.split(jax.random.key(seed), 5)
    object_slices = draw_object_slices(jax.random.fold_in(keys[4], 71), 0)
    probe = scatter_about(keys[1], (MODES, 2, PROBE, PROBE), 0.45, 2.7, jnp.float32)
    positions = draw_positions(jax.random.fold_in(keys[4], 71), 0)
    measured = jnp.clip(0.8 * jax.random.uniform(keys[3], (POS_TOTAL, PROBE, PROBE), jnp.float32) ** level_of(keys[3], (POS_TOTAL, PROBE, PROBE), ((0, 16),), -0.2, 0.2), 0.0, 0.8)
    return dict(object_slices=object_slices, probe=probe, positions=positions, measured=measured)


fresnel = 0.5

def stack_block(real_part, imag_part):
    return jnp.stack([jnp.stack([real_part, -imag_part]), jnp.stack([imag_part, real_part])]).astype(jnp.float32)

def make_tables(pixels):
    highest = lax.Precision.HIGHEST
    steps_idx = jnp.arange(pixels, dtype=jnp.int32)
    product = steps_idx[:, None] * steps_idx[None, :] % pixels
    angle = 2.0 * math.pi / pixels * product.astype(jnp.float32)
    scale = 1.0 / math.sqrt(pixels)
    d_real = jnp.cos(angle) * scale
    d_imag = -jnp.sin(angle) * scale
    freq = jnp.where(steps_idx < pixels // 2, steps_idx, steps_idx - pixels).astype(jnp.float32)
    theta = math.pi * fresnel / pixels * freq * freq
    h_real = jnp.cos(theta)
    h_imag = -jnp.sin(theta)
    a_real = d_real * h_real[None, :] + d_imag * h_imag[None, :]
    a_imag = d_real * h_imag[None, :] - d_imag * h_real[None, :]
    k_real = jnp.dot(a_real, d_real, precision=highest) - jnp.dot(a_imag, d_imag, precision=highest)
    k_imag = jnp.dot(a_real, d_imag, precision=highest) + jnp.dot(a_imag, d_real, precision=highest)
    return (stack_block(k_real, k_imag), stack_block(k_real.T, -k_imag.T), stack_block(d_real, d_imag), stack_block(d_real, -d_imag))

def transform(table, wave):
    highest = lax.Precision.HIGHEST
    middle = jnp.einsum('srij,mrjk->msik', table, wave.astype(jnp.float32), precision=highest)
    return jnp.einsum('mrik,srlk->msil', middle, table, precision=highest)

def multiply(object_patch, wave_in):
    real_part = object_patch[0] * wave_in[:, 0] - object_patch[1] * wave_in[:, 1]
    imag_part = object_patch[0] * wave_in[:, 1] + object_patch[1] * wave_in[:, 0]
    return jnp.stack([real_part, imag_part], axis=1)

def conj_multiply(object_patch, wave_in):
    real_part = object_patch[0] * wave_in[:, 0] + object_patch[1] * wave_in[:, 1]
    imag_part = object_patch[0] * wave_in[:, 1] - object_patch[1] * wave_in[:, 0]
    return jnp.stack([real_part, imag_part], axis=1)

def conj_sum(wave_in, grad_lit):
    real_part = wave_in[:, 0] * grad_lit[:, 0] + wave_in[:, 1] * grad_lit[:, 1]
    imag_part = wave_in[:, 0] * grad_lit[:, 1] - wave_in[:, 1] * grad_lit[:, 0]
    return jnp.stack([lax.optimization_barrier(jnp.sum(real_part, axis=0)), lax.optimization_barrier(jnp.sum(imag_part, axis=0))])

def reference(object_slices, probe, positions, measured):
    pixels = PROBE
    prop_table, prop_adjoint, far_table, far_adjoint = make_tables(pixels)
    offsets = jnp.arange(pixels, dtype=jnp.int32)

    def one_position(grad_total, inputs):
        place, target = inputs
        rows = ((place[0] + offsets) % NX).astype(jnp.int32)
        cols = (place[1] + offsets).astype(jnp.int32)
        patches = object_slices[:, :, rows[:, None], cols[None, :]]

        def forward(wave_in, patch_block):
            lit_wave = multiply(patch_block, wave_in.astype(jnp.float32))
            return (transform(prop_table, lit_wave).astype(jnp.bfloat16), wave_in)
        last_wave, incidents = lax.scan(forward, probe.astype(jnp.bfloat16), patches)
        far_wave = transform(far_table, last_wave)
        residual = lax.optimization_barrier(jnp.sum(far_wave * far_wave, axis=(0, 1))) - target
        seed_wave = transform(far_adjoint, residual * far_wave).astype(jnp.bfloat16)

        def backward(grad_in, pieces):
            patch_block, in_wave = pieces
            grad_lit = transform(prop_adjoint, grad_in)
            grad_term = conj_sum(in_wave.astype(jnp.float32), grad_lit)
            return (conj_multiply(patch_block, grad_lit).astype(jnp.bfloat16), grad_term)
        _, terms = lax.scan(backward, seed_wave, (patches, incidents), reverse=True)
        grad_total = grad_total.at[:, :, rows[:, None], cols[None, :]].add(terms)
        return (grad_total, None)
    start = jnp.zeros(object_slices.shape, jnp.float32)
    grad_total, _ = lax.scan(one_position, start, (positions, measured))
    return grad_total
```

```python
import functools

import jax
import jax.numpy as jnp
import numpy as np
from jax import lax
from jax.experimental import pallas as pl
from jax.experimental.pallas import tpu as pltpu
from jax.sharding import PartitionSpec as P

BF = jnp.bfloat16
F32 = jnp.float32
ANY = pl.BlockSpec(memory_space=pl.ANY)
SMEM = pl.BlockSpec(memory_space=pltpu.MemorySpace.SMEM)
VMEM = pl.BlockSpec(memory_space=pltpu.MemorySpace.VMEM)


@functools.lru_cache
def base_tables(n):
    k = np.arange(n)
    d = np.exp(-2j * np.pi * ((k[:, None] * k[None, :]) % n) / n) / np.sqrt(n)
    q = np.where(k < n // 2, k, k - n).astype(np.float64)
    h = np.exp(-1j * np.pi * 0.5 * q * q / n)
    prop = (np.conj(d) * h[None, :]) @ d
    return np.stack([prop.real, prop.imag, d.real, d.imag]).astype(np.float32)


def tables_kernel(scales, base, out, *, n, slices):
    s = pl.program_id(0)
    which = jnp.where(s < slices, 0, 2)
    re = base[which]
    im = base[which + 1]
    for side, sign in ((0, 1.0), (1, -1.0)):
        scale = scales[side, s]
        a = (re * scale).astype(BF)
        b = im * (scale * sign)
        out[0, side, 0:n, 0:n] = a
        out[0, side, n:2 * n, n:2 * n] = a
        out[0, side, 0:n, n:2 * n] = (-b).astype(BF)
        out[0, side, n:2 * n, 0:n] = b.astype(BF)


def make_tables(n, slices):
    a = 2.0 ** ((np.arange(slices) + 0.5) / slices)
    scales = np.concatenate([np.stack([a, 1.0 / a]), np.ones((2, 1))], axis=1).astype(np.float32)
    return pl.pallas_call(
        functools.partial(tables_kernel, n=n, slices=slices),
        grid=(slices + 1,),
        out_shape=jax.ShapeDtypeStruct((slices + 1, 2, 2 * n, 2 * n), BF),
        in_specs=[SMEM, pl.BlockSpec((4, n, n), lambda s: (0, 0, 0))],
        out_specs=pl.BlockSpec((1, 2, 2 * n, 2 * n), lambda s: (s, 0, 0, 0)),
    )(jnp.asarray(scales), jnp.asarray(base_tables(n)))


def chain_kernel(info, probe, target, m0, m1, m2, m3, tabs_hbm, out_hbm,
                 patch, tabs, inc, cur, lhs, mid, outv, psem, tsem, osem, *, n, slices):
    team, inner = info[1], info[2]
    messages = (m0, m1, m2, m3)
    per = slices // 4

    def patch_copy(s):
        rel = lax.rem(s // per - team + 4, 4)
        entry = jnp.bitwise_xor(lax.rem(s, per), inner)
        return rel, entry

    def table_copy(s):
        return pltpu.make_async_copy(tabs_hbm.at[s], tabs.at[s], tsem.at[s])

    def out_copy(s):
        return pltpu.make_async_copy(outv.at[s], out_hbm.at[s], osem.at[s])

    def to_lhs(m, re, im):
        lhs[0:n, m * n:(m + 1) * n] = re.astype(BF)
        lhs[n:2 * n, m * n:(m + 1) * n] = im.astype(BF)

    def transform(left, right):
        for m in range(2):
            u = jnp.dot(left, lhs[:, m * n:(m + 1) * n], preferred_element_type=F32).astype(BF)
            mid[m * n:(m + 1) * n, 0:n] = u[0:n]
            mid[m * n:(m + 1) * n, n:2 * n] = u[n:2 * n]
        return jnp.dot(mid[...], right, preferred_element_type=F32)

    @pl.when(info[0] == 1)
    def _():
        for s in range(slices):
            table_copy(s).start()
            rel, entry = patch_copy(s)
            for r in range(4):
                @pl.when(rel == r)
                def _():
                    pltpu.make_async_copy(messages[r].at[entry], patch.at[s], psem.at[s]).start()
        table_copy(slices).start()
        for m in range(2):
            for c in range(2):
                x = pltpu.roll(probe[m, c], info[3], 0)
                x = pltpu.roll(x, info[4], 1)
                cur[m * n:(m + 1) * n, c * n:(c + 1) * n] = x.astype(BF).astype(F32)

        def forward(s, carry):
            table_copy(s).wait()
            pltpu.make_async_copy(m0.at[0], patch.at[s], psem.at[s]).wait()
            pr = patch[s, 0].astype(F32)
            pi = patch[s, 1].astype(F32)
            for m in range(2):
                wr = cur[m * n:(m + 1) * n, 0:n]
                wi = cur[m * n:(m + 1) * n, n:2 * n]
                to_lhs(m, pr * wr - pi * wi, pr * wi + pi * wr)
            inc[s] = cur[...].astype(BF)
            cur[...] = transform(tabs[s, 0], tabs[s, 1])
            return carry

        lax.fori_loop(0, slices, forward, 0)
        table_copy(slices).wait()
        for m in range(2):
            to_lhs(m, cur[m * n:(m + 1) * n, 0:n], cur[m * n:(m + 1) * n, n:2 * n])
        cur[...] = transform(tabs[slices, 0], tabs[slices, 1])
        f = [[cur[m * n:(m + 1) * n, c * n:(c + 1) * n] for c in range(2)] for m in range(2)]
        resid = (f[0][0] * f[0][0] + f[0][1] * f[0][1]) + (f[1][0] * f[1][0] + f[1][1] * f[1][1]) - target[...]
        for m in range(2):
            to_lhs(m, resid * f[m][0], resid * f[m][1])
        cur[...] = transform(tabs[slices, 1], tabs[slices, 0])
        for m in range(2):
            to_lhs(m, cur[m * n:(m + 1) * n, 0:n], cur[m * n:(m + 1) * n, n:2 * n])

        def backward(back, carry):
            s = slices - 1 - back
            cur[...] = transform(tabs[s, 1], tabs[s, 0])
            pr = patch[s, 0].astype(F32)
            pi = patch[s, 1].astype(F32)
            tr = jnp.zeros((n, n), F32)
            ti = jnp.zeros((n, n), F32)
            for m in range(2):
                gr = cur[m * n:(m + 1) * n, 0:n]
                gi = cur[m * n:(m + 1) * n, n:2 * n]
                wr = inc[s, m * n:(m + 1) * n, 0:n].astype(F32)
                wi = inc[s, m * n:(m + 1) * n, n:2 * n].astype(F32)
                tr += wr * gr + wi * gi
                ti += wr * gi - wi * gr
                to_lhs(m, pr * gr + pi * gi, pr * gi - pi * gr)
            outv[s, 0] = tr.astype(BF)
            outv[s, 1] = ti.astype(BF)
            out_copy(s).start()
            return carry

        lax.fori_loop(0, slices, backward, 0)
        for s in range(slices):
            out_copy(s).wait()


def chain(info, probe, target, messages, tables):
    n = target.shape[-1]
    slices = tables.shape[0] - 1
    return pl.pallas_call(
        functools.partial(chain_kernel, n=n, slices=slices),
        out_shape=jax.ShapeDtypeStruct((slices, 2, n, n), BF),
        in_specs=[SMEM, VMEM, VMEM] + [ANY] * 5,
        out_specs=ANY,
        scratch_shapes=[
            pltpu.VMEM((slices, 2, n, n), BF),
            pltpu.VMEM((slices + 1, 2, 2 * n, 2 * n), BF),
            pltpu.VMEM((slices, 2 * n, 2 * n), BF),
            pltpu.VMEM((2 * n, 2 * n), F32),
            pltpu.VMEM((2 * n, 2 * n), BF),
            pltpu.VMEM((2 * n, 2 * n), BF),
            pltpu.VMEM((slices, 2, n, n), BF),
            pltpu.SemaphoreType.DMA((slices,)),
            pltpu.SemaphoreType.DMA((slices + 1,)),
            pltpu.SemaphoreType.DMA((slices,)),
        ],
        compiler_params=pltpu.CompilerParams(vmem_limit_bytes=58 << 20),
    )(info, probe, target, *messages, tables)


def window(ref, lead, offset, n):
    width = ref.shape[-1]
    start = pl.multiple_of((offset // n) * n, n)
    after = pl.multiple_of(jnp.minimum(start + n, width - n), n)
    lane = lax.broadcasted_iota(jnp.int32, (ref.shape[-2], n), 1)
    first = ref[lead, :, pl.ds(start, n)].astype(F32)
    second = ref[lead, :, pl.ds(after, n)].astype(F32)
    return jnp.where(lane >= offset % n, first, second)


def own_windows_kernel(places, tile, tile_bf, wins, *, n):
    tile_bf[...] = tile[...].astype(BF)
    for p in range(wins.shape[0]):
        for c in range(2):
            wins[p, c] = window(tile, c, places[p, 1], n).astype(BF)


def own_windows(places, tile, n):
    count = places.shape[0]
    return pl.pallas_call(
        functools.partial(own_windows_kernel, n=n),
        out_shape=(jax.ShapeDtypeStruct(tile.shape, BF), jax.ShapeDtypeStruct((count, 2, tile.shape[1], n), BF)),
        in_specs=[SMEM, VMEM],
        out_specs=(VMEM, VMEM),
        compiler_params=pltpu.CompilerParams(vmem_limit_bytes=40 << 20),
    )(places, tile)


def merge_kernel(places, behind, tile, ahead, out, *, n):
    rows = tile.shape[1]
    row = lax.broadcasted_iota(jnp.int32, (rows, n), 0)
    for p in range(out.shape[0]):
        for c in range(2):
            far = window(ahead, c, places[p, 1], n)
            near = behind[p, c].astype(F32)
            out[p, c, 0:rows] = jnp.where(row >= places[p, 0] % rows, near, far).astype(BF)
            out[p, c, rows:2 * rows] = window(tile, c, places[p, 1], n).astype(BF)


def merge(places, behind, tile, ahead, n):
    count = places.shape[0]
    return pl.pallas_call(
        functools.partial(merge_kernel, n=n),
        out_shape=jax.ShapeDtypeStruct((count, 2, 2 * tile.shape[1], n), BF),
        in_specs=[SMEM, VMEM, VMEM, VMEM],
        out_specs=VMEM,
        compiler_params=pltpu.CompilerParams(vmem_limit_bytes=40 << 20),
    )(places, behind, tile, ahead)


def gather_kernel(own_places, mid_places, far_places, from_own, from_mid, from_far, out, *, n):
    rows = out.shape[1]
    width = out.shape[-1]
    row = lax.broadcasted_iota(jnp.int32, (rows, n), 0)
    lane = lax.broadcasted_iota(jnp.int32, (rows, n), 1)
    out[...] = jnp.zeros_like(out)
    for places, terms, kind in ((own_places, from_own, 0), (mid_places, from_mid, 1), (far_places, from_far, 2)):
        for p in range(places.shape[0]):
            shift = places[p, 0] % rows
            offset = places[p, 1]
            start = pl.multiple_of((offset // n) * n, n)
            after = pl.multiple_of(jnp.minimum(start + n, width - n), n)
            for c in range(2):
                if kind == 1:
                    term = terms[p, c, rows:2 * rows].astype(F32)
                else:
                    term = terms[p, c].astype(F32)
                    keep = row >= shift if kind == 0 else row < shift
                    term = jnp.where(keep, term, 0.0)
                here = lane >= offset % n
                out[c, :, pl.ds(start, n)] += jnp.where(here, term, 0.0)
                out[c, :, pl.ds(after, n)] += jnp.where(here, 0.0, term)


def gather_terms(own_places, mid_places, far_places, from_own, from_mid, from_far, rows, width):
    n = from_mid.shape[-1]
    return pl.pallas_call(
        functools.partial(gather_kernel, n=n),
        out_shape=jax.ShapeDtypeStruct((2, rows, width), F32),
        in_specs=[SMEM, SMEM, SMEM, VMEM, VMEM, VMEM],
        out_specs=VMEM,
        compiler_params=pltpu.CompilerParams(vmem_limit_bytes=40 << 20),
    )(own_places, mid_places, far_places, from_own, from_mid, from_far)


def shifted(block, distance):
    size = lax.axis_size("lat")
    return lax.ppermute(block, "lat", [(i, (i + distance) % size) for i in range(size)])


def team_of(position, lat):
    return (position + 2 * (lat % 2)) % 4


def permute(block, route):
    depth, lat = lax.axis_size("depth"), lax.axis_size("lat")
    pairs = []
    for d in range(depth):
        for m in range(lat):
            to = route(d, m)
            if to is not None:
                pairs.append((d * lat + m, to * lat + m))
    return lax.ppermute(block, ("depth", "lat"), pairs)


def pick(block, index):
    return lax.dynamic_index_in_dim(block, index, 0, False)


def on_device(object_slices, probe, positions, measured):
    n = probe.shape[-1]
    rows, width = object_slices.shape[2:]
    depth_size = lax.axis_size("depth")
    d = lax.axis_index("depth")
    m = lax.axis_index("lat")
    team, inner = d // 4, d % 4
    tile = object_slices[0]

    mid_places = shifted(positions, 1)
    tile_bf, mine = own_windows(positions, tile, n)
    ahead = shifted(tile_bf, -1)
    behind = shifted(mine, 1)
    target = shifted(pick(measured, inner), 1)
    patches = merge(mid_places, behind, tile_bf, ahead, n)

    parts = [pick(patches, inner)]
    for k in (1, 2, 3):
        parts.append(permute(pick(patches, inner ^ k), lambda a, b: (a ^ k)))
    message = jnp.stack(parts)
    messages = [message]
    for k in (1, 2, 3):
        def route(a, b):
            goal = team_of(a % 4, b)
            return goal * 4 + a % 4 if (goal + k) % 4 == a // 4 else None
        messages.append(permute(message, route))

    home = team_of(inner, m)
    place = pick(mid_places, inner)
    info = jnp.stack([(home == team).astype(jnp.int32), team, inner, place[0] % rows, place[1] % n]).astype(jnp.int32)
    tables = make_tables(n, depth_size)
    terms = chain(info, probe, target, messages, tables)

    terms = terms.reshape(4, 4, 2, n, n)
    block = pick(terms, team)
    for k in (1, 2, 3):
        def route(a, b):
            return ((a // 4 + k) % 4) * 4 + a % 4 if team_of(a % 4, b) == a // 4 else None
        got = permute(pick(terms, (team + k) % 4), route)
        block = jnp.where((home + k) % 4 == team, got, block)
    collected = jnp.zeros((4, 2, n, n), BF)
    collected = lax.dynamic_update_index_in_dim(collected, pick(block, inner), inner, 0)
    for k in (1, 2, 3):
        got = permute(pick(block, inner ^ k), lambda a, b: (a ^ k))
        collected = lax.dynamic_update_index_in_dim(collected, got, inner ^ k, 0)

    mixed = collected[:, :, :rows]
    from_own = shifted(mixed, -1)
    from_far = shifted(mixed, 1)
    far_places = shifted(positions, 2)
    total = gather_terms(positions, mid_places, far_places, from_own, collected, from_far, rows, width)
    return total[None]


def solution(mesh):
    return jax.shard_map(
        on_device,
        mesh=mesh,
        in_specs=(P("depth", None, "lat", None), P(), P("lat", None), P("lat", None, None)),
        out_specs=P("depth", None, "lat", None),
        check_vma=False,
    )
```

```python
import functools

import jax
import jax.numpy as jnp
import numpy as np
from jax import lax
from jax.experimental import pallas as pl
from jax.experimental.pallas import tpu as pltpu
from jax.sharding import PartitionSpec as P

BF = jnp.bfloat16
F32 = jnp.float32
ANY = pl.BlockSpec(memory_space=pl.ANY)
SMEM = pl.BlockSpec(memory_space=pltpu.MemorySpace.SMEM)
VMEM = pl.BlockSpec(memory_space=pltpu.MemorySpace.VMEM)


@functools.lru_cache
def base_tables(n):
    k = np.arange(n)
    d = np.exp(-2j * np.pi * ((k[:, None] * k[None, :]) % n) / n) / np.sqrt(n)
    q = np.where(k < n // 2, k, k - n).astype(np.float64)
    h = np.exp(-1j * np.pi * 0.5 * q * q / n)
    prop = (np.conj(d) * h[None, :]) @ d
    return np.stack([prop.real, prop.imag, d.real, d.imag]).astype(np.float32)


def tables_kernel(scales, base, out, *, n, slices):
    s = pl.program_id(0)
    which = jnp.where(s < slices, 0, 2)
    re = base[which]
    im = base[which + 1]
    for side, sign in ((0, 1.0), (1, -1.0)):
        scale = scales[side, s]
        a = (re * scale).astype(BF)
        b = im * (scale * sign)
        out[0, side, 0:n, 0:n] = a
        out[0, side, n:2 * n, n:2 * n] = a
        out[0, side, 0:n, n:2 * n] = (-b).astype(BF)
        out[0, side, n:2 * n, 0:n] = b.astype(BF)


def make_tables(n, slices):
    a = 2.0 ** ((np.arange(slices) + 0.5) / slices)
    scales = np.concatenate([np.stack([a, 1.0 / a]), np.ones((2, 1))], axis=1).astype(np.float32)
    return pl.pallas_call(
        functools.partial(tables_kernel, n=n, slices=slices),
        grid=(slices + 1,),
        out_shape=jax.ShapeDtypeStruct((slices + 1, 2, 2 * n, 2 * n), BF),
        in_specs=[SMEM, pl.BlockSpec((4, n, n), lambda s: (0, 0, 0))],
        out_specs=pl.BlockSpec((1, 2, 2 * n, 2 * n), lambda s: (s, 0, 0, 0)),
    )(jnp.asarray(scales), jnp.asarray(base_tables(n)))


def chain_kernel(plan, places, probe, target, m0, m1, m2, m3, tabs_hbm, o0, o1, o2, o3,
                 patch, tabs, inc, cur, lhs, mid, outv, psem, tsem, osem, *, n, slices, rows):
    messages = (m0, m1, m2, m3)
    outs = (o0, o1, o2, o3)

    def table_copy(s):
        return pltpu.make_async_copy(tabs_hbm.at[s], tabs.at[s], tsem.at[s])

    def to_lhs(m, re, im):
        lhs[0:n, m * n:(m + 1) * n] = re.astype(BF)
        lhs[n:2 * n, m * n:(m + 1) * n] = im.astype(BF)

    def transform(left, right):
        for m in range(2):
            u = jnp.dot(left, lhs[:, m * n:(m + 1) * n], preferred_element_type=F32).astype(BF)
            mid[m * n:(m + 1) * n, 0:n] = u[0:n]
            mid[m * n:(m + 1) * n, n:2 * n] = u[n:2 * n]
        return jnp.dot(mid[...], right, preferred_element_type=F32)

    @pl.when(plan[HANDLER] == 1)
    def _():
        for s in range(slices):
            table_copy(s).start()
            for r in range(4):
                @pl.when(plan[REL + s] == r)
                def _():
                    pltpu.make_async_copy(messages[r].at[plan[ENTRY + s]], patch.at[s], psem.at[s]).start()
        table_copy(slices).start()
        row_shift = lax.rem(places[plan[POSITION], 0], rows)
        col_shift = lax.rem(places[plan[POSITION], 1], n)
        for m in range(2):
            for c in range(2):
                x = pltpu.roll(probe[m, c], row_shift, 0)
                x = pltpu.roll(x, col_shift, 1)
                cur[m * n:(m + 1) * n, c * n:(c + 1) * n] = x.astype(BF).astype(F32)

        def forward(s, carry):
            table_copy(s).wait()
            pltpu.make_async_copy(m0.at[0], patch.at[s], psem.at[s]).wait()
            pr = patch[s, 0].astype(F32)
            pi = patch[s, 1].astype(F32)
            for m in range(2):
                wr = cur[m * n:(m + 1) * n, 0:n]
                wi = cur[m * n:(m + 1) * n, n:2 * n]
                to_lhs(m, pr * wr - pi * wi, pr * wi + pi * wr)
            inc[s] = cur[...].astype(BF)
            cur[...] = transform(tabs[s, 0], tabs[s, 1])
            return carry

        lax.fori_loop(0, slices, forward, 0)
        table_copy(slices).wait()
        for m in range(2):
            to_lhs(m, cur[m * n:(m + 1) * n, 0:n], cur[m * n:(m + 1) * n, n:2 * n])
        cur[...] = transform(tabs[slices, 0], tabs[slices, 1])
        f = [[cur[m * n:(m + 1) * n, c * n:(c + 1) * n] for c in range(2)] for m in range(2)]
        resid = (f[0][0] * f[0][0] + f[0][1] * f[0][1]) + (f[1][0] * f[1][0] + f[1][1] * f[1][1]) - target[...]
        for m in range(2):
            to_lhs(m, resid * f[m][0], resid * f[m][1])
        cur[...] = transform(tabs[slices, 1], tabs[slices, 0])
        for m in range(2):
            to_lhs(m, cur[m * n:(m + 1) * n, 0:n], cur[m * n:(m + 1) * n, n:2 * n])

        def backward(back, carry):
            s = slices - 1 - back
            cur[...] = transform(tabs[s, 1], tabs[s, 0])
            pr = patch[s, 0].astype(F32)
            pi = patch[s, 1].astype(F32)
            tr = jnp.zeros((n, n), F32)
            ti = jnp.zeros((n, n), F32)
            for m in range(2):
                gr = cur[m * n:(m + 1) * n, 0:n]
                gi = cur[m * n:(m + 1) * n, n:2 * n]
                wr = inc[s, m * n:(m + 1) * n, 0:n].astype(F32)
                wi = inc[s, m * n:(m + 1) * n, n:2 * n].astype(F32)
                tr += wr * gr + wi * gi
                ti += wr * gi - wi * gr
                to_lhs(m, pr * gr + pi * gi, pr * gi - pi * gr)
            outv[s, 0] = tr.astype(BF)
            outv[s, 1] = ti.astype(BF)
            for r in range(4):
                @pl.when(plan[REL + s] == r)
                def _():
                    pltpu.make_async_copy(outv.at[s], outs[r].at[plan[ENTRY + s]], osem.at[s]).start()
            return carry

        lax.fori_loop(0, slices, backward, 0)
        for s in range(slices):
            pltpu.make_async_copy(outv.at[s], o0.at[0], osem.at[s]).wait()


def chain(plan, places, probe, target, messages, tables, rows):
    n = target.shape[-1]
    slices = tables.shape[0] - 1
    piece = jax.ShapeDtypeStruct(messages[0].shape, BF)
    return pl.pallas_call(
        functools.partial(chain_kernel, n=n, slices=slices, rows=rows),
        out_shape=(piece,) * 4,
        in_specs=[SMEM, SMEM, VMEM, VMEM] + [ANY] * 5,
        out_specs=(ANY,) * 4,
        scratch_shapes=[
            pltpu.VMEM((slices, 2, n, n), BF),
            pltpu.VMEM((slices + 1, 2, 2 * n, 2 * n), BF),
            pltpu.VMEM((slices, 2 * n, 2 * n), BF),
            pltpu.VMEM((2 * n, 2 * n), F32),
            pltpu.VMEM((2 * n, 2 * n), BF),
            pltpu.VMEM((2 * n, 2 * n), BF),
            pltpu.VMEM((slices, 2, n, n), BF),
            pltpu.SemaphoreType.DMA((slices,)),
            pltpu.SemaphoreType.DMA((slices + 1,)),
            pltpu.SemaphoreType.DMA((slices,)),
        ],
        compiler_params=pltpu.CompilerParams(vmem_limit_bytes=58 << 20),
    )(plan, places, probe, target, *messages, tables)


def window(ref, lead, offset, n):
    width = ref.shape[-1]
    start = pl.multiple_of((offset // n) * n, n)
    after = pl.multiple_of(jnp.minimum(start + n, width - n), n)
    lane = lax.broadcasted_iota(jnp.int32, (ref.shape[-2], n), 1)
    first = ref[lead, :, pl.ds(start, n)].astype(F32)
    second = ref[lead, :, pl.ds(after, n)].astype(F32)
    return jnp.where(lane >= offset % n, first, second)


def own_windows_kernel(places, tile, tile_bf, wins, *, n):
    tile_bf[...] = tile[...].astype(BF)
    for p in range(wins.shape[0]):
        for c in range(2):
            wins[p, c] = window(tile, c, places[p, 1], n).astype(BF)


def own_windows(places, tile, n):
    count = places.shape[0]
    return pl.pallas_call(
        functools.partial(own_windows_kernel, n=n),
        out_shape=(jax.ShapeDtypeStruct(tile.shape, BF), jax.ShapeDtypeStruct((count, 2, tile.shape[1], n), BF)),
        in_specs=[SMEM, VMEM],
        out_specs=(VMEM, VMEM),
        compiler_params=pltpu.CompilerParams(vmem_limit_bytes=40 << 20),
    )(places, tile)


def merge_kernel(plan, places, behind, tile, ahead, *outs, n):
    rows = tile.shape[1]
    row = lax.broadcasted_iota(jnp.int32, (rows, n), 0)
    for k in range(4):
        p = plan[ORDER + k]
        for c in range(2):
            far = window(ahead, c, places[p, 1], n)
            near = behind[p, c].astype(F32)
            outs[k][c, 0:rows] = jnp.where(row >= places[p, 0] % rows, near, far).astype(BF)
            outs[k][c, rows:2 * rows] = window(tile, c, places[p, 1], n).astype(BF)


def merge(plan, places, behind, tile, ahead, n):
    return pl.pallas_call(
        functools.partial(merge_kernel, n=n),
        out_shape=(jax.ShapeDtypeStruct((2, 2 * tile.shape[1], n), BF),) * 4,
        in_specs=[SMEM, SMEM, VMEM, VMEM, VMEM],
        out_specs=(VMEM,) * 4,
        compiler_params=pltpu.CompilerParams(vmem_limit_bytes=40 << 20),
    )(plan, places, behind, tile, ahead)


def gather_kernel(plan, own_places, mid_places, far_places, from_own, m0, m1, m2, m3, from_far, out, *, n):
    rows = out.shape[1]
    width = out.shape[-1]
    row = lax.broadcasted_iota(jnp.int32, (rows, n), 0)
    lane = lax.broadcasted_iota(jnp.int32, (rows, n), 1)
    out[...] = jnp.zeros_like(out)
    mids = (m0, m1, m2, m3)
    for places, kind, order in ((own_places, 0, OTHER), (mid_places, 1, ORDER), (far_places, 2, OTHER)):
        for k in range(4):
            p = plan[order + k]
            shift = places[p, 0] % rows
            offset = places[p, 1]
            start = pl.multiple_of((offset // n) * n, n)
            after = pl.multiple_of(jnp.minimum(start + n, width - n), n)
            for c in range(2):
                if kind == 0:
                    term = jnp.where(row >= shift, from_own[k, c].astype(F32), 0.0)
                elif kind == 1:
                    term = mids[k][c, rows:2 * rows].astype(F32)
                else:
                    term = jnp.where(row < shift, from_far[k, c].astype(F32), 0.0)
                here = lane >= offset % n
                out[c, :, pl.ds(start, n)] += jnp.where(here, term, 0.0)
                out[c, :, pl.ds(after, n)] += jnp.where(here, 0.0, term)


def gather_terms(plan, own_places, mid_places, far_places, from_own, mids, from_far, rows, width):
    n = from_own.shape[-1]
    return pl.pallas_call(
        functools.partial(gather_kernel, n=n),
        out_shape=jax.ShapeDtypeStruct((2, rows, width), F32),
        in_specs=[SMEM] * 4 + [VMEM] * 6,
        out_specs=VMEM,
        compiler_params=pltpu.CompilerParams(vmem_limit_bytes=40 << 20),
    )(plan, own_places, mid_places, far_places, from_own, *mids, from_far)


def shifted(block, distance):
    size = lax.axis_size("lat")
    return lax.ppermute(block, "lat", [(i, (i + distance) % size) for i in range(size)])


HANDLER, POSITION, SOURCE, ORDER, OTHER, REL, ENTRY = 0, 1, 2, 3, 7, 11, 27
GOAL = (((0, 0), (1, 1), (2, 0), (3, 1)), ((1, 2), (0, 3), (3, 2), (2, 3)))


def meet(c, team, j):
    goal, inner = GOAL[c][j]
    flip = inner ^ 2
    if c == 0:
        return inner if (team - goal) % 4 in (0, 1) else flip
    return inner if (team - goal) % 4 in (0, 3) else flip


def place_of(c, d):
    v = (d + 2 * c) % 16
    return v // 4, v % 4


def position_at(c, team, inner):
    found = [j for j in range(4) if meet(c, team, j) == inner]
    assert len(found) == 1
    return found[0]


def device_of(c, team, inner):
    return (4 * team + inner - 2 * c) % 16


@functools.lru_cache
def make_plan():
    out = np.zeros((2, 16, 48), np.int32)
    for c in range(2):
        for d in range(16):
            team, inner = place_of(c, d)
            j = position_at(c, team, inner)
            row = out[c, d]
            row[HANDLER] = GOAL[c][j] == (team, inner)
            row[POSITION] = j
            row[SOURCE] = (team - GOAL[c][j][0]) % 4
            other = place_of(1 - c, d)
            for k in range(4):
                row[ORDER + k] = position_at(c, team, inner ^ k)
                row[OTHER + k] = position_at(1 - c, other[0], other[1] ^ k)
            for s in range(16):
                there, at = place_of(c, s)
                row[REL + s] = (there - team) % 4
                row[ENTRY + s] = at ^ meet(c, there, j)
    return out


def permute(block, route):
    depth, lat = lax.axis_size("depth"), lax.axis_size("lat")
    pairs = []
    for d in range(depth):
        for m in range(lat):
            to = route(m % 2, *place_of(m % 2, d))
            if to is not None:
                pairs.append((d * lat + m, device_of(m % 2, *to) * lat + m))
    return lax.ppermute(block, ("depth", "lat"), pairs)


def within(block, k):
    return permute(block, lambda c, team, inner: (team, inner ^ k))


def towards(block, k):
    def route(c, team, inner):
        goal = GOAL[c][position_at(c, team, inner)]
        return goal if (team - goal[0]) % 4 == k else None
    return permute(block, route)


def away(block, k):
    def route(c, team, inner):
        j = position_at(c, team, inner)
        there = (team + k) % 4
        return (there, meet(c, there, j)) if GOAL[c][j] == (team, inner) else None
    return permute(block, route)


def on_device(object_slices, probe, positions, measured):
    n = probe.shape[-1]
    rows, width = object_slices.shape[2:]
    depth_size = lax.axis_size("depth")
    d = lax.axis_index("depth")
    m = lax.axis_index("lat")
    plan = lax.dynamic_slice(jnp.asarray(make_plan()), (m % 2, d, 0), (1, 1, 48)).reshape(48)
    tile = object_slices[0]

    mid_places = shifted(positions, 1)
    far_places = shifted(positions, 2)
    tile_bf, mine = own_windows(positions, tile, n)
    ahead = shifted(tile_bf, -1)
    behind = shifted(mine, 1)
    target = shifted(lax.dynamic_index_in_dim(measured, plan[OTHER], 0, False), 1)
    tables = make_tables(n, depth_size)
    mid_places, far_places, ahead, behind, target, tables = lax.optimization_barrier(
        (mid_places, far_places, ahead, behind, target, tables))
    parts = merge(plan, mid_places, behind, tile_bf, ahead, n)

    message = jnp.stack([parts[0]] + [within(parts[k], k) for k in (1, 2, 3)])
    messages = [message] + [towards(message, k) for k in (1, 2, 3)]
    terms = chain(plan, mid_places, probe, target, messages, tables, rows)

    block = terms[0]
    for k in (1, 2, 3):
        block = jnp.where(plan[SOURCE] == k, away(terms[k], k), block)
    mids = [block[0]] + [within(block[k], k) for k in (1, 2, 3)]

    mixed = jnp.stack([x[:, :rows] for x in mids])
    from_own = shifted(mixed, -1)
    from_far = shifted(mixed, 1)
    total = gather_terms(plan, positions, mid_places, far_places, from_own, mids, from_far, rows, width)
    return total[None]


def solution(mesh):
    return jax.shard_map(
        on_device,
        mesh=mesh,
        in_specs=(P("depth", None, "lat", None), P(), P("lat", None), P("lat", None, None)),
        out_specs=P("depth", None, "lat", None),
        check_vma=False,
    )
```

```python
import functools

import jax
import jax.numpy as jnp
import numpy as np
from jax import lax
from jax.experimental import pallas as pl
from jax.experimental.pallas import tpu as pltpu
from jax.sharding import PartitionSpec as P

BF = jnp.bfloat16
F32 = jnp.float32
ANY = pl.BlockSpec(memory_space=pl.ANY)
SMEM = pl.BlockSpec(memory_space=pltpu.MemorySpace.SMEM)
VMEM = pl.BlockSpec(memory_space=pltpu.MemorySpace.VMEM)


@functools.lru_cache
def base_tables(n):
    k = np.arange(n)
    d = np.exp(-2j * np.pi * ((k[:, None] * k[None, :]) % n) / n) / np.sqrt(n)
    q = np.where(k < n // 2, k, k - n).astype(np.float64)
    h = np.exp(-1j * np.pi * 0.5 * q * q / n)
    prop = (np.conj(d) * h[None, :]) @ d
    return np.stack([prop.real, prop.imag, d.real, d.imag]).astype(np.float32)


def tables_kernel(scales, base, out, *, n, slices):
    s = pl.program_id(0)
    which = jnp.where(s < slices, 0, 2)
    re = base[which]
    im = base[which + 1]
    for side, sign in ((0, 1.0), (1, -1.0)):
        scale = scales[side, s]
        a = (re * scale).astype(BF)
        b = im * (scale * sign)
        out[0, side, 0:n, 0:n] = a
        out[0, side, n:2 * n, n:2 * n] = a
        out[0, side, 0:n, n:2 * n] = (-b).astype(BF)
        out[0, side, n:2 * n, 0:n] = b.astype(BF)


def make_tables(n, slices):
    a = 2.0 ** ((np.arange(slices) + 0.5) / slices)
    scales = np.concatenate([np.stack([a, 1.0 / a]), np.ones((2, 1))], axis=1).astype(np.float32)
    return pl.pallas_call(
        functools.partial(tables_kernel, n=n, slices=slices),
        grid=(slices + 1,),
        out_shape=jax.ShapeDtypeStruct((slices + 1, 2, 2 * n, 2 * n), BF),
        in_specs=[SMEM, pl.BlockSpec((4, n, n), lambda s: (0, 0, 0))],
        out_specs=pl.BlockSpec((1, 2, 2 * n, 2 * n), lambda s: (s, 0, 0, 0)),
    )(jnp.asarray(scales), jnp.asarray(base_tables(n)))


def chain_kernel(plan, places, probe, target, *refs, n, slices, rows):
    near_in, far_in, tabs_hbm, near_out, far_out = refs[0:4], refs[4:8], refs[8], refs[9:13], refs[13:17]
    (patch, tabs, inc, lhs0, lhs1, mid0, mid1, outv, psem, tsem, osem) = refs[17:]
    lhs, mid = (lhs0, lhs1), (mid0, mid1)
    half = n // 2

    def table_copy(s):
        return pltpu.make_async_copy(tabs_hbm.at[s], tabs.at[s], tsem.at[s])

    def patch_wait(s):
        for h in range(2):
            pltpu.make_async_copy(near_in[0].at[0], patch.at[s, :, pl.ds(h * half, half)], psem.at[h, s]).wait()

    def put(m, re, im):
        lhs[m][0:n] = re.astype(BF)
        lhs[m][n:2 * n] = im.astype(BF)

    def first(m, left):
        u = jnp.dot(left, lhs[m][...], preferred_element_type=F32)
        mid[m][:, 0:n] = u[0:n].astype(BF)
        mid[m][:, n:2 * n] = u[n:2 * n].astype(BF)

    def second(m, right):
        v = jnp.dot(mid[m][...], right, preferred_element_type=F32)
        return v[:, 0:n], v[:, n:2 * n]

    def transform(left, right):
        first(0, left)
        first(1, left)
        return second(0, right), second(1, right)

    def enter(s, m, wr, wi):
        inc[s, m, 0] = wr.astype(BF)
        inc[s, m, 1] = wi.astype(BF)
        pr = patch[s, 0].astype(F32)
        pi = patch[s, 1].astype(F32)
        put(m, pr * wr - pi * wi, pr * wi + pi * wr)

    @pl.when(plan[HANDLER] == 1)
    def _():
        for s in range(slices):
            table_copy(s).start()
            for r in range(4):
                @pl.when(plan[REL + s] == r)
                def _():
                    for h, group in enumerate((near_in, far_in)):
                        pltpu.make_async_copy(group[r].at[plan[ENTRY + s]], patch.at[s, :, pl.ds(h * half, half)], psem.at[h, s]).start()
        table_copy(slices).start()
        row_shift = lax.rem(places[plan[POSITION], 0], rows)
        col_shift = lax.rem(places[plan[POSITION], 1], n)
        rolled = []
        for m in range(2):
            for c in range(2):
                x = pltpu.roll(probe[m, c], row_shift, 0)
                rolled.append(pltpu.roll(x, col_shift, 1).astype(BF).astype(F32))
        patch_wait(0)
        for m in range(2):
            enter(0, m, rolled[2 * m], rolled[2 * m + 1])

        def forward(s, carry):
            table_copy(s).wait()
            patch_wait(s + 1)
            first(0, tabs[s, 0])
            first(1, tabs[s, 0])
            enter(s + 1, 0, *second(0, tabs[s, 1]))
            enter(s + 1, 1, *second(1, tabs[s, 1]))
            return carry

        lax.fori_loop(0, slices - 1, forward, 0)
        table_copy(slices - 1).wait()
        table_copy(slices).wait()
        f = transform(tabs[slices - 1, 0], tabs[slices - 1, 1])
        for m in range(2):
            put(m, *f[m])
        f = transform(tabs[slices, 0], tabs[slices, 1])
        resid = (f[0][0] * f[0][0] + f[0][1] * f[0][1]) + (f[1][0] * f[1][0] + f[1][1] * f[1][1]) - target[...]
        for m in range(2):
            put(m, resid * f[m][0], resid * f[m][1])
        f = transform(tabs[slices, 1], tabs[slices, 0])
        for m in range(2):
            put(m, *f[m])

        def backward(back, carry):
            s = slices - 1 - back
            tr = ti = None
            first(0, tabs[s, 1])
            first(1, tabs[s, 1])
            for m in range(2):
                gr, gi = second(m, tabs[s, 0])
                pr = patch[s, 0].astype(F32)
                pi = patch[s, 1].astype(F32)
                put(m, pr * gr + pi * gi, pr * gi - pi * gr)
                wr = inc[s, m, 0].astype(F32)
                wi = inc[s, m, 1].astype(F32)
                ar = wr * gr + wi * gi
                ai = wr * gi - wi * gr
                tr, ti = (ar, ai) if tr is None else (tr + ar, ti + ai)
            outv[s, 0] = tr.astype(BF)
            outv[s, 1] = ti.astype(BF)
            for r in range(4):
                @pl.when(plan[REL + s] == r)
                def _():
                    for h, group in enumerate((near_out, far_out)):
                        pltpu.make_async_copy(outv.at[s, :, pl.ds(h * half, half)], group[r].at[plan[ENTRY + s]], osem.at[h, s]).start()
            return carry

        lax.fori_loop(0, slices, backward, 0)
        for s in range(slices):
            for h in range(2):
                pltpu.make_async_copy(outv.at[s, :, pl.ds(h * half, half)], near_out[0].at[0], osem.at[h, s]).wait()


def chain(plan, places, probe, target, near, far, tables, rows):
    n = target.shape[-1]
    slices = tables.shape[0] - 1
    piece = jax.ShapeDtypeStruct(near[0].shape, BF)
    return pl.pallas_call(
        functools.partial(chain_kernel, n=n, slices=slices, rows=rows),
        out_shape=(piece,) * 8,
        in_specs=[SMEM, SMEM, VMEM, VMEM] + [ANY] * 9,
        out_specs=(ANY,) * 8,
        scratch_shapes=[
            pltpu.VMEM((slices, 2, n, n), BF),
            pltpu.VMEM((slices + 1, 2, 2 * n, 2 * n), BF),
            pltpu.VMEM((slices, 2, 2, n, n), BF),
            pltpu.VMEM((2 * n, n), BF),
            pltpu.VMEM((2 * n, n), BF),
            pltpu.VMEM((n, 2 * n), BF),
            pltpu.VMEM((n, 2 * n), BF),
            pltpu.VMEM((slices, 2, n, n), BF),
            pltpu.SemaphoreType.DMA((2, slices)),
            pltpu.SemaphoreType.DMA((slices + 1,)),
            pltpu.SemaphoreType.DMA((2, slices)),
        ],
        compiler_params=pltpu.CompilerParams(vmem_limit_bytes=58 << 20),
    )(plan, places, probe, target, *near, *far, tables)


def window(ref, lead, offset, n):
    width = ref.shape[-1]
    start = pl.multiple_of((offset // n) * n, n)
    after = pl.multiple_of(jnp.minimum(start + n, width - n), n)
    lane = lax.broadcasted_iota(jnp.int32, (ref.shape[-2], n), 1)
    first = ref[lead, :, pl.ds(start, n)].astype(F32)
    second = ref[lead, :, pl.ds(after, n)].astype(F32)
    return jnp.where(lane >= offset % n, first, second)


def own_windows_kernel(places, tile, tile_bf, wins, *, n):
    tile_bf[...] = tile[...].astype(BF)
    for p in range(wins.shape[0]):
        for c in range(2):
            wins[p, c] = window(tile, c, places[p, 1], n).astype(BF)


def own_windows(places, tile, n):
    count = places.shape[0]
    return pl.pallas_call(
        functools.partial(own_windows_kernel, n=n),
        out_shape=(jax.ShapeDtypeStruct(tile.shape, BF), jax.ShapeDtypeStruct((count, 2, tile.shape[1], n), BF)),
        in_specs=[SMEM, VMEM],
        out_specs=(VMEM, VMEM),
        compiler_params=pltpu.CompilerParams(vmem_limit_bytes=40 << 20),
    )(places, tile)


def far_kernel(plan, places, tile, *outs, n):
    for k in range(4):
        p = plan[ORDER + k]
        for c in range(2):
            outs[k][c] = window(tile, c, places[p, 1], n).astype(BF)


def far_parts(plan, places, tile, n):
    return pl.pallas_call(
        functools.partial(far_kernel, n=n),
        out_shape=(jax.ShapeDtypeStruct((2, tile.shape[1], n), BF),) * 4,
        in_specs=[SMEM, SMEM, VMEM],
        out_specs=(VMEM,) * 4,
        compiler_params=pltpu.CompilerParams(vmem_limit_bytes=40 << 20),
    )(plan, places, tile)


def near_kernel(plan, places, behind, ahead, *outs, n):
    rows = ahead.shape[1]
    row = lax.broadcasted_iota(jnp.int32, (rows, n), 0)
    for k in range(4):
        p = plan[ORDER + k]
        for c in range(2):
            after = window(ahead, c, places[p, 1], n)
            before = behind[p, c].astype(F32)
            outs[k][c] = jnp.where(row >= places[p, 0] % rows, before, after).astype(BF)


def near_parts(plan, places, behind, ahead, n):
    return pl.pallas_call(
        functools.partial(near_kernel, n=n),
        out_shape=(jax.ShapeDtypeStruct((2, ahead.shape[1], n), BF),) * 4,
        in_specs=[SMEM, SMEM, VMEM, VMEM],
        out_specs=(VMEM,) * 4,
        compiler_params=pltpu.CompilerParams(vmem_limit_bytes=40 << 20),
    )(plan, places, behind, ahead)


def gather_kernel(plan, own_places, mid_places, far_places, from_own, m0, m1, m2, m3, from_far, out, *, n):
    rows = out.shape[1]
    width = out.shape[-1]
    row = lax.broadcasted_iota(jnp.int32, (rows, n), 0)
    lane = lax.broadcasted_iota(jnp.int32, (rows, n), 1)
    out[...] = jnp.zeros_like(out)
    mids = (m0, m1, m2, m3)
    for places, kind, order in ((own_places, 0, OTHER), (mid_places, 1, ORDER), (far_places, 2, OTHER)):
        for k in range(4):
            p = plan[order + k]
            shift = places[p, 0] % rows
            offset = places[p, 1]
            start = pl.multiple_of((offset // n) * n, n)
            after = pl.multiple_of(jnp.minimum(start + n, width - n), n)
            for c in range(2):
                if kind == 0:
                    term = jnp.where(row >= shift, from_own[k, c].astype(F32), 0.0)
                elif kind == 1:
                    term = mids[k][c].astype(F32)
                else:
                    term = jnp.where(row < shift, from_far[k, c].astype(F32), 0.0)
                here = lane >= offset % n
                out[c, :, pl.ds(start, n)] += jnp.where(here, term, 0.0)
                out[c, :, pl.ds(after, n)] += jnp.where(here, 0.0, term)


def gather_terms(plan, own_places, mid_places, far_places, from_own, mids, from_far, rows, width):
    n = from_own.shape[-1]
    return pl.pallas_call(
        functools.partial(gather_kernel, n=n),
        out_shape=jax.ShapeDtypeStruct((2, rows, width), F32),
        in_specs=[SMEM] * 4 + [VMEM] * 6,
        out_specs=VMEM,
        compiler_params=pltpu.CompilerParams(vmem_limit_bytes=40 << 20),
    )(plan, own_places, mid_places, far_places, from_own, *mids, from_far)


def shifted(block, distance):
    size = lax.axis_size("lat")
    return lax.ppermute(block, "lat", [(i, (i + distance) % size) for i in range(size)])


HANDLER, POSITION, SOURCE, ORDER, OTHER, REL, ENTRY = 0, 1, 2, 3, 7, 11, 27
GOAL = (((0, 0), (1, 1), (2, 0), (3, 1)), ((1, 2), (0, 3), (3, 2), (2, 3)))


def meet(c, team, j):
    goal, inner = GOAL[c][j]
    flip = inner ^ 2
    if c == 0:
        return inner if (team - goal) % 4 in (0, 1) else flip
    return inner if (team - goal) % 4 in (0, 3) else flip


def place_of(c, d):
    v = (d + 2 * c) % 16
    return v // 4, v % 4


def position_at(c, team, inner):
    found = [j for j in range(4) if meet(c, team, j) == inner]
    assert len(found) == 1
    return found[0]


def device_of(c, team, inner):
    return (4 * team + inner - 2 * c) % 16


@functools.lru_cache
def make_plan():
    out = np.zeros((2, 16, 48), np.int32)
    for c in range(2):
        for d in range(16):
            team, inner = place_of(c, d)
            j = position_at(c, team, inner)
            row = out[c, d]
            row[HANDLER] = GOAL[c][j] == (team, inner)
            row[POSITION] = j
            row[SOURCE] = (team - GOAL[c][j][0]) % 4
            other = place_of(1 - c, d)
            for k in range(4):
                row[ORDER + k] = position_at(c, team, inner ^ k)
                row[OTHER + k] = position_at(1 - c, other[0], other[1] ^ k)
            for s in range(16):
                there, at = place_of(c, s)
                row[REL + s] = (there - team) % 4
                row[ENTRY + s] = at ^ meet(c, there, j)
    return out


def permute(block, route):
    depth, lat = lax.axis_size("depth"), lax.axis_size("lat")
    pairs = []
    for d in range(depth):
        for m in range(lat):
            to = route(m % 2, *place_of(m % 2, d))
            if to is not None:
                pairs.append((d * lat + m, device_of(m % 2, *to) * lat + m))
    return lax.ppermute(block, ("depth", "lat"), pairs)


def within(block, k):
    return permute(block, lambda c, team, inner: (team, inner ^ k))


def towards(block, k):
    def route(c, team, inner):
        goal = GOAL[c][position_at(c, team, inner)]
        return goal if (team - goal[0]) % 4 == k else None
    return permute(block, route)


def away(block, k):
    def route(c, team, inner):
        j = position_at(c, team, inner)
        there = (team + k) % 4
        return (there, meet(c, there, j)) if GOAL[c][j] == (team, inner) else None
    return permute(block, route)


def on_device(object_slices, probe, positions, measured):
    n = probe.shape[-1]
    rows, width = object_slices.shape[2:]
    depth_size = lax.axis_size("depth")
    d = lax.axis_index("depth")
    m = lax.axis_index("lat")
    plan = lax.dynamic_slice(jnp.asarray(make_plan()), (m % 2, d, 0), (1, 1, 48)).reshape(48)
    tile = object_slices[0]

    mid_places = shifted(positions, 1)
    tile_bf, mine = own_windows(positions, tile, n)
    ahead = shifted(tile_bf, -1)
    behind = shifted(mine, 1)
    target = shifted(lax.dynamic_index_in_dim(measured, plan[OTHER], 0, False), 1)
    far_places = shifted(positions, 2)

    far = far_parts(plan, mid_places, tile_bf, n)
    far_got = [within(far[k], k) for k in (1, 2, 3)]
    far, ahead, behind, target, far_places = lax.optimization_barrier((far, ahead, behind, target, far_places))
    near = near_parts(plan, mid_places, behind, ahead, n)
    near_got = [within(near[k], k) for k in (1, 2, 3)]
    far_message = jnp.stack([far[0]] + far_got)
    far_in = [far_message] + [towards(far_message, k) for k in (1, 2, 3)]
    near_message = jnp.stack([near[0]] + near_got)
    near_in = [near_message] + [towards(near_message, k) for k in (1, 2, 3)]
    tables = make_tables(n, depth_size)
    terms = chain(plan, mid_places, probe, target, near_in, far_in, tables, rows)

    def home(pieces):
        block = pieces[0]
        for k in (1, 2, 3):
            block = jnp.where(plan[SOURCE] == k, away(pieces[k], k), block)
        return block

    near_block = home(terms[:4])
    far_block = home(terms[4:])
    mixed = jnp.stack([near_block[0]] + [within(near_block[k], k) for k in (1, 2, 3)])
    mids = [far_block[0]] + [within(far_block[k], k) for k in (1, 2, 3)]
    from_own = shifted(mixed, -1)
    from_far = shifted(mixed, 1)
    total = gather_terms(plan, positions, mid_places, far_places, from_own, mids, from_far, rows, width)
    return total[None]


def solution(mesh):
    return jax.shard_map(
        on_device,
        mesh=mesh,
        in_specs=(P("depth", None, "lat", None), P(), P("lat", None), P("lat", None, None)),
        out_specs=P("depth", None, "lat", None),
        check_vma=False,
    )
```

```python
import functools

import jax
import jax.numpy as jnp
import numpy as np
from jax import lax
from jax.experimental import pallas as pl
from jax.experimental.pallas import tpu as pltpu
from jax.sharding import PartitionSpec as P

BF = jnp.bfloat16
F32 = jnp.float32
ANY = pl.BlockSpec(memory_space=pl.ANY)
SMEM = pl.BlockSpec(memory_space=pltpu.MemorySpace.SMEM)
VMEM = pl.BlockSpec(memory_space=pltpu.MemorySpace.VMEM)


@functools.lru_cache
def base_tables(n):
    k = np.arange(n)
    d = np.exp(-2j * np.pi * ((k[:, None] * k[None, :]) % n) / n) / np.sqrt(n)
    q = np.where(k < n // 2, k, k - n).astype(np.float64)
    h = np.exp(-1j * np.pi * 0.5 * q * q / n)
    prop = (np.conj(d) * h[None, :]) @ d
    return np.stack([prop.real, prop.imag, d.real, d.imag]).astype(np.float32)


def tables_kernel(scales, base, out, *, n, slices):
    s = pl.program_id(0)
    which = jnp.where(s < slices, 0, 2)
    re = base[which]
    im = base[which + 1]
    for side, sign in ((0, 1.0), (1, -1.0)):
        scale = scales[side, s]
        a = (re * scale).astype(BF)
        b = im * (scale * sign)
        out[0, side, 0:n, 0:n] = a
        out[0, side, n:2 * n, n:2 * n] = a
        out[0, side, 0:n, n:2 * n] = (-b).astype(BF)
        out[0, side, n:2 * n, 0:n] = b.astype(BF)


def make_tables(n, slices):
    a = 2.0 ** ((np.arange(slices) + 0.5) / slices)
    scales = np.concatenate([np.stack([a, 1.0 / a]), np.ones((2, 1))], axis=1).astype(np.float32)
    return pl.pallas_call(
        functools.partial(tables_kernel, n=n, slices=slices),
        grid=(slices + 1,),
        out_shape=jax.ShapeDtypeStruct((slices + 1, 2, 2 * n, 2 * n), BF),
        in_specs=[SMEM, pl.BlockSpec((4, n, n), lambda s: (0, 0, 0))],
        out_specs=pl.BlockSpec((1, 2, 2 * n, 2 * n), lambda s: (s, 0, 0, 0)),
    )(jnp.asarray(scales), jnp.asarray(base_tables(n)))


def chain_kernel(plan, places, probe, behind, *refs, n, slices, rows):
    near_in, far_in, tabs_hbm, outs = refs[0:4], refs[4:8], refs[8], refs[9:13]
    (patch, tabs, inc, lhs0, lhs1, mid0, mid1, outv, target, psem, tsem, osem, gsem) = refs[13:]
    lhs, mid = (lhs0, lhs1), (mid0, mid1)
    half = n // 2

    def table_copy(s):
        return pltpu.make_async_copy(tabs_hbm.at[s], tabs.at[s], tsem.at[s])

    def patch_wait(s):
        for h in range(2):
            pltpu.make_async_copy(near_in[0].at[0], patch.at[s, :, pl.ds(h * half, half)], psem.at[h, s]).wait()

    def put(m, re, im):
        lhs[m][0:n] = re.astype(BF)
        lhs[m][n:2 * n] = im.astype(BF)

    def first(m, left):
        u = jnp.dot(left, lhs[m][...], preferred_element_type=F32)
        mid[m][:, 0:n] = u[0:n].astype(BF)
        mid[m][:, n:2 * n] = u[n:2 * n].astype(BF)

    def second(m, right):
        v = jnp.dot(mid[m][...], right, preferred_element_type=F32)
        return v[:, 0:n], v[:, n:2 * n]

    def transform(left, right):
        first(0, left)
        first(1, left)
        return second(0, right), second(1, right)

    def enter(s, m, wr, wi):
        inc[s, m, 0] = wr.astype(BF)
        inc[s, m, 1] = wi.astype(BF)
        pr = patch[s, 0].astype(F32)
        pi = patch[s, 1].astype(F32)
        put(m, pr * wr - pi * wi, pr * wi + pi * wr)

    @pl.when(plan[HANDLER] == 1)
    def _():
        target_copy = pltpu.make_async_copy(behind.at[pl.ds(behind.shape[0] - 2, 2)], target, gsem)
        target_copy.start()
        for s in range(slices):
            table_copy(s).start()
            for r in range(4):
                @pl.when(plan[REL + s] == r)
                def _():
                    for h, group in enumerate((near_in, far_in)):
                        pltpu.make_async_copy(group[r].at[plan[ENTRY + s]], patch.at[s, :, pl.ds(h * half, half)], psem.at[h, s]).start()
        table_copy(slices).start()
        row_shift = lax.rem(places[plan[POSITION], 0], rows)
        col_shift = lax.rem(places[plan[POSITION], 1], n)
        rolled = []
        for m in range(2):
            for c in range(2):
                x = pltpu.roll(probe[m, c], row_shift, 0)
                rolled.append(pltpu.roll(x, col_shift, 1).astype(BF).astype(F32))
        patch_wait(0)
        for m in range(2):
            enter(0, m, rolled[2 * m], rolled[2 * m + 1])

        def forward(s, carry):
            table_copy(s).wait()
            patch_wait(s + 1)
            first(0, tabs[s, 0])
            first(1, tabs[s, 0])
            enter(s + 1, 0, *second(0, tabs[s, 1]))
            enter(s + 1, 1, *second(1, tabs[s, 1]))
            return carry

        lax.fori_loop(0, slices - 1, forward, 0)
        table_copy(slices - 1).wait()
        table_copy(slices).wait()
        f = transform(tabs[slices - 1, 0], tabs[slices - 1, 1])
        for m in range(2):
            put(m, *f[m])
        f = transform(tabs[slices, 0], tabs[slices, 1])
        target_copy.wait()
        wanted = [target[0, h].astype(F32) + target[1, h].astype(F32) for h in range(2)]
        resid = (f[0][0] * f[0][0] + f[0][1] * f[0][1]) + (f[1][0] * f[1][0] + f[1][1] * f[1][1]) - jnp.concatenate(wanted, axis=0)
        for m in range(2):
            put(m, resid * f[m][0], resid * f[m][1])
        f = transform(tabs[slices, 1], tabs[slices, 0])
        for m in range(2):
            put(m, *f[m])

        def backward(back, carry):
            s = slices - 1 - back
            tr = ti = None
            first(0, tabs[s, 1])
            first(1, tabs[s, 1])
            for m in range(2):
                gr, gi = second(m, tabs[s, 0])
                pr = patch[s, 0].astype(F32)
                pi = patch[s, 1].astype(F32)
                put(m, pr * gr + pi * gi, pr * gi - pi * gr)
                wr = inc[s, m, 0].astype(F32)
                wi = inc[s, m, 1].astype(F32)
                ar = wr * gr + wi * gi
                ai = wr * gi - wi * gr
                tr, ti = (ar, ai) if tr is None else (tr + ar, ti + ai)
            outv[s, 0] = tr.astype(BF)
            outv[s, 1] = ti.astype(BF)
            for r in range(4):
                @pl.when(plan[REL + s] == r)
                def _():
                    pltpu.make_async_copy(outv.at[s], outs[r].at[plan[ENTRY + s]], osem.at[s]).start()
            return carry

        lax.fori_loop(0, slices, backward, 0)
        for s in range(slices):
            pltpu.make_async_copy(outv.at[s], outs[0].at[0], osem.at[s]).wait()


def chain(plan, places, probe, behind, near, far, tables, rows):
    n = probe.shape[-1]
    slices = tables.shape[0] - 1
    piece = jax.ShapeDtypeStruct((slices // 4, 2, n, n), BF)
    return pl.pallas_call(
        functools.partial(chain_kernel, n=n, slices=slices, rows=rows),
        out_shape=(piece,) * 4,
        in_specs=[SMEM, SMEM, VMEM] + [ANY] * 10,
        out_specs=(ANY,) * 4,
        scratch_shapes=[
            pltpu.VMEM((slices, 2, n, n), BF),
            pltpu.VMEM((slices + 1, 2, 2 * n, 2 * n), BF),
            pltpu.VMEM((slices, 2, 2, n, n), BF),
            pltpu.VMEM((2 * n, n), BF),
            pltpu.VMEM((2 * n, n), BF),
            pltpu.VMEM((n, 2 * n), BF),
            pltpu.VMEM((n, 2 * n), BF),
            pltpu.VMEM((slices, 2, n, n), BF),
            pltpu.VMEM((2, 2, n // 2, n), BF),
            pltpu.SemaphoreType.DMA((2, slices)),
            pltpu.SemaphoreType.DMA((slices + 1,)),
            pltpu.SemaphoreType.DMA((slices,)),
            pltpu.SemaphoreType.DMA,
        ],
        compiler_params=pltpu.CompilerParams(vmem_limit_bytes=58 << 20),
    )(plan, places, probe, behind, *near, *far, tables)


def window(ref, lead, offset, n):
    width = ref.shape[-1]
    start = pl.multiple_of((offset // n) * n, n)
    after = pl.multiple_of(jnp.minimum(start + n, width - n), n)
    lane = lax.broadcasted_iota(jnp.int32, (ref.shape[-2], n), 1)
    first = ref[lead, :, pl.ds(start, n)].astype(F32)
    second = ref[lead, :, pl.ds(after, n)].astype(F32)
    return jnp.where(lane >= offset % n, first, second)


def own_windows_kernel(plan, places, tile, measured, tile_bf, wins, target, sem, *, n):
    copy = pltpu.make_async_copy(measured.at[plan[OTHER]], target, sem)
    copy.start()
    rows = tile.shape[1]
    tile_bf[...] = tile[...].astype(BF)
    for p in range(places.shape[0]):
        for c in range(2):
            wins[p, c] = window(tile, c, places[p, 1], n).astype(BF)
    copy.wait()
    for c in range(2):
        x = target[c * rows:(c + 1) * rows]
        high = x.astype(BF)
        wins[places.shape[0], c] = high
        wins[places.shape[0] + 1, c] = (x - high.astype(F32)).astype(BF)


def own_windows(plan, places, tile, measured, n):
    count = places.shape[0]
    return pl.pallas_call(
        functools.partial(own_windows_kernel, n=n),
        out_shape=(jax.ShapeDtypeStruct(tile.shape, BF), jax.ShapeDtypeStruct((count + 2, 2, tile.shape[1], n), BF)),
        in_specs=[SMEM, SMEM, VMEM, ANY],
        out_specs=(VMEM, VMEM),
        scratch_shapes=[pltpu.VMEM((n, n), F32), pltpu.SemaphoreType.DMA],
        compiler_params=pltpu.CompilerParams(vmem_limit_bytes=40 << 20),
    )(plan, places, tile, measured)


def far_kernel(plan, places, tile, *outs, n):
    for k in range(4):
        p = plan[ORDER + k]
        for c in range(2):
            outs[k][c] = window(tile, c, places[p, 1], n).astype(BF)


def far_parts(plan, places, tile, n):
    return pl.pallas_call(
        functools.partial(far_kernel, n=n),
        out_shape=(jax.ShapeDtypeStruct((2, tile.shape[1], n), BF),) * 4,
        in_specs=[SMEM, SMEM, VMEM],
        out_specs=(VMEM,) * 4,
        compiler_params=pltpu.CompilerParams(vmem_limit_bytes=40 << 20),
    )(plan, places, tile)


def near_kernel(plan, places, behind, ahead, *outs, n):
    rows = ahead.shape[1]
    row = lax.broadcasted_iota(jnp.int32, (rows, n), 0)
    for k in range(4):
        p = plan[ORDER + k]
        for c in range(2):
            after = window(ahead, c, places[p, 1], n)
            before = behind[p, c].astype(F32)
            outs[k][c] = jnp.where(row >= places[p, 0] % rows, before, after).astype(BF)


def near_parts(plan, places, behind, ahead, n):
    return pl.pallas_call(
        functools.partial(near_kernel, n=n),
        out_shape=(jax.ShapeDtypeStruct((2, ahead.shape[1], n), BF),) * 4,
        in_specs=[SMEM, SMEM, VMEM, VMEM],
        out_specs=(VMEM,) * 4,
        compiler_params=pltpu.CompilerParams(vmem_limit_bytes=40 << 20),
    )(plan, places, behind, ahead)


def gather_kernel(plan, own_places, mid_places, far_places, from_own, m0, m1, m2, m3, from_far, out, *, n):
    rows = out.shape[1]
    width = out.shape[-1]
    row = lax.broadcasted_iota(jnp.int32, (rows, n), 0)
    lane = lax.broadcasted_iota(jnp.int32, (rows, n), 1)
    out[...] = jnp.zeros_like(out)
    mids = (m0, m1, m2, m3)
    for places, kind, order in ((own_places, 0, OTHER), (mid_places, 1, ORDER), (far_places, 2, OTHER)):
        for k in range(4):
            p = plan[order + k]
            shift = places[p, 0] % rows
            offset = places[p, 1]
            start = pl.multiple_of((offset // n) * n, n)
            after = pl.multiple_of(jnp.minimum(start + n, width - n), n)
            for c in range(2):
                if kind == 0:
                    term = jnp.where(row >= shift, from_own[k, c].astype(F32), 0.0)
                elif kind == 1:
                    term = mids[k][c].astype(F32)
                else:
                    term = jnp.where(row < shift, from_far[k, c].astype(F32), 0.0)
                here = lane >= offset % n
                out[c, :, pl.ds(start, n)] += jnp.where(here, term, 0.0)
                out[c, :, pl.ds(after, n)] += jnp.where(here, 0.0, term)


def gather_terms(plan, own_places, mid_places, far_places, from_own, mids, from_far, rows, width):
    n = from_own.shape[-1]
    return pl.pallas_call(
        functools.partial(gather_kernel, n=n),
        out_shape=jax.ShapeDtypeStruct((2, rows, width), F32),
        in_specs=[SMEM] * 4 + [VMEM] * 6,
        out_specs=VMEM,
        compiler_params=pltpu.CompilerParams(vmem_limit_bytes=40 << 20),
    )(plan, own_places, mid_places, far_places, from_own, *mids, from_far)


def shifted(block, distance):
    size = lax.axis_size("lat")
    return lax.ppermute(block, "lat", [(i, (i + distance) % size) for i in range(size)])


HANDLER, POSITION, SOURCE, ORDER, OTHER, REL, ENTRY = 0, 1, 2, 3, 7, 11, 27
GOAL = (((0, 0), (1, 1), (2, 0), (3, 1)), ((1, 2), (0, 3), (3, 2), (2, 3)))


def meet(c, team, j):
    goal, inner = GOAL[c][j]
    flip = inner ^ 2
    if c == 0:
        return inner if (team - goal) % 4 in (0, 1) else flip
    return inner if (team - goal) % 4 in (0, 3) else flip


def place_of(c, d):
    v = (d + 2 * c) % 16
    return v // 4, v % 4


def position_at(c, team, inner):
    found = [j for j in range(4) if meet(c, team, j) == inner]
    assert len(found) == 1
    return found[0]


def device_of(c, team, inner):
    return (4 * team + inner - 2 * c) % 16


@functools.lru_cache
def make_plan():
    out = np.zeros((2, 16, 48), np.int32)
    for c in range(2):
        for d in range(16):
            team, inner = place_of(c, d)
            j = position_at(c, team, inner)
            row = out[c, d]
            row[HANDLER] = GOAL[c][j] == (team, inner)
            row[POSITION] = j
            row[SOURCE] = (team - GOAL[c][j][0]) % 4
            other = place_of(1 - c, d)
            for k in range(4):
                row[ORDER + k] = position_at(c, team, inner ^ k)
                row[OTHER + k] = position_at(1 - c, other[0], other[1] ^ k)
            for s in range(16):
                there, at = place_of(c, s)
                row[REL + s] = (there - team) % 4
                row[ENTRY + s] = at ^ meet(c, there, j)
    return out


def permute(block, route):
    depth, lat = lax.axis_size("depth"), lax.axis_size("lat")
    pairs = []
    for d in range(depth):
        for m in range(lat):
            to = route(m % 2, *place_of(m % 2, d))
            if to is not None:
                pairs.append((d * lat + m, device_of(m % 2, *to) * lat + m))
    return lax.ppermute(block, ("depth", "lat"), pairs)


def within(block, k):
    return permute(block, lambda c, team, inner: (team, inner ^ k))


def towards(block, k):
    def route(c, team, inner):
        goal = GOAL[c][position_at(c, team, inner)]
        return goal if (team - goal[0]) % 4 == k else None
    return permute(block, route)


def away(block, k):
    def route(c, team, inner):
        j = position_at(c, team, inner)
        there = (team + k) % 4
        return (there, meet(c, there, j)) if GOAL[c][j] == (team, inner) else None
    return permute(block, route)


def on_device(object_slices, probe, positions, measured):
    n = probe.shape[-1]
    rows, width = object_slices.shape[2:]
    depth_size = lax.axis_size("depth")
    d = lax.axis_index("depth")
    m = lax.axis_index("lat")
    plan = lax.dynamic_slice(jnp.asarray(make_plan()), (m % 2, d, 0), (1, 1, 48)).reshape(48)
    tile = object_slices[0]

    mid_places = shifted(positions, 1)
    far_places = shifted(positions, 2)
    tile_bf, mine = own_windows(plan, positions, tile, measured, n)
    tile_bf, mine, mid_places, far_places = lax.optimization_barrier((tile_bf, mine, mid_places, far_places))
    ahead = shifted(tile_bf, -1)
    behind = shifted(mine, 1)

    far = far_parts(plan, mid_places, tile_bf, n)
    far_got = [within(far[k], k) for k in (1, 2, 3)]
    far, ahead, behind = lax.optimization_barrier((far, ahead, behind))
    near = near_parts(plan, mid_places, behind, ahead, n)
    near_got = [within(near[k], k) for k in (1, 2, 3)]
    far_message = jnp.stack([far[0]] + far_got)
    far_in = [far_message] + [towards(far_message, k) for k in (1, 2, 3)]
    near_message = jnp.stack([near[0]] + near_got)
    near_in = [near_message] + [towards(near_message, k) for k in (1, 2, 3)]
    tables = make_tables(n, depth_size)
    terms = chain(plan, mid_places, probe, behind, near_in, far_in, tables, rows)

    block = terms[0]
    for k in (1, 2, 3):
        block = jnp.where(plan[SOURCE] == k, away(terms[k], k), block)
    mixed = jnp.stack([block[0, :, :rows]] + [within(block[k, :, :rows], k) for k in (1, 2, 3)])
    mids = [block[0, :, rows:]] + [within(block[k, :, rows:], k) for k in (1, 2, 3)]
    from_own = shifted(mixed, -1)
    from_far = shifted(mixed, 1)
    total = gather_terms(plan, positions, mid_places, far_places, from_own, mids, from_far, rows, width)
    return total[None]


def solution(mesh):
    return jax.shard_map(
        on_device,
        mesh=mesh,
        in_specs=(P("depth", None, "lat", None), P(), P("lat", None), P("lat", None, None)),
        out_specs=P("depth", None, "lat", None),
        check_vma=False,
    )
```

```python
import functools

import jax
import jax.numpy as jnp
import numpy as np
from jax import lax
from jax.experimental import pallas as pl
from jax.experimental.pallas import tpu as pltpu
from jax.sharding import PartitionSpec as P

BF = jnp.bfloat16
F32 = jnp.float32
ANY = pl.BlockSpec(memory_space=pl.ANY)
SMEM = pl.BlockSpec(memory_space=pltpu.MemorySpace.SMEM)
FIRST = 64
SECOND = 32
LAG = 2
VMEM = pl.BlockSpec(memory_space=pltpu.MemorySpace.VMEM)


@functools.lru_cache
def base_tables(n):
    k = np.arange(n)
    d = np.exp(-2j * np.pi * ((k[:, None] * k[None, :]) % n) / n) / np.sqrt(n)
    q = np.where(k < n // 2, k, k - n).astype(np.float64)
    h = np.exp(-1j * np.pi * 0.5 * q * q / n)
    prop = (np.conj(d) * h[None, :]) @ d
    return np.stack([prop.real, prop.imag, d.real, d.imag]).astype(np.float32)


def tables_kernel(scales, base, out, *, n, slices):
    s = pl.program_id(0)
    which = jnp.where(s < slices, 0, 2)
    re = base[which]
    im = base[which + 1]
    for side, sign in ((0, 1.0), (1, -1.0)):
        scale = scales[side, s]
        a = (re * scale).astype(BF)
        b = im * (scale * sign)
        out[0, side, 0:n, 0:n] = a
        out[0, side, n:2 * n, n:2 * n] = a
        out[0, side, 0:n, n:2 * n] = (-b).astype(BF)
        out[0, side, n:2 * n, 0:n] = b.astype(BF)


def make_tables(n, slices):
    a = 2.0 ** ((np.arange(slices) + 0.5) / slices)
    scales = np.concatenate([np.stack([a, 1.0 / a]), np.ones((2, 1))], axis=1).astype(np.float32)
    return pl.pallas_call(
        functools.partial(tables_kernel, n=n, slices=slices),
        grid=(slices + 1,),
        out_shape=jax.ShapeDtypeStruct((slices + 1, 2, 2 * n, 2 * n), BF),
        in_specs=[SMEM, pl.BlockSpec((4, n, n), lambda s: (0, 0, 0))],
        out_specs=pl.BlockSpec((1, 2, 2 * n, 2 * n), lambda s: (s, 0, 0, 0)),
    )(jnp.asarray(scales), jnp.asarray(base_tables(n)))


def chain_kernel(*refs, n, slices, rows):
    accs = [pltpu.ACC(c)((size, n), F32)
            for size in (FIRST, SECOND) for _ in range(2) for c in range(2) for _ in range(n // size)]
    pl.run_scoped(lambda *scoped: chain_body(*refs, *scoped, n=n, slices=slices, rows=rows), *accs)


def chain_body(plan, places, probe, behind, *refs, n, slices, rows):
    ins, tabs_hbm, outs = refs[0:8], refs[8], refs[9:17]
    (patch, tabs, inc, lhs0, lhs1, mid0, mid1, outv, target, term, psem, tsem, osem, gsem) = refs[17:31]
    accs = list(refs[31:])
    first_acc = [[[accs.pop(0) for _ in range(n // FIRST)] for _ in range(2)] for _ in range(2)]
    second_acc = [[[accs.pop(0) for _ in range(n // SECOND)] for _ in range(2)] for _ in range(2)]
    lhs, mid = (lhs0, lhs1), (mid0, mid1)
    half = n // 2

    def table_copy(s):
        return pltpu.make_async_copy(tabs_hbm.at[s], tabs.at[s], tsem.at[s])

    def patch_wait(s):
        pltpu.make_async_copy(ins[0].at[0], patch.at[s], psem.at[s]).wait()

    def span(i, size):
        return pl.ds(i * size, size)

    def issue(m, accs, size, weights, rows_of, tasks=()):
        for c in range(2):
            for k in range(2):
                pltpu.matmul_push_rhs(weights(c, k), k, c)
        pieces = 2 * (n // size)
        todo = list(tasks)
        for j in range(pieces):
            k, i = divmod(j, n // size)
            for c in range(2):
                pltpu.matmul_acc_lhs(accs[m][c][i], rows_of(c, k, i), load_staged_rhs=k if i == 0 else None)
            left = max(1, pieces - 1 - max(j, LAG))
            take = 0 if j < LAG else -(-len(todo) // left)
            for task in todo[:take]:
                task()
            del todo[:take]
        for task in todo:
            task()

    def first(m, s, side, tasks=()):
        issue(m, first_acc, FIRST, lambda c, k: lhs[m][k * n:(k + 1) * n],
              lambda c, k, i: tabs[s, side, pl.ds(c * n + i * FIRST, FIRST), k * n:(k + 1) * n], tasks)

    def turn(m):
        def one(i, c):
            mid[m][span(i, FIRST), c * n:(c + 1) * n] = pltpu.matmul_pop(first_acc[m][c][i]).astype(BF)
        return [functools.partial(one, i, c) for i in range(n // FIRST) for c in range(2)]

    def second(m, s, side, tasks=()):
        issue(m, second_acc, SECOND, lambda c, k: tabs[s, side, k * n:(k + 1) * n, c * n:(c + 1) * n],
              lambda c, k, i: mid[m][span(i, SECOND), k * n:(k + 1) * n], tasks)

    def pop(m, i):
        return pltpu.matmul_pop(second_acc[m][0][i]), pltpu.matmul_pop(second_acc[m][1][i])

    def put(m, i, re, im):
        lhs[m][pl.ds(i * SECOND, SECOND)] = re.astype(BF)
        lhs[m][pl.ds(n + i * SECOND, SECOND)] = im.astype(BF)

    def enter(s, m, i, wr, wi):
        inc[s, m, 0, span(i, SECOND)] = wr.astype(BF)
        inc[s, m, 1, span(i, SECOND)] = wi.astype(BF)
        pr = patch[s, 0, span(i, SECOND)].astype(F32)
        pi = patch[s, 1, span(i, SECOND)].astype(F32)
        put(m, i, pr * wr - pi * wi, pr * wi + pi * wr)

    def leave(s, m, i, gr, gi):
        pr = patch[s, 0, span(i, SECOND)].astype(F32)
        pi = patch[s, 1, span(i, SECOND)].astype(F32)
        put(m, i, pr * gr + pi * gi, pr * gi - pi * gr)
        wr = inc[s, m, 0, span(i, SECOND)].astype(F32)
        wi = inc[s, m, 1, span(i, SECOND)].astype(F32)
        tr = wr * gr + wi * gi
        ti = wr * gi - wi * gr
        if m == 0:
            term[0, span(i, SECOND)] = tr
            term[1, span(i, SECOND)] = ti
        else:
            outv[s, 0, span(i, SECOND)] = (term[0, span(i, SECOND)] + tr).astype(BF)
            outv[s, 1, span(i, SECOND)] = (term[1, span(i, SECOND)] + ti).astype(BF)

    count = n // SECOND

    def uses(m, use):
        return [functools.partial(lambda i: use(m, i, *pop(m, i)), i) for i in range(count)]

    def run(tasks):
        for task in tasks:
            task()

    def step(s, side, use, after=None):
        second(0, s, side, turn(1))
        second(1, s, side, uses(0, use))
        if after is None:
            run(uses(1, use))
        else:
            first(0, *after, uses(1, use))
            first(1, *after, turn(0))

    @pl.when(plan[HANDLER] == 1)
    def _():
        target_copy = pltpu.make_async_copy(behind.at[pl.ds(behind.shape[0] - 2, 2)], target, gsem)
        target_copy.start()
        for s in range(slices):
            table_copy(s).start()
            for r in range(8):
                @pl.when(plan[REL + s] == r)
                def _():
                    pltpu.make_async_copy(ins[r].at[plan[ENTRY + s]], patch.at[s], psem.at[s]).start()
        table_copy(slices).start()
        row_shift = lax.rem(places[plan[POSITION], 0], rows)
        col_shift = lax.rem(places[plan[POSITION], 1], n)
        for m in range(2):
            for c in range(2):
                x = pltpu.roll(probe[m, c], row_shift, 0)
                term[c] = pltpu.roll(x, col_shift, 1).astype(BF).astype(F32)
            if m == 0:
                patch_wait(0)
                table_copy(0).wait()
            for i in range(count):
                enter(0, m, i, term[0, span(i, SECOND)], term[1, span(i, SECOND)])
            first(m, 0, 0)
        run(turn(0))

        def forward(s, carry):
            table_copy(s + 1).wait()
            patch_wait(s + 1)
            step(s, 1, lambda m, i, re, im: enter(s + 1, m, i, re, im), (s + 1, 0))
            return carry

        lax.fori_loop(0, slices - 1, forward, 0)
        table_copy(slices).wait()
        step(slices - 1, 1, put, (slices, 0))
        target_copy.wait()
        second(0, slices, 1, turn(1))
        second(1, slices, 1)
        for i in range(count):
            ar, ai = pop(0, i)
            br, bi = pop(1, i)
            h, at = divmod(i * SECOND, half)
            wanted = target[0, h, pl.ds(at, SECOND)].astype(F32) + target[1, h, pl.ds(at, SECOND)].astype(F32)
            resid = (ar * ar + ai * ai) + (br * br + bi * bi) - wanted
            put(0, i, resid * ar, resid * ai)
            put(1, i, resid * br, resid * bi)
        first(0, slices, 1)
        first(1, slices, 1, turn(0))
        step(slices, 0, put, (slices - 1, 1))

        def send(s):
            for r in range(8):
                @pl.when(plan[REL + s] == r)
                def _():
                    pltpu.make_async_copy(outv.at[s], outs[r].at[plan[ENTRY + s]], osem.at[s]).start()

        def backward(back, carry):
            s = slices - 1 - back
            step(s, 0, lambda m, i, re, im: leave(s, m, i, re, im), (s - 1, 1))
            send(s)
            return carry

        lax.fori_loop(0, slices - 1, backward, 0)
        step(0, 0, lambda m, i, re, im: leave(0, m, i, re, im))
        send(0)
        for s in range(slices):
            pltpu.make_async_copy(outv.at[s], outs[0].at[0], osem.at[s]).wait()


def chain(plan, places, probe, behind, messages, tables, rows):
    n = probe.shape[-1]
    slices = tables.shape[0] - 1
    piece = jax.ShapeDtypeStruct(messages[0].shape, BF)
    return pl.pallas_call(
        functools.partial(chain_kernel, n=n, slices=slices, rows=rows),
        out_shape=(piece,) * 8,
        in_specs=[SMEM, SMEM, VMEM] + [ANY] * 10,
        out_specs=(ANY,) * 8,
        scratch_shapes=[
            pltpu.VMEM((slices, 2, n, n), BF),
            pltpu.VMEM((slices + 1, 2, 2 * n, 2 * n), BF),
            pltpu.VMEM((slices, 2, 2, n, n), BF),
            pltpu.VMEM((2 * n, n), BF),
            pltpu.VMEM((2 * n, n), BF),
            pltpu.VMEM((n, 2 * n), BF),
            pltpu.VMEM((n, 2 * n), BF),
            pltpu.VMEM((slices, 2, n, n), BF),
            pltpu.VMEM((2, 2, n // 2, n), BF),
            pltpu.VMEM((2, n, n), F32),
            pltpu.SemaphoreType.DMA((slices,)),
            pltpu.SemaphoreType.DMA((slices + 1,)),
            pltpu.SemaphoreType.DMA((slices,)),
            pltpu.SemaphoreType.DMA,
        ],
        compiler_params=pltpu.CompilerParams(vmem_limit_bytes=58 << 20),
    )(plan, places, probe, behind, *messages, tables)


def window(ref, lead, offset, n):
    width = ref.shape[-1]
    start = pl.multiple_of((offset // n) * n, n)
    after = pl.multiple_of(jnp.minimum(start + n, width - n), n)
    lane = lax.broadcasted_iota(jnp.int32, (ref.shape[-2], n), 1)
    first = ref[lead, :, pl.ds(start, n)].astype(F32)
    second = ref[lead, :, pl.ds(after, n)].astype(F32)
    return jnp.where(lane >= offset % n, first, second)


def own_windows_kernel(plan, places, tile, measured, tile_bf, wins, target, sem, *, n):
    copy = pltpu.make_async_copy(measured.at[plan[OTHER]], target, sem)
    copy.start()
    rows = tile.shape[1]
    tile_bf[...] = tile[...].astype(BF)
    for p in range(places.shape[0]):
        for c in range(2):
            wins[p, c] = window(tile, c, places[p, 1], n).astype(BF)
    copy.wait()
    for c in range(2):
        x = target[c * rows:(c + 1) * rows]
        high = x.astype(BF)
        wins[places.shape[0], c] = high
        wins[places.shape[0] + 1, c] = (x - high.astype(F32)).astype(BF)


def own_windows(plan, places, tile, measured, n):
    count = places.shape[0]
    return pl.pallas_call(
        functools.partial(own_windows_kernel, n=n),
        out_shape=(jax.ShapeDtypeStruct(tile.shape, BF), jax.ShapeDtypeStruct((count + 2, 2, tile.shape[1], n), BF)),
        in_specs=[SMEM, SMEM, VMEM, ANY],
        out_specs=(VMEM, VMEM),
        scratch_shapes=[pltpu.VMEM((n, n), F32), pltpu.SemaphoreType.DMA],
        compiler_params=pltpu.CompilerParams(vmem_limit_bytes=40 << 20),
    )(plan, places, tile, measured)


def merge_kernel(plan, places, behind, tile, ahead, even, odd, given, *, n):
    rows = tile.shape[1]
    row = lax.broadcasted_iota(jnp.int32, (rows, n), 0)
    for k, out in enumerate((even.at[0], odd.at[0], given.at[0], given.at[1])):
        p = plan[ORDER + k]
        for c in range(2):
            after = window(ahead, c, places[p, 1], n)
            before = behind[p, c].astype(F32)
            out[c, 0:rows] = jnp.where(row >= places[p, 0] % rows, before, after).astype(BF)
            out[c, rows:2 * rows] = window(tile, c, places[p, 1], n).astype(BF)


def merge(plan, places, behind, tile, ahead, n):
    shape = (2, 2 * tile.shape[1], n)
    return pl.pallas_call(
        functools.partial(merge_kernel, n=n),
        out_shape=tuple(jax.ShapeDtypeStruct((k,) + shape, BF) for k in (1, 1, 2)),
        in_specs=[SMEM, SMEM, VMEM, VMEM, VMEM],
        out_specs=(VMEM,) * 3,
        compiler_params=pltpu.CompilerParams(vmem_limit_bytes=40 << 20),
    )(plan, places, behind, tile, ahead)


def gather_kernel(plan, own_places, mid_places, far_places, from_own, even, odd, given, from_far, out, *, n):
    rows = out.shape[1]
    width = out.shape[-1]
    row = lax.broadcasted_iota(jnp.int32, (rows, n), 0)
    lane = lax.broadcasted_iota(jnp.int32, (rows, n), 1)
    out[...] = jnp.zeros_like(out)
    mids = (even.at[0], odd.at[0], given.at[0], given.at[1])
    for places, kind, order in ((own_places, 0, OTHER), (mid_places, 1, ORDER), (far_places, 2, OTHER)):
        for k in range(4):
            p = plan[order + k]
            shift = places[p, 0] % rows
            offset = places[p, 1]
            start = pl.multiple_of((offset // n) * n, n)
            after = pl.multiple_of(jnp.minimum(start + n, width - n), n)
            for c in range(2):
                if kind == 0:
                    term = jnp.where(row >= shift, from_own[k, c].astype(F32), 0.0)
                elif kind == 1:
                    term = mids[k][c, rows:2 * rows].astype(F32)
                else:
                    term = jnp.where(row < shift, from_far[k, c].astype(F32), 0.0)
                here = lane >= offset % n
                out[c, :, pl.ds(start, n)] += jnp.where(here, term, 0.0)
                out[c, :, pl.ds(after, n)] += jnp.where(here, 0.0, term)


def gather_terms(plan, own_places, mid_places, far_places, from_own, mids, from_far, rows, width):
    n = from_own.shape[-1]
    return pl.pallas_call(
        functools.partial(gather_kernel, n=n),
        out_shape=jax.ShapeDtypeStruct((2, rows, width), F32),
        in_specs=[SMEM] * 4 + [VMEM] * 5,
        out_specs=VMEM,
        compiler_params=pltpu.CompilerParams(vmem_limit_bytes=40 << 20),
    )(plan, own_places, mid_places, far_places, from_own, *mids, from_far)


def shifted(block, distance):
    size = lax.axis_size("lat")
    return lax.ppermute(block, "lat", [(i, (i + distance) % size) for i in range(size)])


HANDLER, POSITION, EVEN, ODD, ORDER, OTHER, REL, ENTRY = 0, 1, 2, 3, 4, 8, 12, 28
GOAL = (((0, 0, 0), (1, 0, 1), (2, 0, 0), (3, 0, 1)), ((1, 1, 0), (0, 1, 1), (3, 1, 0), (2, 1, 1)))


def meet(c, team, j):
    goal, lo, _ = GOAL[c][j]
    return lo if (team - goal) % 4 in ((0, 1), (0, 3))[c] else 1 - lo


def place_of(c, d):
    v = (d + 2 * c) % 16
    return v // 4, v // 2 % 2, v % 2


def device_of(c, team, lo, y):
    return (4 * team + 2 * lo + y - 2 * c) % 16


def kept(c, team, lo):
    found = [(j, (team - GOAL[c][j][0]) % 4) for j in range(4) if meet(c, team, j) == lo]
    found.sort(key=lambda x: x[1] % 2)
    assert [k % 2 for _, k in found] == [0, 1]
    return found


@functools.lru_cache
def make_plan():
    out = np.zeros((2, 16, 48), np.int32)
    for c in range(2):
        for d in range(16):
            team, lo, y = place_of(c, d)
            row = out[c, d]
            (even, near), (odd, far) = kept(c, team, lo)
            row[EVEN] = 2 * near + (y ^ GOAL[c][even][2])
            row[ODD] = 2 * far + (y ^ GOAL[c][odd][2])
            j = even
            row[HANDLER] = GOAL[c][j] == (team, lo, y)
            row[POSITION] = j
            row[ORDER:ORDER + 4] = [even, odd] + [j for j, _ in kept(c, team, 1 - lo)]
            team2, lo2, _ = place_of(1 - c, d)
            row[OTHER:OTHER + 4] = [j for j, _ in kept(1 - c, team2, lo2) + kept(1 - c, team2, 1 - lo2)]
            for s in range(16):
                there, at, side = place_of(c, s)
                row[REL + s] = 2 * ((there - team) % 4) + (side ^ y)
                row[ENTRY + s] = at ^ meet(c, there, j)
    return out


def permute(block, route):
    depth, lat = lax.axis_size("depth"), lax.axis_size("lat")
    pairs = []
    for d in range(depth):
        for m in range(lat):
            to = route(m % 2, *place_of(m % 2, d))
            if to is not None:
                pairs.append((d * lat + m, device_of(m % 2, *to) * lat + m))
    return lax.ppermute(block, ("depth", "lat"), pairs)


def across(block):
    return permute(block, lambda c, team, lo, y: (team, 1 - lo, y))


def towards(block, k, e):
    def route(c, team, lo, y):
        for j, away in kept(c, team, lo):
            if away == k and y ^ e == GOAL[c][j][2]:
                return GOAL[c][j]
        return None
    return permute(block, route)


def away(block, k, e):
    def route(c, team, lo, y):
        for j in range(4):
            if GOAL[c][j] == (team, lo, y):
                there = (team + k) % 4
                return there, meet(c, there, j), y ^ e
        return None
    return permute(block, route)


def on_device(object_slices, probe, positions, measured):
    n = probe.shape[-1]
    rows, width = object_slices.shape[2:]
    depth_size = lax.axis_size("depth")
    d = lax.axis_index("depth")
    m = lax.axis_index("lat")
    plan = lax.dynamic_slice(jnp.asarray(make_plan()), (m % 2, d, 0), (1, 1, 48)).reshape(48)
    tile = object_slices[0]

    tile_bf, mine = own_windows(plan, positions, tile, measured, n)
    ahead = shifted(tile_bf, -1)
    behind = shifted(mine, 1)
    mid_places = shifted(positions, 1)
    far_places = shifted(positions, 2)
    mid_places, far_places, ahead, behind = lax.optimization_barrier((mid_places, far_places, ahead, behind))
    even, odd, given = merge(plan, mid_places, behind, tile_bf, ahead, n)

    got = across(given)
    kinds = (jnp.concatenate([even, got[0:1]]), jnp.concatenate([odd, got[1:2]]))
    order = [(2, 0), (1, 0), (3, 0), (2, 1), (1, 1), (3, 1), (0, 1)]
    messages = {(k, e): towards(kinds[k % 2], k, e) for k, e in order}
    messages[0, 0] = kinds[0]
    tables = make_tables(n, depth_size)
    slots = [(k, e) for k in range(4) for e in range(2)]
    terms = dict(zip(slots, chain(plan, mid_places, probe, behind, [messages[x] for x in slots], tables, rows)))

    got = {x: away(terms[x], *x) for x in order}
    even = terms[0, 0]
    for k, e in ((0, 1), (2, 0), (2, 1)):
        even = jnp.where(plan[EVEN] == 2 * k + e, got[k, e], even)
    odd = got[1, 0]
    for k, e in ((1, 1), (3, 0), (3, 1)):
        odd = jnp.where(plan[ODD] == 2 * k + e, got[k, e], odd)
    given = across(jnp.stack([even[1], odd[1]]))
    mixed = jnp.stack([even[0, :, :rows], odd[0, :, :rows], given[0, :, :rows], given[1, :, :rows]])
    from_own = shifted(mixed, -1)
    from_far = shifted(mixed, 1)
    total = gather_terms(plan, positions, mid_places, far_places, from_own, (even, odd, given), from_far, rows, width)
    return total[None]


def solution(mesh):
    return jax.shard_map(
        on_device,
        mesh=mesh,
        in_specs=(P("depth", None, "lat", None), P(), P("lat", None), P("lat", None, None)),
        out_specs=P("depth", None, "lat", None),
        check_vma=False,
    )
```

```python
import functools

import jax
import jax.numpy as jnp
import numpy as np
from jax import lax
from jax.experimental import pallas as pl
from jax.experimental.pallas import tpu as pltpu
from jax.sharding import PartitionSpec as P

BF = jnp.bfloat16
F32 = jnp.float32
ANY = pl.BlockSpec(memory_space=pl.ANY)
SMEM = pl.BlockSpec(memory_space=pltpu.MemorySpace.SMEM)
FIRST = 64
SECOND = 32
LAG = 2
VMEM = pl.BlockSpec(memory_space=pltpu.MemorySpace.VMEM)


@functools.lru_cache
def base_tables(n):
    k = np.arange(n)
    d = np.exp(-2j * np.pi * ((k[:, None] * k[None, :]) % n) / n) / np.sqrt(n)
    q = np.where(k < n // 2, k, k - n).astype(np.float64)
    h = np.exp(-1j * np.pi * 0.5 * q * q / n)
    prop = (np.conj(d) * h[None, :]) @ d
    return np.stack([prop.real, prop.imag, d.real, d.imag]).astype(np.float32)


def tables_kernel(scales, base, out, *, n, slices):
    s = pl.program_id(0)
    which = jnp.where(s < slices, 0, 2)
    re = base[which]
    im = base[which + 1]
    for side, sign in ((0, 1.0), (1, -1.0)):
        scale = scales[side, s]
        a = (re * scale).astype(BF)
        b = im * (scale * sign)
        out[0, side, 0:n, 0:n] = a
        out[0, side, n:2 * n, n:2 * n] = a
        out[0, side, 0:n, n:2 * n] = (-b).astype(BF)
        out[0, side, n:2 * n, 0:n] = b.astype(BF)


def make_tables(n, slices):
    a = 2.0 ** ((np.arange(slices) + 0.5) / slices)
    scales = np.concatenate([np.stack([a, 1.0 / a]), np.ones((2, 1))], axis=1).astype(np.float32)
    return pl.pallas_call(
        functools.partial(tables_kernel, n=n, slices=slices),
        grid=(slices + 1,),
        out_shape=jax.ShapeDtypeStruct((slices + 1, 2, 2 * n, 2 * n), BF),
        in_specs=[SMEM, pl.BlockSpec((4, n, n), lambda s: (0, 0, 0))],
        out_specs=pl.BlockSpec((1, 2, 2 * n, 2 * n), lambda s: (s, 0, 0, 0)),
    )(jnp.asarray(scales), jnp.asarray(base_tables(n)))


def chain_kernel(*refs, n, slices, rows):
    accs = [pltpu.ACC(c)((size, n), F32)
            for size in (FIRST, SECOND) for _ in range(2) for c in range(2) for _ in range(n // size)]
    pl.run_scoped(lambda *scoped: chain_body(*refs, *scoped, n=n, slices=slices, rows=rows), *accs)


def chain_body(plan, places, probe, behind, *refs, n, slices, rows):
    ins, tabs_hbm, near_out, far_out = refs[0:4], refs[4], refs[5:9], refs[9:13]
    (patch, tabs, inc, lhs0, lhs1, mid0, mid1, outv, target, term, psem, tsem, osem, gsem) = refs[13:27]
    accs = list(refs[27:])
    first_acc = [[[accs.pop(0) for _ in range(n // FIRST)] for _ in range(2)] for _ in range(2)]
    second_acc = [[[accs.pop(0) for _ in range(n // SECOND)] for _ in range(2)] for _ in range(2)]
    lhs, mid = (lhs0, lhs1), (mid0, mid1)
    half = n // 2

    def table_copy(s):
        return pltpu.make_async_copy(tabs_hbm.at[s], tabs.at[s], tsem.at[s])

    def patch_wait(s):
        pltpu.make_async_copy(ins[0].at[0], patch.at[s], psem.at[s]).wait()

    def span(i, size):
        return pl.ds(i * size, size)

    def issue(m, accs, size, weights, rows_of, tasks=()):
        for c in range(2):
            for k in range(2):
                pltpu.matmul_push_rhs(weights(c, k), k, c)
        pieces = 2 * (n // size)
        todo = list(tasks)
        for j in range(pieces):
            k, i = divmod(j, n // size)
            for c in range(2):
                pltpu.matmul_acc_lhs(accs[m][c][i], rows_of(c, k, i), load_staged_rhs=k if i == 0 else None)
            left = max(1, pieces - 1 - max(j, LAG))
            take = 0 if j < LAG else -(-len(todo) // left)
            for task in todo[:take]:
                task()
            del todo[:take]
        for task in todo:
            task()

    def first(m, s, side, tasks=()):
        issue(m, first_acc, FIRST, lambda c, k: lhs[m][k * n:(k + 1) * n],
              lambda c, k, i: tabs[s, side, pl.ds(c * n + i * FIRST, FIRST), k * n:(k + 1) * n], tasks)

    def turn(m):
        def one(i, c):
            mid[m][span(i, FIRST), c * n:(c + 1) * n] = pltpu.matmul_pop(first_acc[m][c][i]).astype(BF)
        return [functools.partial(one, i, c) for i in range(n // FIRST) for c in range(2)]

    def second(m, s, side, tasks=()):
        issue(m, second_acc, SECOND, lambda c, k: tabs[s, side, k * n:(k + 1) * n, c * n:(c + 1) * n],
              lambda c, k, i: mid[m][span(i, SECOND), k * n:(k + 1) * n], tasks)

    def pop(m, i):
        return pltpu.matmul_pop(second_acc[m][0][i]), pltpu.matmul_pop(second_acc[m][1][i])

    def put(m, i, re, im):
        lhs[m][pl.ds(i * SECOND, SECOND)] = re.astype(BF)
        lhs[m][pl.ds(n + i * SECOND, SECOND)] = im.astype(BF)

    def enter(s, m, i, wr, wi):
        inc[s, m, 0, span(i, SECOND)] = wr.astype(BF)
        inc[s, m, 1, span(i, SECOND)] = wi.astype(BF)
        pr = patch[s, 0, span(i, SECOND)].astype(F32)
        pi = patch[s, 1, span(i, SECOND)].astype(F32)
        put(m, i, pr * wr - pi * wi, pr * wi + pi * wr)

    def leave(s, m, i, gr, gi):
        pr = patch[s, 0, span(i, SECOND)].astype(F32)
        pi = patch[s, 1, span(i, SECOND)].astype(F32)
        put(m, i, pr * gr + pi * gi, pr * gi - pi * gr)
        wr = inc[s, m, 0, span(i, SECOND)].astype(F32)
        wi = inc[s, m, 1, span(i, SECOND)].astype(F32)
        tr = wr * gr + wi * gi
        ti = wr * gi - wi * gr
        if m == 0:
            term[0, span(i, SECOND)] = tr
            term[1, span(i, SECOND)] = ti
        else:
            outv[s, 0, span(i, SECOND)] = (term[0, span(i, SECOND)] + tr).astype(BF)
            outv[s, 1, span(i, SECOND)] = (term[1, span(i, SECOND)] + ti).astype(BF)

    count = n // SECOND

    def uses(m, use):
        return [functools.partial(lambda i: use(m, i, *pop(m, i)), i) for i in range(count)]

    def run(tasks):
        for task in tasks:
            task()

    def step(s, side, use, after=None):
        second(0, s, side, turn(1))
        second(1, s, side, uses(0, use))
        if after is None:
            run(uses(1, use))
        else:
            first(0, *after, uses(1, use))
            first(1, *after, turn(0))

    @pl.when(plan[HANDLER] == 1)
    def _():
        target_copy = pltpu.make_async_copy(behind.at[pl.ds(behind.shape[0] - 2, 2)], target, gsem)
        target_copy.start()
        for s in range(slices):
            table_copy(s).start()
            for r in range(4):
                @pl.when(plan[REL + s] == r)
                def _():
                    pltpu.make_async_copy(ins[r].at[plan[ENTRY + s]], patch.at[s], psem.at[s]).start()
        table_copy(slices).start()
        row_shift = lax.rem(places[plan[POSITION], 0], rows)
        col_shift = lax.rem(places[plan[POSITION], 1], n)
        for m in range(2):
            for c in range(2):
                x = pltpu.roll(probe[m, c], row_shift, 0)
                term[c] = pltpu.roll(x, col_shift, 1).astype(BF).astype(F32)
            if m == 0:
                patch_wait(0)
                table_copy(0).wait()
            for i in range(count):
                enter(0, m, i, term[0, span(i, SECOND)], term[1, span(i, SECOND)])
            first(m, 0, 0)
        run(turn(0))

        def forward(s, carry):
            table_copy(s + 1).wait()
            patch_wait(s + 1)
            step(s, 1, lambda m, i, re, im: enter(s + 1, m, i, re, im), (s + 1, 0))
            return carry

        lax.fori_loop(0, slices - 1, forward, 0)
        table_copy(slices).wait()
        step(slices - 1, 1, put, (slices, 0))
        target_copy.wait()
        second(0, slices, 1, turn(1))
        second(1, slices, 1)
        for i in range(count):
            ar, ai = pop(0, i)
            br, bi = pop(1, i)
            h, at = divmod(i * SECOND, half)
            wanted = target[0, h, pl.ds(at, SECOND)].astype(F32) + target[1, h, pl.ds(at, SECOND)].astype(F32)
            resid = (ar * ar + ai * ai) + (br * br + bi * bi) - wanted
            put(0, i, resid * ar, resid * ai)
            put(1, i, resid * br, resid * bi)
        first(0, slices, 1)
        first(1, slices, 1, turn(0))
        step(slices, 0, put, (slices - 1, 1))

        def send(s):
            for r in range(4):
                @pl.when(plan[REL + s] == r)
                def _():
                    for h, group in enumerate((near_out, far_out)):
                        pltpu.make_async_copy(outv.at[s, :, pl.ds(h * half, half)], group[r].at[plan[ENTRY + s]], osem.at[h, s]).start()

        def backward(back, carry):
            s = slices - 1 - back
            step(s, 0, lambda m, i, re, im: leave(s, m, i, re, im), (s - 1, 1))
            send(s)
            return carry

        lax.fori_loop(0, slices - 1, backward, 0)
        step(0, 0, lambda m, i, re, im: leave(0, m, i, re, im))
        send(0)
        for s in range(slices):
            for h in range(2):
                pltpu.make_async_copy(outv.at[s, :, pl.ds(h * half, half)], near_out[0].at[0], osem.at[h, s]).wait()


def chain(plan, places, probe, behind, messages, tables, rows):
    n = probe.shape[-1]
    slices = tables.shape[0] - 1
    piece = jax.ShapeDtypeStruct((slices // 4, 2, n // 2, n), BF)
    return pl.pallas_call(
        functools.partial(chain_kernel, n=n, slices=slices, rows=rows),
        out_shape=(piece,) * 8,
        in_specs=[SMEM, SMEM, VMEM] + [ANY] * 6,
        out_specs=(ANY,) * 8,
        scratch_shapes=[
            pltpu.VMEM((slices, 2, n, n), BF),
            pltpu.VMEM((slices + 1, 2, 2 * n, 2 * n), BF),
            pltpu.VMEM((slices, 2, 2, n, n), BF),
            pltpu.VMEM((2 * n, n), BF),
            pltpu.VMEM((2 * n, n), BF),
            pltpu.VMEM((n, 2 * n), BF),
            pltpu.VMEM((n, 2 * n), BF),
            pltpu.VMEM((slices, 2, n, n), BF),
            pltpu.VMEM((2, 2, n // 2, n), BF),
            pltpu.VMEM((2, n, n), F32),
            pltpu.SemaphoreType.DMA((slices,)),
            pltpu.SemaphoreType.DMA((slices + 1,)),
            pltpu.SemaphoreType.DMA((2, slices)),
            pltpu.SemaphoreType.DMA,
        ],
        compiler_params=pltpu.CompilerParams(vmem_limit_bytes=58 << 20),
    )(plan, places, probe, behind, *messages, tables)


def window(ref, lead, offset, n):
    width = ref.shape[-1]
    start = pl.multiple_of((offset // n) * n, n)
    after = pl.multiple_of(jnp.minimum(start + n, width - n), n)
    lane = lax.broadcasted_iota(jnp.int32, (ref.shape[-2], n), 1)
    first = ref[lead, :, pl.ds(start, n)].astype(F32)
    second = ref[lead, :, pl.ds(after, n)].astype(F32)
    return jnp.where(lane >= offset % n, first, second)


def own_windows_kernel(places, tile_hbm, measured, tile_bf, wins, tile, target, sems, *, n, ahead_at, parts=4):
    rows = tile_hbm.shape[1]
    size = rows // parts
    copies = [pltpu.make_async_copy(tile_hbm.at[:, pl.ds(q * size, size)], tile.at[:, pl.ds(q * size, size)], sems.at[q])
              for q in range(parts)]
    for copy in copies:
        copy.start()
    me = lax.axis_index("lat") % 2 * 16 + lax.axis_index("depth")
    which = jnp.int32(0)
    for at, position in enumerate(ahead_at):
        which = jnp.where(me == at, jnp.int32(position), which)
    wanted = pltpu.make_async_copy(measured.at[which], target, sems.at[parts])
    wanted.start()
    for q, copy in enumerate(copies):
        copy.wait()
        part = pl.ds(q * size, size)
        tile_bf[:, part] = tile[:, part].astype(BF)
        for p in range(places.shape[0]):
            for c in range(2):
                wins[p, c, part] = window(tile.at[:, part], c, places[p, 1], n).astype(BF)
    wanted.wait()
    for c in range(2):
        x = target[c * rows:(c + 1) * rows]
        high = x.astype(BF)
        wins[places.shape[0], c] = high
        wins[places.shape[0] + 1, c] = (x - high.astype(F32)).astype(BF)


def own_windows(places, tile, measured, n):
    count = places.shape[0]
    hbm = functools.partial(pltpu.with_memory_space_constraint, memory_space=pltpu.HBM)
    ahead_at = tuple(int(x) for x in make_plan()[:, :, OTHER].ravel())
    return pl.pallas_call(
        functools.partial(own_windows_kernel, n=n, ahead_at=ahead_at),
        out_shape=(jax.ShapeDtypeStruct(tile.shape, BF), jax.ShapeDtypeStruct((count + 2, 2, tile.shape[1], n), BF)),
        in_specs=[SMEM, ANY, ANY],
        out_specs=(VMEM, VMEM),
        scratch_shapes=[pltpu.VMEM(tile.shape, F32), pltpu.VMEM((n, n), F32), pltpu.SemaphoreType.DMA((5,))],
        compiler_params=pltpu.CompilerParams(vmem_limit_bytes=40 << 20),
    )(places, hbm(tile), hbm(measured))


def merge_kernel(plan, places, behind, tile, ahead, *outs, n):
    rows = tile.shape[1]
    row = lax.broadcasted_iota(jnp.int32, (rows, n), 0)
    for k in range(4):
        p = plan[ORDER + k]
        for c in range(2):
            far = window(ahead, c, places[p, 1], n)
            near = behind[p, c].astype(F32)
            outs[k][c, 0:rows] = jnp.where(row >= places[p, 0] % rows, near, far).astype(BF)
            outs[k][c, rows:2 * rows] = window(tile, c, places[p, 1], n).astype(BF)


def merge(plan, places, behind, tile, ahead, n):
    return pl.pallas_call(
        functools.partial(merge_kernel, n=n),
        out_shape=(jax.ShapeDtypeStruct((2, 2 * tile.shape[1], n), BF),) * 4,
        in_specs=[SMEM, SMEM, VMEM, VMEM, VMEM],
        out_specs=(VMEM,) * 4,
        compiler_params=pltpu.CompilerParams(vmem_limit_bytes=40 << 20),
    )(plan, places, behind, tile, ahead)


def gather_kernel(plan, own_places, mid_places, far_places, from_own, m0, m1, m2, m3, from_far, out, *, n):
    rows = out.shape[1]
    width = out.shape[-1]
    row = lax.broadcasted_iota(jnp.int32, (rows, n), 0)
    lane = lax.broadcasted_iota(jnp.int32, (rows, n), 1)
    out[...] = jnp.zeros_like(out)
    mids = (m0, m1, m2, m3)
    for places, kind, order in ((own_places, 0, OTHER), (mid_places, 1, ORDER), (far_places, 2, OTHER)):
        for k in range(4):
            p = plan[order + k]
            shift = places[p, 0] % rows
            offset = places[p, 1]
            start = pl.multiple_of((offset // n) * n, n)
            after = pl.multiple_of(jnp.minimum(start + n, width - n), n)
            for c in range(2):
                if kind == 0:
                    term = jnp.where(row >= shift, from_own[k, c].astype(F32), 0.0)
                elif kind == 1:
                    term = mids[k][c].astype(F32)
                else:
                    term = jnp.where(row < shift, from_far[k, c].astype(F32), 0.0)
                here = lane >= offset % n
                out[c, :, pl.ds(start, n)] += jnp.where(here, term, 0.0)
                out[c, :, pl.ds(after, n)] += jnp.where(here, 0.0, term)


def gather_terms(plan, own_places, mid_places, far_places, from_own, mids, from_far, rows, width):
    n = from_own.shape[-1]
    return pl.pallas_call(
        functools.partial(gather_kernel, n=n),
        out_shape=jax.ShapeDtypeStruct((2, rows, width), F32),
        in_specs=[SMEM] * 4 + [VMEM] * 6,
        out_specs=VMEM,
        compiler_params=pltpu.CompilerParams(vmem_limit_bytes=40 << 20),
    )(plan, own_places, mid_places, far_places, from_own, *mids, from_far)


def shifted(block, distance):
    size = lax.axis_size("lat")
    return lax.ppermute(block, "lat", [(i, (i + distance) % size) for i in range(size)])


HANDLER, POSITION, SOURCE, ORDER, OTHER, REL, ENTRY = 0, 1, 2, 3, 7, 11, 27
GOAL = (((0, 0), (1, 1), (2, 0), (3, 1)), ((1, 2), (0, 3), (3, 2), (2, 3)))


def meet(c, team, j):
    goal, inner = GOAL[c][j]
    flip = inner ^ 2
    if c == 0:
        return inner if (team - goal) % 4 in (0, 1) else flip
    return inner if (team - goal) % 4 in (0, 3) else flip


def place_of(c, d):
    v = (d + 2 * c) % 16
    return v // 4, v % 4


def position_at(c, team, inner):
    found = [j for j in range(4) if meet(c, team, j) == inner]
    assert len(found) == 1
    return found[0]


def device_of(c, team, inner):
    return (4 * team + inner - 2 * c) % 16


@functools.lru_cache
def make_plan():
    out = np.zeros((2, 16, 48), np.int32)
    for c in range(2):
        for d in range(16):
            team, inner = place_of(c, d)
            j = position_at(c, team, inner)
            row = out[c, d]
            row[HANDLER] = GOAL[c][j] == (team, inner)
            row[POSITION] = j
            row[SOURCE] = (team - GOAL[c][j][0]) % 4
            other = place_of(1 - c, d)
            for k in range(4):
                row[ORDER + k] = position_at(c, team, inner ^ k)
                row[OTHER + k] = position_at(1 - c, other[0], other[1] ^ k)
            for s in range(16):
                there, at = place_of(c, s)
                row[REL + s] = (there - team) % 4
                row[ENTRY + s] = at ^ meet(c, there, j)
    return out


def permute(block, route):
    depth, lat = lax.axis_size("depth"), lax.axis_size("lat")
    pairs = []
    for d in range(depth):
        for m in range(lat):
            to = route(m % 2, *place_of(m % 2, d))
            if to is not None:
                pairs.append((d * lat + m, device_of(m % 2, *to) * lat + m))
    return lax.ppermute(block, ("depth", "lat"), pairs)


def within(block, k):
    return permute(block, lambda c, team, inner: (team, inner ^ k))


def towards(block, k):
    def route(c, team, inner):
        goal = GOAL[c][position_at(c, team, inner)]
        return goal if (team - goal[0]) % 4 == k else None
    return permute(block, route)


def away(block, k):
    def route(c, team, inner):
        j = position_at(c, team, inner)
        there = (team + k) % 4
        return (there, meet(c, there, j)) if GOAL[c][j] == (team, inner) else None
    return permute(block, route)


def on_device(object_slices, probe, positions, measured):
    n = probe.shape[-1]
    rows, width = object_slices.shape[2:]
    depth_size = lax.axis_size("depth")
    d = lax.axis_index("depth")
    m = lax.axis_index("lat")
    plan = lax.dynamic_slice(jnp.asarray(make_plan()), (m % 2, d, 0), (1, 1, 48)).reshape(48)
    tile = object_slices[0]

    tile_bf, mine = own_windows(positions, tile, measured, n)
    ahead = shifted(tile_bf, -1)
    behind = shifted(mine, 1)
    mid_places = shifted(positions, 1)
    far_places = shifted(positions, 2)
    mid_places, far_places, ahead, behind = lax.optimization_barrier((mid_places, far_places, ahead, behind))
    parts = merge(plan, mid_places, behind, tile_bf, ahead, n)

    message = jnp.stack([parts[0]] + [within(parts[k], k) for k in (1, 2, 3)])
    messages = [message] + [towards(message, k) for k in (1, 2, 3)]
    tables = make_tables(n, depth_size)
    terms = chain(plan, mid_places, probe, behind, messages, tables, rows)

    def home(pieces):
        block = pieces[0]
        for k in (1, 2, 3):
            block = jnp.where(plan[SOURCE] == k, away(pieces[k], k), block)
        return block

    near_block = home(terms[:4])
    far_block = home(terms[4:])
    mixed = jnp.stack([near_block[0]] + [within(near_block[k], k) for k in (1, 2, 3)])
    mids = [far_block[0]] + [within(far_block[k], k) for k in (1, 2, 3)]
    from_own = shifted(mixed, -1)
    from_far = shifted(mixed, 1)
    total = gather_terms(plan, positions, mid_places, far_places, from_own, mids, from_far, rows, width)
    return total[None]


def solution(mesh):
    return jax.shard_map(
        on_device,
        mesh=mesh,
        in_specs=(P("depth", None, "lat", None), P(), P("lat", None), P("lat", None, None)),
        out_specs=P("depth", None, "lat", None),
        check_vma=False,
    )
```

```python
import functools

import jax
import jax.numpy as jnp
import numpy as np
from jax import lax
from jax.experimental import pallas as pl
from jax.experimental.pallas import tpu as pltpu
from jax.sharding import PartitionSpec as P

BF = jnp.bfloat16
F32 = jnp.float32
ANY = pl.BlockSpec(memory_space=pl.ANY)
SMEM = pl.BlockSpec(memory_space=pltpu.MemorySpace.SMEM)
FIRST = 64
SECOND = 32
LAG = 2
VMEM = pl.BlockSpec(memory_space=pltpu.MemorySpace.VMEM)


@functools.lru_cache
def base_tables(n):
    k = np.arange(n)
    d = np.exp(-2j * np.pi * ((k[:, None] * k[None, :]) % n) / n) / np.sqrt(n)
    q = np.where(k < n // 2, k, k - n).astype(np.float64)
    h = np.exp(-1j * np.pi * 0.5 * q * q / n)
    prop = (np.conj(d) * h[None, :]) @ d
    return np.stack([prop.real, prop.imag, d.real, d.imag]).astype(np.float32)


def tables_kernel(scales, base, out, *, n, slices):
    s = pl.program_id(0)
    which = jnp.where(s < slices, 0, 2)
    re = base[which]
    im = base[which + 1]
    for side, sign in ((0, 1.0), (1, -1.0)):
        scale = scales[side, s]
        a = (re * scale).astype(BF)
        b = im * (scale * sign)
        out[0, side, 0:n, 0:n] = a
        out[0, side, n:2 * n, n:2 * n] = a
        out[0, side, 0:n, n:2 * n] = (-b).astype(BF)
        out[0, side, n:2 * n, 0:n] = b.astype(BF)


def make_tables(n, slices):
    a = 2.0 ** ((np.arange(slices) + 0.5) / slices)
    scales = np.concatenate([np.stack([a, 1.0 / a]), np.ones((2, 1))], axis=1).astype(np.float32)
    return pl.pallas_call(
        functools.partial(tables_kernel, n=n, slices=slices),
        grid=(slices + 1,),
        out_shape=jax.ShapeDtypeStruct((slices + 1, 2, 2 * n, 2 * n), BF),
        in_specs=[SMEM, pl.BlockSpec((4, n, n), lambda s: (0, 0, 0))],
        out_specs=pl.BlockSpec((1, 2, 2 * n, 2 * n), lambda s: (s, 0, 0, 0)),
    )(jnp.asarray(scales), jnp.asarray(base_tables(n)))


def chain_kernel(*refs, n, slices):
    accs = [pltpu.ACC(c)((size, n), F32)
            for size in (FIRST, SECOND) for _ in range(2) for c in range(2) for _ in range(n // size)]
    pl.run_scoped(lambda *scoped: chain_body(*refs, *scoped, n=n, slices=slices), *accs)


def chain_body(plan, wave, behind, *refs, n, slices):
    ins, tabs_hbm, near_out, far_out = refs[0:4], refs[4], refs[5:9], refs[9:13]
    (patch, tabs, inc, lhs0, lhs1, mid0, mid1, outv, target, term, psem, tsem, osem, gsem) = refs[13:27]
    accs = list(refs[27:])
    first_acc = [[[accs.pop(0) for _ in range(n // FIRST)] for _ in range(2)] for _ in range(2)]
    second_acc = [[[accs.pop(0) for _ in range(n // SECOND)] for _ in range(2)] for _ in range(2)]
    lhs, mid = (lhs0, lhs1), (mid0, mid1)
    half = n // 2

    def table_copy(s):
        return pltpu.make_async_copy(tabs_hbm.at[s], tabs.at[s], tsem.at[s])

    def patch_wait(s):
        pltpu.make_async_copy(ins[0].at[0], patch.at[s], psem.at[s]).wait()

    def span(i, size):
        return pl.ds(i * size, size)

    def issue(m, accs, size, weights, rows_of, tasks=()):
        for c in range(2):
            for k in range(2):
                pltpu.matmul_push_rhs(weights(c, k), k, c)
        pieces = 2 * (n // size)
        todo = list(tasks)
        for j in range(pieces):
            k, i = divmod(j, n // size)
            for c in range(2):
                pltpu.matmul_acc_lhs(accs[m][c][i], rows_of(c, k, i), load_staged_rhs=k if i == 0 else None)
            left = max(1, pieces - 1 - max(j, LAG))
            take = 0 if j < LAG else -(-len(todo) // left)
            for task in todo[:take]:
                task()
            del todo[:take]
        for task in todo:
            task()

    def first(m, s, side, tasks=()):
        issue(m, first_acc, FIRST, lambda c, k: lhs[m][k * n:(k + 1) * n],
              lambda c, k, i: tabs[s, side, pl.ds(c * n + i * FIRST, FIRST), k * n:(k + 1) * n], tasks)

    def turn(m):
        def one(i, c):
            mid[m][span(i, FIRST), c * n:(c + 1) * n] = pltpu.matmul_pop(first_acc[m][c][i]).astype(BF)
        return [functools.partial(one, i, c) for i in range(n // FIRST) for c in range(2)]

    def second(m, s, side, tasks=()):
        issue(m, second_acc, SECOND, lambda c, k: tabs[s, side, k * n:(k + 1) * n, c * n:(c + 1) * n],
              lambda c, k, i: mid[m][span(i, SECOND), k * n:(k + 1) * n], tasks)

    def pop(m, i):
        return pltpu.matmul_pop(second_acc[m][0][i]), pltpu.matmul_pop(second_acc[m][1][i])

    def put(m, i, re, im):
        lhs[m][pl.ds(i * SECOND, SECOND)] = re.astype(BF)
        lhs[m][pl.ds(n + i * SECOND, SECOND)] = im.astype(BF)

    def enter(s, m, i, wr, wi):
        inc[s, m, 0, span(i, SECOND)] = wr.astype(BF)
        inc[s, m, 1, span(i, SECOND)] = wi.astype(BF)
        pr = patch[s, 0, span(i, SECOND)].astype(F32)
        pi = patch[s, 1, span(i, SECOND)].astype(F32)
        put(m, i, pr * wr - pi * wi, pr * wi + pi * wr)

    def leave(s, m, i, gr, gi):
        pr = patch[s, 0, span(i, SECOND)].astype(F32)
        pi = patch[s, 1, span(i, SECOND)].astype(F32)
        put(m, i, pr * gr + pi * gi, pr * gi - pi * gr)
        wr = inc[s, m, 0, span(i, SECOND)].astype(F32)
        wi = inc[s, m, 1, span(i, SECOND)].astype(F32)
        tr = wr * gr + wi * gi
        ti = wr * gi - wi * gr
        if m == 0:
            term[0, span(i, SECOND)] = tr
            term[1, span(i, SECOND)] = ti
        else:
            outv[s, 0, span(i, SECOND)] = (term[0, span(i, SECOND)] + tr).astype(BF)
            outv[s, 1, span(i, SECOND)] = (term[1, span(i, SECOND)] + ti).astype(BF)

    count = n // SECOND

    def uses(m, use):
        return [functools.partial(lambda i: use(m, i, *pop(m, i)), i) for i in range(count)]

    def run(tasks):
        for task in tasks:
            task()

    def step(s, side, use, after=None):
        second(0, s, side, turn(1))
        second(1, s, side, uses(0, use))
        if after is None:
            run(uses(1, use))
        else:
            first(0, *after, uses(1, use))
            first(1, *after, turn(0))

    @pl.when(plan[HANDLER] == 1)
    def _():
        target_copy = pltpu.make_async_copy(behind.at[pl.ds(behind.shape[0] - 2, 2)], target, gsem)
        target_copy.start()
        for s in range(slices):
            table_copy(s).start()
            for r in range(4):
                @pl.when(plan[REL + s] == r)
                def _():
                    pltpu.make_async_copy(ins[r].at[plan[ENTRY + s]], patch.at[s], psem.at[s]).start()
        table_copy(slices).start()
        patch_wait(0)
        table_copy(0).wait()
        for m in range(2):
            for i in range(count):
                enter(0, m, i, wave[m, 0, span(i, SECOND)].astype(F32), wave[m, 1, span(i, SECOND)].astype(F32))
            first(m, 0, 0)
        run(turn(0))

        def forward(s, carry):
            table_copy(s + 1).wait()
            patch_wait(s + 1)
            step(s, 1, lambda m, i, re, im: enter(s + 1, m, i, re, im), (s + 1, 0))
            return carry

        lax.fori_loop(0, slices - 1, forward, 0)
        table_copy(slices).wait()
        step(slices - 1, 1, put, (slices, 0))
        target_copy.wait()
        second(0, slices, 1, turn(1))
        second(1, slices, 1)
        for i in range(count):
            ar, ai = pop(0, i)
            br, bi = pop(1, i)
            h, at = divmod(i * SECOND, half)
            wanted = target[0, h, pl.ds(at, SECOND)].astype(F32) + target[1, h, pl.ds(at, SECOND)].astype(F32)
            resid = (ar * ar + ai * ai) + (br * br + bi * bi) - wanted
            put(0, i, resid * ar, resid * ai)
            put(1, i, resid * br, resid * bi)
        first(0, slices, 1)
        first(1, slices, 1, turn(0))
        step(slices, 0, put, (slices - 1, 1))

        def send(s):
            for r in range(4):
                @pl.when(plan[REL + s] == r)
                def _():
                    for h, group in enumerate((near_out, far_out)):
                        pltpu.make_async_copy(outv.at[s, :, pl.ds(h * half, half)], group[r].at[plan[ENTRY + s]], osem.at[h, s]).start()

        def backward(back, carry):
            s = slices - 1 - back
            step(s, 0, lambda m, i, re, im: leave(s, m, i, re, im), (s - 1, 1))
            send(s)
            return carry

        lax.fori_loop(0, slices - 1, backward, 0)
        step(0, 0, lambda m, i, re, im: leave(0, m, i, re, im))
        send(0)
        for s in range(slices):
            for h in range(2):
                pltpu.make_async_copy(outv.at[s, :, pl.ds(h * half, half)], near_out[0].at[0], osem.at[h, s]).wait()


def chain(plan, wave, behind, messages, tables):
    n = wave.shape[-1]
    slices = tables.shape[0] - 1
    piece = jax.ShapeDtypeStruct((slices // 4, 2, n // 2, n), BF)
    return pl.pallas_call(
        functools.partial(chain_kernel, n=n, slices=slices),
        out_shape=(piece,) * 8,
        in_specs=[SMEM, VMEM] + [ANY] * 6,
        out_specs=(ANY,) * 8,
        scratch_shapes=[
            pltpu.VMEM((slices, 2, n, n), BF),
            pltpu.VMEM((slices + 1, 2, 2 * n, 2 * n), BF),
            pltpu.VMEM((slices, 2, 2, n, n), BF),
            pltpu.VMEM((2 * n, n), BF),
            pltpu.VMEM((2 * n, n), BF),
            pltpu.VMEM((n, 2 * n), BF),
            pltpu.VMEM((n, 2 * n), BF),
            pltpu.VMEM((slices, 2, n, n), BF),
            pltpu.VMEM((2, 2, n // 2, n), BF),
            pltpu.VMEM((2, n, n), F32),
            pltpu.SemaphoreType.DMA((slices,)),
            pltpu.SemaphoreType.DMA((slices + 1,)),
            pltpu.SemaphoreType.DMA((2, slices)),
            pltpu.SemaphoreType.DMA,
        ],
        compiler_params=pltpu.CompilerParams(vmem_limit_bytes=58 << 20),
    )(plan, wave, behind, *messages, tables)


def window(ref, lead, offset, n):
    width = ref.shape[-1]
    start = pl.multiple_of((offset // n) * n, n)
    after = pl.multiple_of(jnp.minimum(start + n, width - n), n)
    lane = lax.broadcasted_iota(jnp.int32, (ref.shape[-2], n), 1)
    first = ref[lead, :, pl.ds(start, n)].astype(F32)
    second = ref[lead, :, pl.ds(after, n)].astype(F32)
    return jnp.where(lane >= offset % n, first, second)


def own_windows_kernel(places, tile, measured, wins, target, sem, *, n, ahead_at):
    rows = tile.shape[1]
    me = lax.axis_index("lat") % 2 * 16 + lax.axis_index("depth")
    which = jnp.int32(0)
    for at, position in enumerate(ahead_at):
        which = jnp.where(me == at, jnp.int32(position), which)
    wanted = pltpu.make_async_copy(measured.at[which], target, sem)
    wanted.start()
    for p in range(places.shape[0]):
        for c in range(2):
            wins[p, c] = window(tile, c, places[p, 1], n).astype(BF)
    wanted.wait()
    for c in range(2):
        x = target[c * rows:(c + 1) * rows]
        high = x.astype(BF)
        wins[places.shape[0], c] = high
        wins[places.shape[0] + 1, c] = (x - high.astype(F32)).astype(BF)


def own_windows(places, tile, measured, n):
    count = places.shape[0]
    ahead_at = tuple(int(x) for x in make_plan()[:, :, OTHER].ravel())
    return pl.pallas_call(
        functools.partial(own_windows_kernel, n=n, ahead_at=ahead_at),
        out_shape=jax.ShapeDtypeStruct((count + 2, 2, tile.shape[1], n), BF),
        in_specs=[SMEM, VMEM, ANY],
        out_specs=VMEM,
        scratch_shapes=[pltpu.VMEM((n, n), F32), pltpu.SemaphoreType.DMA],
        compiler_params=pltpu.CompilerParams(vmem_limit_bytes=40 << 20),
    )(places, tile, pltpu.with_memory_space_constraint(measured, pltpu.HBM))


def roll_kernel(plan, places, probe, out, *, rows, n):
    row_shift = lax.rem(places[plan[POSITION], 0], rows)
    col_shift = lax.rem(places[plan[POSITION], 1], n)
    for m in range(probe.shape[0]):
        for c in range(2):
            x = pltpu.roll(probe[m, c], row_shift, 0)
            out[m, c] = pltpu.roll(x, col_shift, 1).astype(BF)


def roll_probe(plan, places, probe, rows):
    return pl.pallas_call(
        functools.partial(roll_kernel, rows=rows, n=probe.shape[-1]),
        out_shape=jax.ShapeDtypeStruct(probe.shape, BF),
        in_specs=[SMEM, SMEM, VMEM],
        out_specs=VMEM,
        compiler_params=pltpu.CompilerParams(vmem_limit_bytes=40 << 20),
    )(plan, places, probe)


def merge_kernel(plan, places, behind, tile, ahead, *outs, n):
    rows = tile.shape[1]
    row = lax.broadcasted_iota(jnp.int32, (rows, n), 0)
    for k in range(4):
        p = plan[ORDER + k]
        for c in range(2):
            far = window(ahead, c, places[p, 1], n)
            near = behind[p, c].astype(F32)
            outs[k][c, 0:rows] = jnp.where(row >= places[p, 0] % rows, near, far).astype(BF)
            outs[k][c, rows:2 * rows] = window(tile, c, places[p, 1], n).astype(BF)


def merge(plan, places, behind, tile, ahead, n):
    return pl.pallas_call(
        functools.partial(merge_kernel, n=n),
        out_shape=(jax.ShapeDtypeStruct((2, 2 * tile.shape[1], n), BF),) * 4,
        in_specs=[SMEM, SMEM, VMEM, VMEM, VMEM],
        out_specs=(VMEM,) * 4,
        compiler_params=pltpu.CompilerParams(vmem_limit_bytes=40 << 20),
    )(plan, places, behind, tile, ahead)


def add_window(out, places, p, c, term, n):
    width = out.shape[-1]
    offset = places[p, 1]
    start = pl.multiple_of((offset // n) * n, n)
    after = pl.multiple_of(jnp.minimum(start + n, width - n), n)
    here = lax.broadcasted_iota(jnp.int32, term.shape, 1) >= offset % n
    out[c, :, pl.ds(start, n)] += jnp.where(here, term, 0.0)
    out[c, :, pl.ds(after, n)] += jnp.where(here, 0.0, term)


def halo_terms_kernel(plan, own_places, far_places, from_own, from_far, out, *, n):
    rows = out.shape[1]
    row = lax.broadcasted_iota(jnp.int32, (rows, n), 0)
    out[...] = jnp.zeros_like(out)
    for k in range(4):
        p = plan[OTHER + k]
        for c in range(2):
            term = jnp.where(row >= own_places[p, 0] % rows, from_own[k, c].astype(F32), 0.0)
            add_window(out, own_places, p, c, term, n)
            term = jnp.where(row < far_places[p, 0] % rows, from_far[k, c].astype(F32), 0.0)
            add_window(out, far_places, p, c, term, n)


def halo_terms(plan, own_places, far_places, from_own, from_far, width):
    _, _, rows, n = from_own.shape
    return pl.pallas_call(
        functools.partial(halo_terms_kernel, n=n),
        out_shape=jax.ShapeDtypeStruct((2, rows, width), F32),
        in_specs=[SMEM] * 3 + [VMEM] * 2,
        out_specs=VMEM,
        compiler_params=pltpu.CompilerParams(vmem_limit_bytes=40 << 20),
    )(plan, own_places, far_places, from_own, from_far)


def own_terms_kernel(plan, places, total, m0, m1, m2, m3, out_hbm, out, sems, *, n):
    out[...] = total[...]
    for c in range(2):
        for k, ref in enumerate((m0, m1, m2, m3)):
            add_window(out, places, plan[ORDER + k], c, ref[c].astype(F32), n)
        pltpu.make_async_copy(out.at[c], out_hbm.at[c], sems.at[c]).start()
    for c in range(2):
        pltpu.make_async_copy(out.at[c], out_hbm.at[c], sems.at[c]).wait()


def own_terms(plan, places, total, mids):
    return pl.pallas_call(
        functools.partial(own_terms_kernel, n=mids[0].shape[-1]),
        out_shape=jax.ShapeDtypeStruct(total.shape, F32),
        in_specs=[SMEM] * 2 + [VMEM] * 5,
        out_specs=ANY,
        scratch_shapes=[pltpu.VMEM(total.shape, F32), pltpu.SemaphoreType.DMA((2,))],
        compiler_params=pltpu.CompilerParams(vmem_limit_bytes=40 << 20),
    )(plan, places, total, *mids)


def shifted(block, distance):
    size = lax.axis_size("lat")
    return lax.ppermute(block, "lat", [(i, (i + distance) % size) for i in range(size)])


HANDLER, POSITION, SOURCE, ORDER, OTHER, REL, ENTRY = 0, 1, 2, 3, 7, 11, 27
GOAL = (((0, 0), (1, 1), (2, 0), (3, 1)), ((1, 2), (0, 3), (3, 2), (2, 3)))


def meet(c, team, j):
    goal, inner = GOAL[c][j]
    flip = inner ^ 2
    if c == 0:
        return inner if (team - goal) % 4 in (0, 1) else flip
    return inner if (team - goal) % 4 in (0, 3) else flip


def place_of(c, d):
    v = (d + 2 * c) % 16
    return v // 4, v % 4


def position_at(c, team, inner):
    found = [j for j in range(4) if meet(c, team, j) == inner]
    assert len(found) == 1
    return found[0]


def device_of(c, team, inner):
    return (4 * team + inner - 2 * c) % 16


@functools.lru_cache
def make_plan():
    out = np.zeros((2, 16, 48), np.int32)
    for c in range(2):
        for d in range(16):
            team, inner = place_of(c, d)
            j = position_at(c, team, inner)
            row = out[c, d]
            row[HANDLER] = GOAL[c][j] == (team, inner)
            row[POSITION] = j
            row[SOURCE] = (team - GOAL[c][j][0]) % 4
            other = place_of(1 - c, d)
            for k in range(4):
                row[ORDER + k] = position_at(c, team, inner ^ k)
                row[OTHER + k] = position_at(1 - c, other[0], other[1] ^ k)
            for s in range(16):
                there, at = place_of(c, s)
                row[REL + s] = (there - team) % 4
                row[ENTRY + s] = at ^ meet(c, there, j)
    return out


def permute(block, route):
    depth, lat = lax.axis_size("depth"), lax.axis_size("lat")
    pairs = []
    for d in range(depth):
        for m in range(lat):
            to = route(m % 2, *place_of(m % 2, d))
            if to is not None:
                pairs.append((d * lat + m, device_of(m % 2, *to) * lat + m))
    return lax.ppermute(block, ("depth", "lat"), pairs)


def within(block, k):
    return permute(block, lambda c, team, inner: (team, inner ^ k))


def towards(block, k):
    def route(c, team, inner):
        goal = GOAL[c][position_at(c, team, inner)]
        return goal if (team - goal[0]) % 4 == k else None
    return permute(block, route)


def away(block, k):
    def route(c, team, inner):
        j = position_at(c, team, inner)
        there = (team + k) % 4
        return (there, meet(c, there, j)) if GOAL[c][j] == (team, inner) else None
    return permute(block, route)


def on_device(object_slices, probe, positions, measured):
    n = probe.shape[-1]
    rows, width = object_slices.shape[2:]
    depth_size = lax.axis_size("depth")
    d = lax.axis_index("depth")
    m = lax.axis_index("lat")
    plan = lax.dynamic_slice(jnp.asarray(make_plan()), (m % 2, d, 0), (1, 1, 48)).reshape(48)
    tile = object_slices[0]

    tile_bf = tile.astype(BF)
    ahead = shifted(tile_bf, -1)
    mine = own_windows(positions, tile_bf, measured, n)
    behind = shifted(mine, 1)
    mid_places = shifted(positions, 1)
    far_places = shifted(positions, 2)
    mid_places, far_places, ahead, behind = lax.optimization_barrier((mid_places, far_places, ahead, behind))
    parts = merge(plan, mid_places, behind, tile_bf, ahead, n)

    message = jnp.stack([parts[0]] + [within(parts[k], k) for k in (1, 2, 3)])
    messages = [message] + [towards(message, k) for k in (1, 2, 3)]
    tables = make_tables(n, depth_size)
    wave = roll_probe(plan, mid_places, probe, rows)
    terms = chain(plan, wave, behind, messages, tables)

    def home(pieces):
        block = pieces[0]
        for k in (1, 2, 3):
            block = jnp.where(plan[SOURCE] == k, away(pieces[k], k), block)
        return block

    near_block = home(terms[:4])
    far_block = home(terms[4:])
    mixed = jnp.stack([near_block[0]] + [within(near_block[k], k) for k in (1, 2, 3)])
    mids = [far_block[0]] + [within(far_block[k], k) for k in (1, 2, 3)]
    from_own = shifted(mixed, -1)
    from_far = shifted(mixed, 1)
    total = halo_terms(plan, positions, far_places, from_own, from_far, width)
    return own_terms(plan, mid_places, total, mids)[None]


def solution(mesh):
    return jax.shard_map(
        on_device,
        mesh=mesh,
        in_specs=(P("depth", None, "lat", None), P(), P("lat", None), P("lat", None, None)),
        out_specs=P("depth", None, "lat", None),
        check_vma=False,
    )
```

```python
import functools

import jax
import jax.numpy as jnp
import numpy as np
from jax import lax
from jax.experimental import pallas as pl
from jax.experimental.pallas import tpu as pltpu
from jax.sharding import PartitionSpec as P

BF = jnp.bfloat16
F32 = jnp.float32
ANY = pl.BlockSpec(memory_space=pl.ANY)
SMEM = pl.BlockSpec(memory_space=pltpu.MemorySpace.SMEM)
FIRST = 64
SECOND = 32
LAG = 2
VMEM = pl.BlockSpec(memory_space=pltpu.MemorySpace.VMEM)


@functools.lru_cache
def base_tables(n):
    k = np.arange(n)
    d = np.exp(-2j * np.pi * ((k[:, None] * k[None, :]) % n) / n) / np.sqrt(n)
    q = np.where(k < n // 2, k, k - n).astype(np.float64)
    h = np.exp(-1j * np.pi * 0.5 * q * q / n)
    prop = (np.conj(d) * h[None, :]) @ d
    return np.stack([prop.real, prop.imag, d.real, d.imag]).astype(np.float32)


def tables_kernel(scales, base, out, *, n, slices):
    s = pl.program_id(0)
    which = jnp.where(s < slices, 0, 2)
    re = base[which]
    im = base[which + 1]
    for side, sign in ((0, 1.0), (1, -1.0)):
        scale = scales[side, s]
        a = (re * scale).astype(BF)
        b = im * (scale * sign)
        out[0, side, 0:n, 0:n] = a
        out[0, side, n:2 * n, n:2 * n] = a
        out[0, side, 0:n, n:2 * n] = (-b).astype(BF)
        out[0, side, n:2 * n, 0:n] = b.astype(BF)


def make_tables(n, slices):
    a = 2.0 ** ((np.arange(slices) + 0.5) / slices)
    scales = np.concatenate([np.stack([a, 1.0 / a]), np.ones((2, 1))], axis=1).astype(np.float32)
    return pl.pallas_call(
        functools.partial(tables_kernel, n=n, slices=slices),
        grid=(slices + 1,),
        out_shape=jax.ShapeDtypeStruct((slices + 1, 2, 2 * n, 2 * n), BF),
        in_specs=[SMEM, pl.BlockSpec((4, n, n), lambda s: (0, 0, 0))],
        out_specs=pl.BlockSpec((1, 2, 2 * n, 2 * n), lambda s: (s, 0, 0, 0)),
    )(jnp.asarray(scales), jnp.asarray(base_tables(n)))


def chain_kernel(*refs, n, slices):
    accs = [pltpu.ACC(c)((size, n), F32)
            for size in (FIRST, SECOND) for _ in range(2) for c in range(2) for _ in range(n // size)]
    pl.run_scoped(lambda *scoped: chain_body(*refs, *scoped, n=n, slices=slices), *accs)


def chain_body(plan, wave, wanted, *refs, n, slices):
    ins, tabs_hbm, near_out, far_out = refs[0:4], refs[4], refs[5:9], refs[9:13]
    (patch, tabs, inc, lhs0, lhs1, mid0, mid1, outv, target, term, psem, tsem, osem, gsem) = refs[13:27]
    accs = list(refs[27:])
    first_acc = [[[accs.pop(0) for _ in range(n // FIRST)] for _ in range(2)] for _ in range(2)]
    second_acc = [[[accs.pop(0) for _ in range(n // SECOND)] for _ in range(2)] for _ in range(2)]
    lhs, mid = (lhs0, lhs1), (mid0, mid1)
    half = n // 2

    def table_copy(s):
        return pltpu.make_async_copy(tabs_hbm.at[s], tabs.at[s], tsem.at[s])

    def patch_wait(s):
        pltpu.make_async_copy(ins[0].at[0], patch.at[s], psem.at[s]).wait()

    def span(i, size):
        return pl.ds(i * size, size)

    def issue(m, accs, size, weights, rows_of, tasks=()):
        for c in range(2):
            for k in range(2):
                pltpu.matmul_push_rhs(weights(c, k), k, c)
        pieces = 2 * (n // size)
        todo = list(tasks)
        for j in range(pieces):
            k, i = divmod(j, n // size)
            for c in range(2):
                pltpu.matmul_acc_lhs(accs[m][c][i], rows_of(c, k, i), load_staged_rhs=k if i == 0 else None)
            left = max(1, pieces - 1 - max(j, LAG))
            take = 0 if j < LAG else -(-len(todo) // left)
            for task in todo[:take]:
                task()
            del todo[:take]
        for task in todo:
            task()

    def first(m, s, side, tasks=()):
        issue(m, first_acc, FIRST, lambda c, k: lhs[m][k * n:(k + 1) * n],
              lambda c, k, i: tabs[s, side, pl.ds(c * n + i * FIRST, FIRST), k * n:(k + 1) * n], tasks)

    def turn(m):
        def one(i, c):
            mid[m][span(i, FIRST), c * n:(c + 1) * n] = pltpu.matmul_pop(first_acc[m][c][i]).astype(BF)
        return [functools.partial(one, i, c) for i in range(n // FIRST) for c in range(2)]

    def second(m, s, side, tasks=()):
        issue(m, second_acc, SECOND, lambda c, k: tabs[s, side, k * n:(k + 1) * n, c * n:(c + 1) * n],
              lambda c, k, i: mid[m][span(i, SECOND), k * n:(k + 1) * n], tasks)

    def pop(m, i):
        return pltpu.matmul_pop(second_acc[m][0][i]), pltpu.matmul_pop(second_acc[m][1][i])

    def put(m, i, re, im):
        lhs[m][pl.ds(i * SECOND, SECOND)] = re.astype(BF)
        lhs[m][pl.ds(n + i * SECOND, SECOND)] = im.astype(BF)

    def enter(s, m, i, wr, wi):
        inc[s, m, 0, span(i, SECOND)] = wr.astype(BF)
        inc[s, m, 1, span(i, SECOND)] = wi.astype(BF)
        pr = patch[s, 0, span(i, SECOND)].astype(F32)
        pi = patch[s, 1, span(i, SECOND)].astype(F32)
        put(m, i, pr * wr - pi * wi, pr * wi + pi * wr)

    def leave(s, m, i, gr, gi):
        pr = patch[s, 0, span(i, SECOND)].astype(F32)
        pi = patch[s, 1, span(i, SECOND)].astype(F32)
        put(m, i, pr * gr + pi * gi, pr * gi - pi * gr)
        wr = inc[s, m, 0, span(i, SECOND)].astype(F32)
        wi = inc[s, m, 1, span(i, SECOND)].astype(F32)
        tr = wr * gr + wi * gi
        ti = wr * gi - wi * gr
        if m == 0:
            term[0, span(i, SECOND)] = tr
            term[1, span(i, SECOND)] = ti
        else:
            outv[s, 0, span(i, SECOND)] = (term[0, span(i, SECOND)] + tr).astype(BF)
            outv[s, 1, span(i, SECOND)] = (term[1, span(i, SECOND)] + ti).astype(BF)

    count = n // SECOND

    def uses(m, use):
        return [functools.partial(lambda i: use(m, i, *pop(m, i)), i) for i in range(count)]

    def run(tasks):
        for task in tasks:
            task()

    def step(s, side, use, after=None):
        second(0, s, side, turn(1))
        second(1, s, side, uses(0, use))
        if after is None:
            run(uses(1, use))
        else:
            first(0, *after, uses(1, use))
            first(1, *after, turn(0))

    @pl.when(plan[HANDLER] == 1)
    def _():
        target_copy = pltpu.make_async_copy(wanted, target, gsem)
        target_copy.start()
        for s in range(slices):
            table_copy(s).start()
            for r in range(4):
                @pl.when(plan[REL + s] == r)
                def _():
                    pltpu.make_async_copy(ins[r].at[plan[ENTRY + s]], patch.at[s], psem.at[s]).start()
        table_copy(slices).start()
        patch_wait(0)
        table_copy(0).wait()
        for m in range(2):
            for i in range(count):
                enter(0, m, i, wave[m, 0, span(i, SECOND)].astype(F32), wave[m, 1, span(i, SECOND)].astype(F32))
            first(m, 0, 0)
        run(turn(0))

        def forward(s, carry):
            table_copy(s + 1).wait()
            patch_wait(s + 1)
            step(s, 1, lambda m, i, re, im: enter(s + 1, m, i, re, im), (s + 1, 0))
            return carry

        lax.fori_loop(0, slices - 1, forward, 0)
        table_copy(slices).wait()
        step(slices - 1, 1, put, (slices, 0))
        target_copy.wait()
        second(0, slices, 1, turn(1))
        second(1, slices, 1)
        for i in range(count):
            ar, ai = pop(0, i)
            br, bi = pop(1, i)
            resid = (ar * ar + ai * ai) + (br * br + bi * bi) - target[span(i, SECOND)]
            put(0, i, resid * ar, resid * ai)
            put(1, i, resid * br, resid * bi)
        first(0, slices, 1)
        first(1, slices, 1, turn(0))
        step(slices, 0, put, (slices - 1, 1))

        def send(s):
            for r in range(4):
                @pl.when(plan[REL + s] == r)
                def _():
                    for h, group in enumerate((near_out, far_out)):
                        pltpu.make_async_copy(outv.at[s, :, pl.ds(h * half, half)], group[r].at[plan[ENTRY + s]], osem.at[h, s]).start()

        def backward(back, carry):
            s = slices - 1 - back
            step(s, 0, lambda m, i, re, im: leave(s, m, i, re, im), (s - 1, 1))
            send(s)
            return carry

        lax.fori_loop(0, slices - 1, backward, 0)
        step(0, 0, lambda m, i, re, im: leave(0, m, i, re, im))
        send(0)
        for s in range(slices):
            for h in range(2):
                pltpu.make_async_copy(outv.at[s, :, pl.ds(h * half, half)], near_out[0].at[0], osem.at[h, s]).wait()


def chain(plan, wave, wanted, messages, tables):
    n = wave.shape[-1]
    slices = tables.shape[0] - 1
    piece = jax.ShapeDtypeStruct((slices // 4, 2, n // 2, n), BF)
    return pl.pallas_call(
        functools.partial(chain_kernel, n=n, slices=slices),
        out_shape=(piece,) * 8,
        in_specs=[SMEM, VMEM] + [ANY] * 6,
        out_specs=(ANY,) * 8,
        scratch_shapes=[
            pltpu.VMEM((slices, 2, n, n), BF),
            pltpu.VMEM((slices + 1, 2, 2 * n, 2 * n), BF),
            pltpu.VMEM((slices, 2, 2, n, n), BF),
            pltpu.VMEM((2 * n, n), BF),
            pltpu.VMEM((2 * n, n), BF),
            pltpu.VMEM((n, 2 * n), BF),
            pltpu.VMEM((n, 2 * n), BF),
            pltpu.VMEM((slices, 2, n, n), BF),
            pltpu.VMEM((n, n), F32),
            pltpu.VMEM((2, n, n), F32),
            pltpu.SemaphoreType.DMA((slices,)),
            pltpu.SemaphoreType.DMA((slices + 1,)),
            pltpu.SemaphoreType.DMA((2, slices)),
            pltpu.SemaphoreType.DMA,
        ],
        compiler_params=pltpu.CompilerParams(vmem_limit_bytes=58 << 20),
    )(plan, wave, wanted, *messages, tables)


def window(ref, lead, offset, n):
    width = ref.shape[-1]
    start = pl.multiple_of((offset // n) * n, n)
    after = pl.multiple_of(jnp.minimum(start + n, width - n), n)
    lane = lax.broadcasted_iota(jnp.int32, (ref.shape[-2], n), 1)
    first = ref[lead, :, pl.ds(start, n)].astype(F32)
    second = ref[lead, :, pl.ds(after, n)].astype(F32)
    return jnp.where(lane >= offset % n, first, second)


def own_windows_kernel(places, tile, wins, *, n):
    for p in range(places.shape[0]):
        for c in range(2):
            wins[p, c] = window(tile, c, places[p, 1], n).astype(BF)


def own_windows(places, tile, n):
    return pl.pallas_call(
        functools.partial(own_windows_kernel, n=n),
        out_shape=jax.ShapeDtypeStruct((places.shape[0], 2, tile.shape[1], n), BF),
        in_specs=[SMEM, VMEM],
        out_specs=VMEM,
        compiler_params=pltpu.CompilerParams(vmem_limit_bytes=40 << 20),
    )(places, tile)


def roll_kernel(plan, places, probe, out, *, rows, n):
    row_shift = lax.rem(places[plan[POSITION], 0], rows)
    col_shift = lax.rem(places[plan[POSITION], 1], n)
    for m in range(probe.shape[0]):
        for c in range(2):
            x = pltpu.roll(probe[m, c], row_shift, 0)
            out[m, c] = pltpu.roll(x, col_shift, 1).astype(BF)


def roll_probe(plan, places, probe, rows):
    return pl.pallas_call(
        functools.partial(roll_kernel, rows=rows, n=probe.shape[-1]),
        out_shape=jax.ShapeDtypeStruct(probe.shape, BF),
        in_specs=[SMEM, SMEM, VMEM],
        out_specs=VMEM,
        compiler_params=pltpu.CompilerParams(vmem_limit_bytes=40 << 20),
    )(plan, places, probe)


def merge_kernel(plan, places, behind, tile, ahead, *outs, n):
    rows = tile.shape[1]
    row = lax.broadcasted_iota(jnp.int32, (rows, n), 0)
    for k in range(4):
        p = plan[ORDER + k]
        for c in range(2):
            far = window(ahead, c, places[p, 1], n)
            near = behind[p, c].astype(F32)
            outs[k][c, 0:rows] = jnp.where(row >= places[p, 0] % rows, near, far).astype(BF)
            outs[k][c, rows:2 * rows] = window(tile, c, places[p, 1], n).astype(BF)


def merge(plan, places, behind, tile, ahead, n):
    return pl.pallas_call(
        functools.partial(merge_kernel, n=n),
        out_shape=(jax.ShapeDtypeStruct((2, 2 * tile.shape[1], n), BF),) * 4,
        in_specs=[SMEM, SMEM, VMEM, VMEM, VMEM],
        out_specs=(VMEM,) * 4,
        compiler_params=pltpu.CompilerParams(vmem_limit_bytes=40 << 20),
    )(plan, places, behind, tile, ahead)


def add_window(out, places, p, c, term, n):
    width = out.shape[-1]
    offset = places[p, 1]
    start = pl.multiple_of((offset // n) * n, n)
    after = pl.multiple_of(jnp.minimum(start + n, width - n), n)
    here = lax.broadcasted_iota(jnp.int32, term.shape, 1) >= offset % n
    out[c, :, pl.ds(start, n)] += jnp.where(here, term, 0.0)
    out[c, :, pl.ds(after, n)] += jnp.where(here, 0.0, term)


def halo_terms_kernel(plan, own_places, far_places, from_own, from_far, out, *, n):
    rows = out.shape[1]
    row = lax.broadcasted_iota(jnp.int32, (rows, n), 0)
    out[...] = jnp.zeros_like(out)
    for k in range(4):
        p = plan[OTHER + k]
        for c in range(2):
            term = jnp.where(row >= own_places[p, 0] % rows, from_own[k, c].astype(F32), 0.0)
            add_window(out, own_places, p, c, term, n)
            term = jnp.where(row < far_places[p, 0] % rows, from_far[k, c].astype(F32), 0.0)
            add_window(out, far_places, p, c, term, n)


def halo_terms(plan, own_places, far_places, from_own, from_far, width):
    _, _, rows, n = from_own.shape
    return pl.pallas_call(
        functools.partial(halo_terms_kernel, n=n),
        out_shape=jax.ShapeDtypeStruct((2, rows, width), F32),
        in_specs=[SMEM] * 3 + [VMEM] * 2,
        out_specs=VMEM,
        compiler_params=pltpu.CompilerParams(vmem_limit_bytes=40 << 20),
    )(plan, own_places, far_places, from_own, from_far)


def own_terms_kernel(plan, places, total, m0, m1, m2, m3, out_hbm, out, sems, *, n):
    out[...] = total[...]
    for c in range(2):
        for k, ref in enumerate((m0, m1, m2, m3)):
            add_window(out, places, plan[ORDER + k], c, ref[c].astype(F32), n)
        pltpu.make_async_copy(out.at[c], out_hbm.at[c], sems.at[c]).start()
    for c in range(2):
        pltpu.make_async_copy(out.at[c], out_hbm.at[c], sems.at[c]).wait()


def own_terms(plan, places, total, mids):
    return pl.pallas_call(
        functools.partial(own_terms_kernel, n=mids[0].shape[-1]),
        out_shape=jax.ShapeDtypeStruct(total.shape, F32),
        in_specs=[SMEM] * 2 + [VMEM] * 5,
        out_specs=ANY,
        scratch_shapes=[pltpu.VMEM(total.shape, F32), pltpu.SemaphoreType.DMA((2,))],
        compiler_params=pltpu.CompilerParams(vmem_limit_bytes=40 << 20),
    )(plan, places, total, *mids)


def shifted(block, distance):
    size = lax.axis_size("lat")
    return lax.ppermute(block, "lat", [(i, (i + distance) % size) for i in range(size)])


HANDLER, POSITION, SOURCE, ORDER, OTHER, REL, ENTRY = 0, 1, 2, 3, 7, 11, 27
GOAL = (((0, 0), (1, 1), (2, 0), (3, 1)), ((1, 2), (0, 3), (3, 2), (2, 3)))


def meet(c, team, j):
    goal, inner = GOAL[c][j]
    flip = inner ^ 2
    if c == 0:
        return inner if (team - goal) % 4 in (0, 1) else flip
    return inner if (team - goal) % 4 in (0, 3) else flip


def place_of(c, d):
    v = (d + 2 * c) % 16
    return v // 4, v % 4


def position_at(c, team, inner):
    found = [j for j in range(4) if meet(c, team, j) == inner]
    assert len(found) == 1
    return found[0]


def device_of(c, team, inner):
    return (4 * team + inner - 2 * c) % 16


@functools.lru_cache
def make_plan():
    out = np.zeros((2, 16, 48), np.int32)
    for c in range(2):
        for d in range(16):
            team, inner = place_of(c, d)
            j = position_at(c, team, inner)
            row = out[c, d]
            row[HANDLER] = GOAL[c][j] == (team, inner)
            row[POSITION] = j
            row[SOURCE] = (team - GOAL[c][j][0]) % 4
            other = place_of(1 - c, d)
            for k in range(4):
                row[ORDER + k] = position_at(c, team, inner ^ k)
                row[OTHER + k] = position_at(1 - c, other[0], other[1] ^ k)
            for s in range(16):
                there, at = place_of(c, s)
                row[REL + s] = (there - team) % 4
                row[ENTRY + s] = at ^ meet(c, there, j)
    return out


def permute(block, route):
    depth, lat = lax.axis_size("depth"), lax.axis_size("lat")
    pairs = []
    for d in range(depth):
        for m in range(lat):
            to = route(m % 2, *place_of(m % 2, d))
            if to is not None:
                pairs.append((d * lat + m, device_of(m % 2, *to) * lat + m))
    return lax.ppermute(block, ("depth", "lat"), pairs)


def within(block, k):
    return permute(block, lambda c, team, inner: (team, inner ^ k))


def towards(block, k):
    def route(c, team, inner):
        goal = GOAL[c][position_at(c, team, inner)]
        return goal if (team - goal[0]) % 4 == k else None
    return permute(block, route)


def away(block, k):
    def route(c, team, inner):
        j = position_at(c, team, inner)
        there = (team + k) % 4
        return (there, meet(c, there, j)) if GOAL[c][j] == (team, inner) else None
    return permute(block, route)


def on_device(object_slices, probe, positions, measured):
    n = probe.shape[-1]
    rows, width = object_slices.shape[2:]
    depth_size = lax.axis_size("depth")
    d = lax.axis_index("depth")
    m = lax.axis_index("lat")
    plan = lax.dynamic_slice(jnp.asarray(make_plan()), (m % 2, d, 0), (1, 1, 48)).reshape(48)
    tile = object_slices[0]

    tile_bf = tile.astype(BF)
    ahead = shifted(tile_bf, -1)
    mine = own_windows(positions, tile_bf, n)
    behind = shifted(mine, 1)
    mid_places = shifted(positions, 1)
    far_places = shifted(positions, 2)
    mid_places, far_places, ahead, behind = lax.optimization_barrier((mid_places, far_places, ahead, behind))
    parts = merge(plan, mid_places, behind, tile_bf, ahead, n)

    measured, parts = lax.optimization_barrier((measured, parts))
    target = shifted(lax.dynamic_index_in_dim(measured, plan[OTHER], 0, False), 1)

    message = jnp.stack([parts[0]] + [within(parts[k], k) for k in (1, 2, 3)])
    messages = [message] + [towards(message, k) for k in (1, 2, 3)]
    tables = make_tables(n, depth_size)
    wave = roll_probe(plan, mid_places, probe, rows)
    terms = tuple(chain(plan, wave, target, messages, tables))

    def home(pieces):
        block = pieces[0]
        for k in (1, 2, 3):
            block = jnp.where(plan[SOURCE] == k, away(pieces[k], k), block)
        return block

    near_block = home(terms[:4])
    near_got = [within(near_block[k], k) for k in (1, 2, 3)]
    late, near_got[2] = lax.optimization_barrier((terms[7], near_got[2]))
    far_block = home(terms[4:7] + (late,))
    mixed = jnp.stack([near_block[0]] + near_got)
    mids = [far_block[0]] + [within(far_block[k], k) for k in (1, 2, 3)]
    from_own = shifted(mixed, -1)
    from_far = shifted(mixed, 1)
    total = halo_terms(plan, positions, far_places, from_own, from_far, width)
    return own_terms(plan, mid_places, total, mids)[None]


def solution(mesh):
    return jax.shard_map(
        on_device,
        mesh=mesh,
        in_specs=(P("depth", None, "lat", None), P(), P("lat", None), P("lat", None, None)),
        out_specs=P("depth", None, "lat", None),
        check_vma=False,
    )
```

```python
import functools

import jax
import jax.numpy as jnp
import numpy as np
from jax import lax
from jax.experimental import pallas as pl
from jax.experimental.pallas import tpu as pltpu
from jax.sharding import PartitionSpec as P

BF = jnp.bfloat16
F32 = jnp.float32
ANY = pl.BlockSpec(memory_space=pl.ANY)
SMEM = pl.BlockSpec(memory_space=pltpu.MemorySpace.SMEM)
FIRST = 64
SECOND = 32
LAG = 2
VMEM = pl.BlockSpec(memory_space=pltpu.MemorySpace.VMEM)


@functools.lru_cache
def base_tables(n):
    k = np.arange(n)
    d = np.exp(-2j * np.pi * ((k[:, None] * k[None, :]) % n) / n) / np.sqrt(n)
    q = np.where(k < n // 2, k, k - n).astype(np.float64)
    h = np.exp(-1j * np.pi * 0.5 * q * q / n)
    prop = (np.conj(d) * h[None, :]) @ d
    return np.stack([prop.real, prop.imag, d.real, d.imag]).astype(np.float32)


def tables_kernel(scales, base, out, *, n, slices):
    s = pl.program_id(0)
    which = jnp.where(s < slices, 0, 2)
    re = base[which]
    im = base[which + 1]
    for side, sign in ((0, 1.0), (1, -1.0)):
        scale = scales[side, s]
        a = (re * scale).astype(BF)
        b = im * (scale * sign)
        out[0, side, 0:n, 0:n] = a
        out[0, side, n:2 * n, n:2 * n] = a
        out[0, side, 0:n, n:2 * n] = (-b).astype(BF)
        out[0, side, n:2 * n, 0:n] = b.astype(BF)


def make_tables(n, slices):
    a = 2.0 ** ((np.arange(slices) + 0.5) / slices)
    scales = np.concatenate([np.stack([a, 1.0 / a]), np.ones((2, 1))], axis=1).astype(np.float32)
    return pl.pallas_call(
        functools.partial(tables_kernel, n=n, slices=slices),
        grid=(slices + 1,),
        out_shape=jax.ShapeDtypeStruct((slices + 1, 2, 2 * n, 2 * n), BF),
        in_specs=[SMEM, pl.BlockSpec((4, n, n), lambda s: (0, 0, 0))],
        out_specs=pl.BlockSpec((1, 2, 2 * n, 2 * n), lambda s: (s, 0, 0, 0)),
    )(jnp.asarray(scales), jnp.asarray(base_tables(n)))


def chain_kernel(*refs, n, slices):
    accs = [pltpu.ACC(c)((size, n), F32)
            for size in (FIRST, SECOND) for _ in range(2) for c in range(2) for _ in range(n // size)]
    pl.run_scoped(lambda *scoped: chain_body(*refs, *scoped, n=n, slices=slices), *accs)


def chain_body(plan, wave, wanted, *refs, n, slices):
    ins, tabs_hbm, near_out, far_out = refs[0:4], refs[4], refs[5:9], refs[9:13]
    (patch, tabs, inc, lhs0, lhs1, mid0, mid1, outv, target, term, psem, tsem, osem, gsem) = refs[13:27]
    accs = list(refs[27:])
    first_acc = [[[accs.pop(0) for _ in range(n // FIRST)] for _ in range(2)] for _ in range(2)]
    second_acc = [[[accs.pop(0) for _ in range(n // SECOND)] for _ in range(2)] for _ in range(2)]
    lhs, mid = (lhs0, lhs1), (mid0, mid1)
    half = n // 2

    def table_copy(s):
        return pltpu.make_async_copy(tabs_hbm.at[s], tabs.at[s], tsem.at[s])

    def patch_wait(s):
        pltpu.make_async_copy(ins[0].at[0], patch.at[s], psem.at[s]).wait()

    def span(i, size):
        return pl.ds(i * size, size)

    def issue(m, accs, size, weights, rows_of, tasks=()):
        for c in range(2):
            for k in range(2):
                pltpu.matmul_push_rhs(weights(c, k), k, c)
        pieces = 2 * (n // size)
        todo = list(tasks)
        for j in range(pieces):
            k, i = divmod(j, n // size)
            for c in range(2):
                pltpu.matmul_acc_lhs(accs[m][c][i], rows_of(c, k, i), load_staged_rhs=k if i == 0 else None)
            left = max(1, pieces - 1 - max(j, LAG))
            take = 0 if j < LAG else -(-len(todo) // left)
            for task in todo[:take]:
                task()
            del todo[:take]
        for task in todo:
            task()

    def first(m, s, side, tasks=()):
        issue(m, first_acc, FIRST, lambda c, k: lhs[m][k * n:(k + 1) * n],
              lambda c, k, i: tabs[s, side, pl.ds(c * n + i * FIRST, FIRST), k * n:(k + 1) * n], tasks)

    def turn(m):
        def one(i, c):
            mid[m][span(i, FIRST), c * n:(c + 1) * n] = pltpu.matmul_pop(first_acc[m][c][i]).astype(BF)
        return [functools.partial(one, i, c) for i in range(n // FIRST) for c in range(2)]

    def second(m, s, side, tasks=()):
        issue(m, second_acc, SECOND, lambda c, k: tabs[s, side, k * n:(k + 1) * n, c * n:(c + 1) * n],
              lambda c, k, i: mid[m][span(i, SECOND), k * n:(k + 1) * n], tasks)

    def pop(m, i):
        return pltpu.matmul_pop(second_acc[m][0][i]), pltpu.matmul_pop(second_acc[m][1][i])

    def put(m, i, re, im):
        lhs[m][pl.ds(i * SECOND, SECOND)] = re.astype(BF)
        lhs[m][pl.ds(n + i * SECOND, SECOND)] = im.astype(BF)

    def enter(s, m, i, wr, wi):
        inc[s, m, 0, span(i, SECOND)] = wr.astype(BF)
        inc[s, m, 1, span(i, SECOND)] = wi.astype(BF)
        pr = patch[s, 0, span(i, SECOND)].astype(F32)
        pi = patch[s, 1, span(i, SECOND)].astype(F32)
        put(m, i, pr * wr - pi * wi, pr * wi + pi * wr)

    def leave(s, m, i, gr, gi):
        pr = patch[s, 0, span(i, SECOND)].astype(F32)
        pi = patch[s, 1, span(i, SECOND)].astype(F32)
        put(m, i, pr * gr + pi * gi, pr * gi - pi * gr)
        wr = inc[s, m, 0, span(i, SECOND)].astype(F32)
        wi = inc[s, m, 1, span(i, SECOND)].astype(F32)
        tr = wr * gr + wi * gi
        ti = wr * gi - wi * gr
        if m == 0:
            term[0, span(i, SECOND)] = tr
            term[1, span(i, SECOND)] = ti
        else:
            outv[s, 0, span(i, SECOND)] = (term[0, span(i, SECOND)] + tr).astype(BF)
            outv[s, 1, span(i, SECOND)] = (term[1, span(i, SECOND)] + ti).astype(BF)

    count = n // SECOND

    def uses(m, use):
        return [functools.partial(lambda i: use(m, i, *pop(m, i)), i) for i in range(count)]

    def run(tasks):
        for task in tasks:
            task()

    def step(s, side, use, after=None):
        second(0, s, side, turn(1))
        second(1, s, side, uses(0, use))
        if after is None:
            run(uses(1, use))
        else:
            first(0, *after, uses(1, use))
            first(1, *after, turn(0))

    @pl.when(plan[HANDLER] == 1)
    def _():
        target_copy = pltpu.make_async_copy(wanted, target, gsem)
        target_copy.start()
        for s in range(slices):
            table_copy(s).start()
            for r in range(4):
                @pl.when(plan[REL + s] == r)
                def _():
                    pltpu.make_async_copy(ins[r].at[plan[ENTRY + s]], patch.at[s], psem.at[s]).start()
        table_copy(slices).start()
        patch_wait(0)
        table_copy(0).wait()
        for m in range(2):
            for i in range(count):
                enter(0, m, i, wave[m, 0, span(i, SECOND)].astype(F32), wave[m, 1, span(i, SECOND)].astype(F32))
            first(m, 0, 0)
        run(turn(0))

        def forward(s, carry):
            table_copy(s + 1).wait()
            patch_wait(s + 1)
            step(s, 1, lambda m, i, re, im: enter(s + 1, m, i, re, im), (s + 1, 0))
            return carry

        lax.fori_loop(0, slices - 1, forward, 0)
        table_copy(slices).wait()
        step(slices - 1, 1, put, (slices, 0))
        target_copy.wait()
        second(0, slices, 1, turn(1))
        second(1, slices, 1)
        for i in range(count):
            ar, ai = pop(0, i)
            br, bi = pop(1, i)
            resid = (ar * ar + ai * ai) + (br * br + bi * bi) - target[span(i, SECOND)]
            put(0, i, resid * ar, resid * ai)
            put(1, i, resid * br, resid * bi)
        first(0, slices, 1)
        first(1, slices, 1, turn(0))
        step(slices, 0, put, (slices - 1, 1))

        def send(s):
            for r in range(4):
                @pl.when(plan[REL + s] == r)
                def _():
                    for h, group in enumerate((near_out, far_out)):
                        pltpu.make_async_copy(outv.at[s, :, pl.ds(h * half, half)], group[r].at[plan[ENTRY + s]], osem.at[h, s]).start()

        def backward(back, carry):
            s = slices - 1 - back
            step(s, 0, lambda m, i, re, im: leave(s, m, i, re, im), (s - 1, 1))
            send(s)
            return carry

        lax.fori_loop(0, slices - 1, backward, 0)
        step(0, 0, lambda m, i, re, im: leave(0, m, i, re, im))
        send(0)
        for s in range(slices):
            for h in range(2):
                pltpu.make_async_copy(outv.at[s, :, pl.ds(h * half, half)], near_out[0].at[0], osem.at[h, s]).wait()


def chain(plan, wave, wanted, messages, tables):
    n = wave.shape[-1]
    slices = tables.shape[0] - 1
    piece = jax.ShapeDtypeStruct((slices // 4, 2, n // 2, n), BF)
    return pl.pallas_call(
        functools.partial(chain_kernel, n=n, slices=slices),
        out_shape=(piece,) * 8,
        in_specs=[SMEM, VMEM] + [ANY] * 6,
        out_specs=(ANY,) * 8,
        scratch_shapes=[
            pltpu.VMEM((slices, 2, n, n), BF),
            pltpu.VMEM((slices + 1, 2, 2 * n, 2 * n), BF),
            pltpu.VMEM((slices, 2, 2, n, n), BF),
            pltpu.VMEM((2 * n, n), BF),
            pltpu.VMEM((2 * n, n), BF),
            pltpu.VMEM((n, 2 * n), BF),
            pltpu.VMEM((n, 2 * n), BF),
            pltpu.VMEM((slices, 2, n, n), BF),
            pltpu.VMEM((n, n), F32),
            pltpu.VMEM((2, n, n), F32),
            pltpu.SemaphoreType.DMA((slices,)),
            pltpu.SemaphoreType.DMA((slices + 1,)),
            pltpu.SemaphoreType.DMA((2, slices)),
            pltpu.SemaphoreType.DMA,
        ],
        compiler_params=pltpu.CompilerParams(vmem_limit_bytes=58 << 20),
    )(plan, wave, wanted, *messages, tables)


def window(ref, lead, offset, n):
    width = ref.shape[-1]
    start = pl.multiple_of((offset // n) * n, n)
    after = pl.multiple_of(jnp.minimum(start + n, width - n), n)
    lane = lax.broadcasted_iota(jnp.int32, (ref.shape[-2], n), 1)
    first = ref[lead, :, pl.ds(start, n)].astype(F32)
    second = ref[lead, :, pl.ds(after, n)].astype(F32)
    return jnp.where(lane >= offset % n, first, second)


def own_windows_kernel(places, tile, wins, *, n):
    for p in range(places.shape[0]):
        for c in range(2):
            wins[p, c] = window(tile, c, places[p, 1], n).astype(BF)


def own_windows(places, tile, n):
    return pl.pallas_call(
        functools.partial(own_windows_kernel, n=n),
        out_shape=jax.ShapeDtypeStruct((places.shape[0], 2, tile.shape[1], n), BF),
        in_specs=[SMEM, VMEM],
        out_specs=VMEM,
        compiler_params=pltpu.CompilerParams(vmem_limit_bytes=40 << 20),
    )(places, tile)


def roll_kernel(plan, places, probe, out, *, rows, n):
    row_shift = lax.rem(places[plan[POSITION], 0], rows)
    col_shift = lax.rem(places[plan[POSITION], 1], n)
    for m in range(probe.shape[0]):
        for c in range(2):
            x = pltpu.roll(probe[m, c], row_shift, 0)
            out[m, c] = pltpu.roll(x, col_shift, 1).astype(BF)


def roll_probe(plan, places, probe, rows):
    return pl.pallas_call(
        functools.partial(roll_kernel, rows=rows, n=probe.shape[-1]),
        out_shape=jax.ShapeDtypeStruct(probe.shape, BF),
        in_specs=[SMEM, SMEM, VMEM],
        out_specs=VMEM,
        compiler_params=pltpu.CompilerParams(vmem_limit_bytes=40 << 20),
    )(plan, places, probe)


def merge_kernel(plan, places, behind, tile, ahead, *outs, n):
    rows = tile.shape[1]
    row = lax.broadcasted_iota(jnp.int32, (rows, n), 0)
    for k in range(4):
        p = plan[ORDER + k]
        for c in range(2):
            far = window(ahead, c, places[p, 1], n)
            near = behind[p, c].astype(F32)
            outs[k][c, 0:rows] = jnp.where(row >= places[p, 0] % rows, near, far).astype(BF)
            outs[k][c, rows:2 * rows] = window(tile, c, places[p, 1], n).astype(BF)


def merge(plan, places, behind, tile, ahead, n):
    return pl.pallas_call(
        functools.partial(merge_kernel, n=n),
        out_shape=(jax.ShapeDtypeStruct((2, 2 * tile.shape[1], n), BF),) * 4,
        in_specs=[SMEM, SMEM, VMEM, VMEM, VMEM],
        out_specs=(VMEM,) * 4,
        compiler_params=pltpu.CompilerParams(vmem_limit_bytes=40 << 20),
    )(plan, places, behind, tile, ahead)


def add_window(out, places, p, c, term, n):
    width = out.shape[-1]
    offset = places[p, 1]
    start = pl.multiple_of((offset // n) * n, n)
    after = pl.multiple_of(jnp.minimum(start + n, width - n), n)
    here = lax.broadcasted_iota(jnp.int32, term.shape, 1) >= offset % n
    out[c, :, pl.ds(start, n)] += jnp.where(here, term, 0.0)
    out[c, :, pl.ds(after, n)] += jnp.where(here, 0.0, term)


def halo_terms_kernel(plan, own_places, far_places, from_own, from_far, out, *, n):
    rows = out.shape[1]
    row = lax.broadcasted_iota(jnp.int32, (rows, n), 0)
    out[...] = jnp.zeros_like(out)
    for k in range(4):
        p = plan[OTHER + k]
        for c in range(2):
            term = jnp.where(row >= own_places[p, 0] % rows, from_own[k, c].astype(F32), 0.0)
            add_window(out, own_places, p, c, term, n)
            term = jnp.where(row < far_places[p, 0] % rows, from_far[k, c].astype(F32), 0.0)
            add_window(out, far_places, p, c, term, n)


def halo_terms(plan, own_places, far_places, from_own, from_far, width):
    _, _, rows, n = from_own.shape
    return pl.pallas_call(
        functools.partial(halo_terms_kernel, n=n),
        out_shape=jax.ShapeDtypeStruct((2, rows, width), F32),
        in_specs=[SMEM] * 3 + [VMEM] * 2,
        out_specs=VMEM,
        compiler_params=pltpu.CompilerParams(vmem_limit_bytes=40 << 20),
    )(plan, own_places, far_places, from_own, from_far)


def own_terms_kernel(plan, places, total, m0, m1, m2, m3, out_hbm, out, sems, *, n):
    out[...] = total[...]
    for c in range(2):
        for k, ref in enumerate((m0, m1, m2, m3)):
            add_window(out, places, plan[ORDER + k], c, ref[c].astype(F32), n)
        pltpu.make_async_copy(out.at[c], out_hbm.at[c], sems.at[c]).start()
    for c in range(2):
        pltpu.make_async_copy(out.at[c], out_hbm.at[c], sems.at[c]).wait()


def own_terms(plan, places, total, mids):
    return pl.pallas_call(
        functools.partial(own_terms_kernel, n=mids[0].shape[-1]),
        out_shape=jax.ShapeDtypeStruct(total.shape, F32),
        in_specs=[SMEM] * 2 + [VMEM] * 5,
        out_specs=ANY,
        scratch_shapes=[pltpu.VMEM(total.shape, F32), pltpu.SemaphoreType.DMA((2,))],
        compiler_params=pltpu.CompilerParams(vmem_limit_bytes=40 << 20),
    )(plan, places, total, *mids)


def shifted(block, distance):
    size = lax.axis_size("lat")
    return lax.ppermute(block, "lat", [(i, (i + distance) % size) for i in range(size)])


HANDLER, POSITION, SOURCE, ORDER, OTHER, REL, ENTRY = 0, 1, 2, 3, 7, 11, 27
GOAL = (((0, 0), (1, 1), (2, 0), (3, 1)), ((1, 2), (0, 3), (3, 2), (2, 3)))


def meet(c, team, j):
    goal, inner = GOAL[c][j]
    flip = inner ^ 2
    if c == 0:
        return inner if (team - goal) % 4 in (0, 1) else flip
    return inner if (team - goal) % 4 in (0, 3) else flip


def place_of(c, d):
    v = (d + 2 * c) % 16
    return v // 4, v % 4


def position_at(c, team, inner):
    found = [j for j in range(4) if meet(c, team, j) == inner]
    assert len(found) == 1
    return found[0]


def device_of(c, team, inner):
    return (4 * team + inner - 2 * c) % 16


@functools.lru_cache
def make_plan():
    out = np.zeros((2, 16, 48), np.int32)
    for c in range(2):
        for d in range(16):
            team, inner = place_of(c, d)
            j = position_at(c, team, inner)
            row = out[c, d]
            row[HANDLER] = GOAL[c][j] == (team, inner)
            row[POSITION] = j
            row[SOURCE] = (team - GOAL[c][j][0]) % 4
            other = place_of(1 - c, d)
            for k in range(4):
                row[ORDER + k] = position_at(c, team, inner ^ k)
                row[OTHER + k] = position_at(1 - c, other[0], other[1] ^ k)
            for s in range(16):
                there, at = place_of(c, s)
                row[REL + s] = (there - team) % 4
                row[ENTRY + s] = at ^ meet(c, there, j)
    return out


def permute(block, route):
    depth, lat = lax.axis_size("depth"), lax.axis_size("lat")
    pairs = []
    for d in range(depth):
        for m in range(lat):
            to = route(m % 2, *place_of(m % 2, d))
            if to is not None:
                pairs.append((d * lat + m, device_of(m % 2, *to) * lat + m))
    return lax.ppermute(block, ("depth", "lat"), pairs)


def within(block, k):
    return permute(block, lambda c, team, inner: (team, inner ^ k))


def towards(block, k):
    def route(c, team, inner):
        goal = GOAL[c][position_at(c, team, inner)]
        return goal if (team - goal[0]) % 4 == k else None
    return permute(block, route)


def away(block, k):
    def route(c, team, inner):
        j = position_at(c, team, inner)
        there = (team + k) % 4
        return (there, meet(c, there, j)) if GOAL[c][j] == (team, inner) else None
    return permute(block, route)


def on_device(object_slices, probe, positions, measured):
    n = probe.shape[-1]
    rows, width = object_slices.shape[2:]
    depth_size = lax.axis_size("depth")
    d = lax.axis_index("depth")
    m = lax.axis_index("lat")
    plan = lax.dynamic_slice(jnp.asarray(make_plan()), (m % 2, d, 0), (1, 1, 48)).reshape(48)
    tile = object_slices[0]

    tile_bf = tile.astype(BF)
    ahead = shifted(tile_bf, -1)
    mine = own_windows(positions, tile_bf, n)
    behind = shifted(mine, 1)
    mid_places = shifted(positions, 1)
    far_places = shifted(positions, 2)
    mid_places, far_places, ahead, behind = lax.optimization_barrier((mid_places, far_places, ahead, behind))
    parts = merge(plan, mid_places, behind, tile_bf, ahead, n)

    measured, parts = lax.optimization_barrier((measured, parts))
    target = shifted(lax.dynamic_index_in_dim(measured, plan[OTHER], 0, False), 1)

    message = jnp.stack([parts[0]] + [within(parts[k], k) for k in (1, 2, 3)])
    messages = [message] + [towards(message, k) for k in (1, 2, 3)]
    tables = make_tables(n, depth_size)
    wave = roll_probe(plan, mid_places, probe, rows)
    wave, source = lax.optimization_barrier((wave, [plan[SOURCE] == k for k in (1, 2, 3)]))
    terms = tuple(chain(plan, wave, target, messages, tables))

    def home(pieces):
        block = pieces[0]
        for k in (1, 2, 3):
            block = jnp.where(source[k - 1], away(pieces[k], k), block)
        return block

    near_block = home(terms[:4])
    far_block = home(terms[4:])
    mixed = jnp.stack([near_block[0]] + [within(near_block[k], k) for k in (1, 2, 3)])
    mids = [far_block[0]] + [within(far_block[k], k) for k in (1, 2, 3)]
    from_own = shifted(mixed, -1)
    from_far = shifted(mixed, 1)
    total = halo_terms(plan, positions, far_places, from_own, from_far, width)
    return own_terms(plan, mid_places, total, mids)[None]


def solution(mesh):
    return jax.shard_map(
        on_device,
        mesh=mesh,
        in_specs=(P("depth", None, "lat", None), P(), P("lat", None), P("lat", None, None)),
        out_specs=P("depth", None, "lat", None),
        check_vma=False,
    )
```

```python
import functools

import jax
import jax.numpy as jnp
import numpy as np
from jax import lax
from jax.experimental import pallas as pl
from jax.experimental.pallas import tpu as pltpu
from jax.sharding import PartitionSpec as P

BF = jnp.bfloat16
F32 = jnp.float32
ANY = pl.BlockSpec(memory_space=pl.ANY)
SMEM = pl.BlockSpec(memory_space=pltpu.MemorySpace.SMEM)
FIRST = 64
SECOND = 32
LAG = 2
VMEM = pl.BlockSpec(memory_space=pltpu.MemorySpace.VMEM)


@functools.lru_cache
def base_tables(n):
    k = np.arange(n)
    d = np.exp(-2j * np.pi * ((k[:, None] * k[None, :]) % n) / n) / np.sqrt(n)
    q = np.where(k < n // 2, k, k - n).astype(np.float64)
    h = np.exp(-1j * np.pi * 0.5 * q * q / n)
    prop = (np.conj(d) * h[None, :]) @ d
    return np.stack([prop.real, prop.imag, d.real, d.imag]).astype(np.float32)


def tables_kernel(scales, base, out, *, n, slices):
    s = pl.program_id(0)
    which = jnp.where(s < slices, 0, 2)
    re = base[which]
    im = base[which + 1]
    for side, sign in ((0, 1.0), (1, -1.0)):
        scale = scales[side, s]
        a = (re * scale).astype(BF)
        b = im * (scale * sign)
        out[0, side, 0:n, 0:n] = a
        out[0, side, n:2 * n, n:2 * n] = a
        out[0, side, 0:n, n:2 * n] = (-b).astype(BF)
        out[0, side, n:2 * n, 0:n] = b.astype(BF)


def make_tables(n, slices):
    a = 2.0 ** ((np.arange(slices) + 0.5) / slices)
    scales = np.concatenate([np.stack([a, 1.0 / a]), np.ones((2, 1))], axis=1).astype(np.float32)
    return pl.pallas_call(
        functools.partial(tables_kernel, n=n, slices=slices),
        grid=(slices + 1,),
        out_shape=jax.ShapeDtypeStruct((slices + 1, 2, 2 * n, 2 * n), BF),
        in_specs=[SMEM, pl.BlockSpec((4, n, n), lambda s: (0, 0, 0))],
        out_specs=pl.BlockSpec((1, 2, 2 * n, 2 * n), lambda s: (s, 0, 0, 0)),
    )(jnp.asarray(scales), jnp.asarray(base_tables(n)))


def chain_kernel(*refs, n, slices):
    accs = [pltpu.ACC(c)((size, n), F32)
            for size in (FIRST, SECOND) for _ in range(2) for c in range(2) for _ in range(n // size)]
    pl.run_scoped(lambda *scoped: chain_body(*refs, *scoped, n=n, slices=slices), *accs)


def chain_body(plan, wave, wanted, *refs, n, slices):
    ins, tabs_hbm, near_out, far_out = refs[0:4], refs[4], refs[5:9], refs[9:13]
    (patch, tabs, inc, lhs0, lhs1, mid0, mid1, outv, target, term, psem, tsem, osem, gsem) = refs[13:27]
    accs = list(refs[27:])
    first_acc = [[[accs.pop(0) for _ in range(n // FIRST)] for _ in range(2)] for _ in range(2)]
    second_acc = [[[accs.pop(0) for _ in range(n // SECOND)] for _ in range(2)] for _ in range(2)]
    lhs, mid = (lhs0, lhs1), (mid0, mid1)
    half = n // 2

    def table_copy(s):
        return pltpu.make_async_copy(tabs_hbm.at[s], tabs.at[s], tsem.at[s])

    def patch_wait(s):
        pltpu.make_async_copy(ins[0].at[0], patch.at[s], psem.at[s]).wait()

    def span(i, size):
        return pl.ds(i * size, size)

    def issue(m, accs, size, weights, rows_of, tasks=()):
        for c in range(2):
            for k in range(2):
                pltpu.matmul_push_rhs(weights(c, k), k, c)
        pieces = 2 * (n // size)
        todo = list(tasks)
        for j in range(pieces):
            k, i = divmod(j, n // size)
            for c in range(2):
                pltpu.matmul_acc_lhs(accs[m][c][i], rows_of(c, k, i), load_staged_rhs=k if i == 0 else None)
            left = max(1, pieces - 1 - max(j, LAG))
            take = 0 if j < LAG else -(-len(todo) // left)
            for task in todo[:take]:
                task()
            del todo[:take]
        for task in todo:
            task()

    def first(m, s, side, tasks=()):
        issue(m, first_acc, FIRST, lambda c, k: lhs[m][k * n:(k + 1) * n],
              lambda c, k, i: tabs[s, side, pl.ds(c * n + i * FIRST, FIRST), k * n:(k + 1) * n], tasks)

    def turn(m):
        def one(i, c):
            mid[m][span(i, FIRST), c * n:(c + 1) * n] = pltpu.matmul_pop(first_acc[m][c][i]).astype(BF)
        return [functools.partial(one, i, c) for i in range(n // FIRST) for c in range(2)]

    def second(m, s, side, tasks=()):
        issue(m, second_acc, SECOND, lambda c, k: tabs[s, side, k * n:(k + 1) * n, c * n:(c + 1) * n],
              lambda c, k, i: mid[m][span(i, SECOND), k * n:(k + 1) * n], tasks)

    def pop(m, i):
        return pltpu.matmul_pop(second_acc[m][0][i]), pltpu.matmul_pop(second_acc[m][1][i])

    def put(m, i, re, im):
        lhs[m][pl.ds(i * SECOND, SECOND)] = re.astype(BF)
        lhs[m][pl.ds(n + i * SECOND, SECOND)] = im.astype(BF)

    def enter(s, m, i, wr, wi):
        inc[s, m, 0, span(i, SECOND)] = wr.astype(BF)
        inc[s, m, 1, span(i, SECOND)] = wi.astype(BF)
        pr = patch[s, 0, span(i, SECOND)].astype(F32)
        pi = patch[s, 1, span(i, SECOND)].astype(F32)
        put(m, i, pr * wr - pi * wi, pr * wi + pi * wr)

    def leave(s, m, i, gr, gi):
        pr = patch[s, 0, span(i, SECOND)].astype(F32)
        pi = patch[s, 1, span(i, SECOND)].astype(F32)
        put(m, i, pr * gr + pi * gi, pr * gi - pi * gr)
        wr = inc[s, m, 0, span(i, SECOND)].astype(F32)
        wi = inc[s, m, 1, span(i, SECOND)].astype(F32)
        tr = wr * gr + wi * gi
        ti = wr * gi - wi * gr
        if m == 0:
            term[0, span(i, SECOND)] = tr
            term[1, span(i, SECOND)] = ti
        else:
            outv[s, 0, span(i, SECOND)] = (term[0, span(i, SECOND)] + tr).astype(BF)
            outv[s, 1, span(i, SECOND)] = (term[1, span(i, SECOND)] + ti).astype(BF)

    count = n // SECOND

    def uses(m, use):
        return [functools.partial(lambda i: use(m, i, *pop(m, i)), i) for i in range(count)]

    def run(tasks):
        for task in tasks:
            task()

    def step(s, side, use, after=None):
        second(0, s, side, turn(1))
        second(1, s, side, uses(0, use))
        if after is None:
            run(uses(1, use))
        else:
            first(0, *after, uses(1, use))
            first(1, *after, turn(0))

    @pl.when(plan[HANDLER] == 1)
    def _():
        target_copy = pltpu.make_async_copy(wanted, target, gsem)
        target_copy.start()
        for s in range(slices):
            table_copy(s).start()
            for r in range(4):
                @pl.when(plan[REL + s] == r)
                def _():
                    pltpu.make_async_copy(ins[r].at[plan[ENTRY + s]], patch.at[s], psem.at[s]).start()
        table_copy(slices).start()
        patch_wait(0)
        table_copy(0).wait()
        for m in range(2):
            for i in range(count):
                enter(0, m, i, wave[m, 0, span(i, SECOND)].astype(F32), wave[m, 1, span(i, SECOND)].astype(F32))
            first(m, 0, 0)
        run(turn(0))

        def forward(s, carry):
            table_copy(s + 1).wait()
            patch_wait(s + 1)
            step(s, 1, lambda m, i, re, im: enter(s + 1, m, i, re, im), (s + 1, 0))
            return carry

        lax.fori_loop(0, slices - 1, forward, 0)
        table_copy(slices).wait()
        step(slices - 1, 1, put, (slices, 0))
        target_copy.wait()
        second(0, slices, 1, turn(1))
        second(1, slices, 1)
        for i in range(count):
            ar, ai = pop(0, i)
            br, bi = pop(1, i)
            resid = (ar * ar + ai * ai) + (br * br + bi * bi) - target[span(i, SECOND)]
            put(0, i, resid * ar, resid * ai)
            put(1, i, resid * br, resid * bi)
        first(0, slices, 1)
        first(1, slices, 1, turn(0))
        step(slices, 0, put, (slices - 1, 1))

        def send(s):
            for r in range(4):
                @pl.when(plan[REL + s] == r)
                def _():
                    for h, group in enumerate((near_out, far_out)):
                        pltpu.make_async_copy(outv.at[s, :, pl.ds(h * half, half)], group[r].at[plan[ENTRY + s]], osem.at[h, s]).start()

        def backward(back, carry):
            s = slices - 1 - back
            step(s, 0, lambda m, i, re, im: leave(s, m, i, re, im), (s - 1, 1))
            send(s)
            return carry

        lax.fori_loop(0, slices - 1, backward, 0)
        step(0, 0, lambda m, i, re, im: leave(0, m, i, re, im))
        send(0)
        for s in range(slices):
            for h in range(2):
                pltpu.make_async_copy(outv.at[s, :, pl.ds(h * half, half)], near_out[0].at[0], osem.at[h, s]).wait()


def chain(plan, wave, wanted, messages, tables):
    n = wave.shape[-1]
    slices = tables.shape[0] - 1
    piece = jax.ShapeDtypeStruct((slices // 4, 2, n // 2, n), BF)
    return pl.pallas_call(
        functools.partial(chain_kernel, n=n, slices=slices),
        out_shape=(piece,) * 8,
        in_specs=[SMEM, VMEM] + [ANY] * 6,
        out_specs=(ANY,) * 8,
        scratch_shapes=[
            pltpu.VMEM((slices, 2, n, n), BF),
            pltpu.VMEM((slices + 1, 2, 2 * n, 2 * n), BF),
            pltpu.VMEM((slices, 2, 2, n, n), BF),
            pltpu.VMEM((2 * n, n), BF),
            pltpu.VMEM((2 * n, n), BF),
            pltpu.VMEM((n, 2 * n), BF),
            pltpu.VMEM((n, 2 * n), BF),
            pltpu.VMEM((slices, 2, n, n), BF),
            pltpu.VMEM((n, n), F32),
            pltpu.VMEM((2, n, n), F32),
            pltpu.SemaphoreType.DMA((slices,)),
            pltpu.SemaphoreType.DMA((slices + 1,)),
            pltpu.SemaphoreType.DMA((2, slices)),
            pltpu.SemaphoreType.DMA,
        ],
        compiler_params=pltpu.CompilerParams(vmem_limit_bytes=58 << 20),
    )(plan, wave, wanted, *messages, tables)


def window(ref, lead, offset, n):
    width = ref.shape[-1]
    start = pl.multiple_of((offset // n) * n, n)
    after = pl.multiple_of(jnp.minimum(start + n, width - n), n)
    lane = lax.broadcasted_iota(jnp.int32, (ref.shape[-2], n), 1)
    first = ref[lead, :, pl.ds(start, n)].astype(F32)
    second = ref[lead, :, pl.ds(after, n)].astype(F32)
    return jnp.where(lane >= offset % n, first, second)


def own_windows_kernel(places, tile, wins, *, n):
    for p in range(places.shape[0]):
        for c in range(2):
            wins[p, c] = window(tile, c, places[p, 1], n).astype(BF)


def own_windows(places, tile, n):
    return pl.pallas_call(
        functools.partial(own_windows_kernel, n=n),
        out_shape=jax.ShapeDtypeStruct((places.shape[0], 2, tile.shape[1], n), BF),
        in_specs=[SMEM, VMEM],
        out_specs=VMEM,
        compiler_params=pltpu.CompilerParams(vmem_limit_bytes=40 << 20),
    )(places, tile)


def roll_kernel(plan, places, probe, out, *, rows, n):
    row_shift = lax.rem(places[plan[POSITION], 0], rows)
    col_shift = lax.rem(places[plan[POSITION], 1], n)
    for m in range(probe.shape[0]):
        for c in range(2):
            x = pltpu.roll(probe[m, c], row_shift, 0)
            out[m, c] = pltpu.roll(x, col_shift, 1).astype(BF)


def roll_probe(plan, places, probe, rows):
    return pl.pallas_call(
        functools.partial(roll_kernel, rows=rows, n=probe.shape[-1]),
        out_shape=jax.ShapeDtypeStruct(probe.shape, BF),
        in_specs=[SMEM, SMEM, VMEM],
        out_specs=VMEM,
        compiler_params=pltpu.CompilerParams(vmem_limit_bytes=40 << 20),
    )(plan, places, probe)


def merge_kernel(plan, places, behind, tile, ahead, *outs, n):
    rows = tile.shape[1]
    row = lax.broadcasted_iota(jnp.int32, (rows, n), 0)
    for k in range(4):
        p = plan[ORDER + k]
        for c in range(2):
            far = window(ahead, c, places[p, 1], n)
            near = behind[p, c].astype(F32)
            outs[k][c, 0:rows] = jnp.where(row >= places[p, 0] % rows, near, far).astype(BF)
            outs[k][c, rows:2 * rows] = window(tile, c, places[p, 1], n).astype(BF)


def merge(plan, places, behind, tile, ahead, n):
    return pl.pallas_call(
        functools.partial(merge_kernel, n=n),
        out_shape=(jax.ShapeDtypeStruct((2, 2 * tile.shape[1], n), BF),) * 4,
        in_specs=[SMEM, SMEM, VMEM, VMEM, VMEM],
        out_specs=(VMEM,) * 4,
        compiler_params=pltpu.CompilerParams(vmem_limit_bytes=40 << 20),
    )(plan, places, behind, tile, ahead)


def add_window(out, places, p, c, term, n):
    width = out.shape[-1]
    offset = places[p, 1]
    start = pl.multiple_of((offset // n) * n, n)
    after = pl.multiple_of(jnp.minimum(start + n, width - n), n)
    here = lax.broadcasted_iota(jnp.int32, term.shape, 1) >= offset % n
    out[c, :, pl.ds(start, n)] += jnp.where(here, term, 0.0)
    out[c, :, pl.ds(after, n)] += jnp.where(here, 0.0, term)


def halo_terms_kernel(plan, own_places, far_places, from_own, from_far, out, *, n):
    rows = out.shape[1]
    row = lax.broadcasted_iota(jnp.int32, (rows, n), 0)
    out[...] = jnp.zeros_like(out)
    for k in range(4):
        p = plan[OTHER + k]
        for c in range(2):
            term = jnp.where(row >= own_places[p, 0] % rows, from_own[k, c].astype(F32), 0.0)
            add_window(out, own_places, p, c, term, n)
            term = jnp.where(row < far_places[p, 0] % rows, from_far[k, c].astype(F32), 0.0)
            add_window(out, far_places, p, c, term, n)


def halo_terms(plan, own_places, far_places, from_own, from_far, width):
    _, _, rows, n = from_own.shape
    return pl.pallas_call(
        functools.partial(halo_terms_kernel, n=n),
        out_shape=jax.ShapeDtypeStruct((2, rows, width), F32),
        in_specs=[SMEM] * 3 + [VMEM] * 2,
        out_specs=VMEM,
        compiler_params=pltpu.CompilerParams(vmem_limit_bytes=40 << 20),
    )(plan, own_places, far_places, from_own, from_far)


def own_terms_kernel(plan, places, total, m0, m1, m2, m3, out_hbm, out, sems, *, n):
    out[...] = total[...]
    for c in range(2):
        for k, ref in enumerate((m0, m1, m2, m3)):
            add_window(out, places, plan[ORDER + k], c, ref[c].astype(F32), n)
        pltpu.make_async_copy(out.at[c], out_hbm.at[c], sems.at[c]).start()
    for c in range(2):
        pltpu.make_async_copy(out.at[c], out_hbm.at[c], sems.at[c]).wait()


def own_terms(plan, places, total, mids):
    return pl.pallas_call(
        functools.partial(own_terms_kernel, n=mids[0].shape[-1]),
        out_shape=jax.ShapeDtypeStruct(total.shape, F32),
        in_specs=[SMEM] * 2 + [VMEM] * 5,
        out_specs=ANY,
        scratch_shapes=[pltpu.VMEM(total.shape, F32), pltpu.SemaphoreType.DMA((2,))],
        compiler_params=pltpu.CompilerParams(vmem_limit_bytes=40 << 20),
    )(plan, places, total, *mids)


def shifted(block, distance):
    size = lax.axis_size("lat")
    return lax.ppermute(block, "lat", [(i, (i + distance) % size) for i in range(size)])


HANDLER, POSITION, SOURCE, ORDER, OTHER, REL, ENTRY = 0, 1, 2, 3, 7, 11, 27
GOAL = (((0, 0), (1, 1), (2, 0), (3, 1)), ((1, 2), (0, 3), (3, 2), (2, 3)))


def meet(c, team, j):
    goal, inner = GOAL[c][j]
    flip = inner ^ 2
    if c == 0:
        return inner if (team - goal) % 4 in (0, 1) else flip
    return inner if (team - goal) % 4 in (0, 3) else flip


def place_of(c, d):
    v = (d + 2 * c) % 16
    return v // 4, v % 4


def position_at(c, team, inner):
    found = [j for j in range(4) if meet(c, team, j) == inner]
    assert len(found) == 1
    return found[0]


def device_of(c, team, inner):
    return (4 * team + inner - 2 * c) % 16


@functools.lru_cache
def make_plan():
    out = np.zeros((2, 16, 48), np.int32)
    for c in range(2):
        for d in range(16):
            team, inner = place_of(c, d)
            j = position_at(c, team, inner)
            row = out[c, d]
            row[HANDLER] = GOAL[c][j] == (team, inner)
            row[POSITION] = j
            row[SOURCE] = (team - GOAL[c][j][0]) % 4
            other = place_of(1 - c, d)
            for k in range(4):
                row[ORDER + k] = position_at(c, team, inner ^ k)
                row[OTHER + k] = position_at(1 - c, other[0], other[1] ^ k)
            for s in range(16):
                there, at = place_of(c, s)
                row[REL + s] = (there - team) % 4
                row[ENTRY + s] = at ^ meet(c, there, j)
    return out


def permute(block, route):
    depth, lat = lax.axis_size("depth"), lax.axis_size("lat")
    pairs = []
    for d in range(depth):
        for m in range(lat):
            to = route(m % 2, *place_of(m % 2, d))
            if to is not None:
                pairs.append((d * lat + m, device_of(m % 2, *to) * lat + m))
    return lax.ppermute(block, ("depth", "lat"), pairs)


def within(block, k):
    return permute(block, lambda c, team, inner: (team, inner ^ k))


def towards(block, k):
    def route(c, team, inner):
        goal = GOAL[c][position_at(c, team, inner)]
        return goal if (team - goal[0]) % 4 == k else None
    return permute(block, route)


def away(block, k):
    def route(c, team, inner):
        j = position_at(c, team, inner)
        there = (team + k) % 4
        return (there, meet(c, there, j)) if GOAL[c][j] == (team, inner) else None
    return permute(block, route)


def on_device(object_slices, probe, positions, measured):
    n = probe.shape[-1]
    rows, width = object_slices.shape[2:]
    depth_size = lax.axis_size("depth")
    d = lax.axis_index("depth")
    m = lax.axis_index("lat")
    plan = lax.dynamic_slice(jnp.asarray(make_plan()), (m % 2, d, 0), (1, 1, 48)).reshape(48)
    tile = object_slices[0]

    tile_bf = tile.astype(BF)
    ahead = shifted(tile_bf, -1)
    mine = own_windows(positions, tile_bf, n)
    behind = shifted(mine, 1)
    mid_places = shifted(positions, 1)
    mid_places, ahead, behind = lax.optimization_barrier((mid_places, ahead, behind))
    parts = merge(plan, mid_places, behind, tile_bf, ahead, n)

    measured, late_positions, parts = lax.optimization_barrier((measured, positions, parts))
    far_places = shifted(late_positions, 2)
    target = shifted(lax.dynamic_index_in_dim(measured, plan[OTHER], 0, False), 1)

    message = jnp.stack([parts[0]] + [within(parts[k], k) for k in (1, 2, 3)])
    messages = {0: message} | {k: towards(message, k) for k in (2, 1, 3)}
    messages = [messages[k] for k in range(4)]
    tables = make_tables(n, depth_size)
    wave = roll_probe(plan, mid_places, probe, rows)
    wave, source, far_places = lax.optimization_barrier((wave, [plan[SOURCE] == k for k in (1, 2, 3)], far_places))
    terms = tuple(chain(plan, wave, target, messages, tables))

    def home(pieces):
        block = pieces[0]
        for k in (2, 1, 3):
            block = jnp.where(source[k - 1], away(pieces[k], k), block)
        return block

    near_block = home(terms[:4])
    far_block = home(terms[4:])
    mixed = jnp.stack([near_block[0]] + [within(near_block[k], k) for k in (1, 2, 3)])
    mids = [far_block[0]] + [within(far_block[k], k) for k in (1, 2, 3)]
    from_own = shifted(mixed, -1)
    from_far = shifted(mixed, 1)
    total = halo_terms(plan, positions, far_places, from_own, from_far, width)
    return own_terms(plan, mid_places, total, mids)[None]


def solution(mesh):
    return jax.shard_map(
        on_device,
        mesh=mesh,
        in_specs=(P("depth", None, "lat", None), P(), P("lat", None), P("lat", None, None)),
        out_specs=P("depth", None, "lat", None),
        check_vma=False,
    )
```

```python
import functools

import jax
import jax.numpy as jnp
import numpy as np
from jax import lax
from jax.experimental import pallas as pl
from jax.experimental.pallas import tpu as pltpu
from jax.sharding import PartitionSpec as P

BF = jnp.bfloat16
F32 = jnp.float32
ANY = pl.BlockSpec(memory_space=pl.ANY)
SMEM = pl.BlockSpec(memory_space=pltpu.MemorySpace.SMEM)
FIRST = 64
SECOND = 32
LAG = 2
VMEM = pl.BlockSpec(memory_space=pltpu.MemorySpace.VMEM)


@functools.lru_cache
def base_tables(n):
    k = np.arange(n)
    d = np.exp(-2j * np.pi * ((k[:, None] * k[None, :]) % n) / n) / np.sqrt(n)
    q = np.where(k < n // 2, k, k - n).astype(np.float64)
    h = np.exp(-1j * np.pi * 0.5 * q * q / n)
    prop = (np.conj(d) * h[None, :]) @ d
    return np.stack([prop.real, prop.imag, d.real, d.imag]).astype(np.float32)


def tables_kernel(scales, base, out, *, n, slices):
    s = pl.program_id(0)
    which = jnp.where(s < slices, 0, 2)
    re = base[which]
    im = base[which + 1]
    for side, sign in ((0, 1.0), (1, -1.0)):
        scale = scales[side, s]
        a = (re * scale).astype(BF)
        b = im * (scale * sign)
        out[0, side, 0:n, 0:n] = a
        out[0, side, n:2 * n, n:2 * n] = a
        out[0, side, 0:n, n:2 * n] = (-b).astype(BF)
        out[0, side, n:2 * n, 0:n] = b.astype(BF)


def make_tables(n, slices):
    a = 2.0 ** ((np.arange(slices) + 0.5) / slices)
    scales = np.concatenate([np.stack([a, 1.0 / a]), np.ones((2, 1))], axis=1).astype(np.float32)
    return pl.pallas_call(
        functools.partial(tables_kernel, n=n, slices=slices),
        grid=(slices + 1,),
        out_shape=jax.ShapeDtypeStruct((slices + 1, 2, 2 * n, 2 * n), BF),
        in_specs=[SMEM, pl.BlockSpec((4, n, n), lambda s: (0, 0, 0))],
        out_specs=pl.BlockSpec((1, 2, 2 * n, 2 * n), lambda s: (s, 0, 0, 0)),
    )(jnp.asarray(scales), jnp.asarray(base_tables(n)))


def chain_kernel(*refs, n, slices):
    accs = [pltpu.ACC(c)((size, n), F32)
            for size in (FIRST, SECOND) for _ in range(2) for c in range(2) for _ in range(n // size)]
    pl.run_scoped(lambda *scoped: chain_body(*refs, *scoped, n=n, slices=slices), *accs)


def chain_body(plan, wave, wanted, *refs, n, slices):
    ins, tabs_hbm, near_out, far_out = refs[3::-1], refs[4], refs[5:9], refs[9:13]
    (patch, tabs, inc, lhs0, lhs1, mid0, mid1, outv, target, term, psem, tsem, osem, gsem) = refs[13:27]
    accs = list(refs[27:])
    first_acc = [[[accs.pop(0) for _ in range(n // FIRST)] for _ in range(2)] for _ in range(2)]
    second_acc = [[[accs.pop(0) for _ in range(n // SECOND)] for _ in range(2)] for _ in range(2)]
    lhs, mid = (lhs0, lhs1), (mid0, mid1)
    half = n // 2

    def table_copy(s):
        return pltpu.make_async_copy(tabs_hbm.at[s], tabs.at[s], tsem.at[s])

    def patch_wait(s):
        pltpu.make_async_copy(ins[0].at[0], patch.at[s], psem.at[s]).wait()

    def span(i, size):
        return pl.ds(i * size, size)

    def issue(m, accs, size, weights, rows_of, tasks=()):
        for c in range(2):
            for k in range(2):
                pltpu.matmul_push_rhs(weights(c, k), k, c)
        pieces = 2 * (n // size)
        todo = list(tasks)
        for j in range(pieces):
            k, i = divmod(j, n // size)
            for c in range(2):
                pltpu.matmul_acc_lhs(accs[m][c][i], rows_of(c, k, i), load_staged_rhs=k if i == 0 else None)
            left = max(1, pieces - 1 - max(j, LAG))
            take = 0 if j < LAG else -(-len(todo) // left)
            for task in todo[:take]:
                task()
            del todo[:take]
        for task in todo:
            task()

    def first(m, s, side, tasks=()):
        issue(m, first_acc, FIRST, lambda c, k: lhs[m][k * n:(k + 1) * n],
              lambda c, k, i: tabs[s, side, pl.ds(c * n + i * FIRST, FIRST), k * n:(k + 1) * n], tasks)

    def turn(m):
        def one(i, c):
            mid[m][span(i, FIRST), c * n:(c + 1) * n] = pltpu.matmul_pop(first_acc[m][c][i]).astype(BF)
        return [functools.partial(one, i, c) for i in range(n // FIRST) for c in range(2)]

    def second(m, s, side, tasks=()):
        issue(m, second_acc, SECOND, lambda c, k: tabs[s, side, k * n:(k + 1) * n, c * n:(c + 1) * n],
              lambda c, k, i: mid[m][span(i, SECOND), k * n:(k + 1) * n], tasks)

    def pop(m, i):
        return pltpu.matmul_pop(second_acc[m][0][i]), pltpu.matmul_pop(second_acc[m][1][i])

    def put(m, i, re, im):
        lhs[m][pl.ds(i * SECOND, SECOND)] = re.astype(BF)
        lhs[m][pl.ds(n + i * SECOND, SECOND)] = im.astype(BF)

    def enter(s, m, i, wr, wi):
        inc[s, m, 0, span(i, SECOND)] = wr.astype(BF)
        inc[s, m, 1, span(i, SECOND)] = wi.astype(BF)
        pr = patch[s, 0, span(i, SECOND)].astype(F32)
        pi = patch[s, 1, span(i, SECOND)].astype(F32)
        put(m, i, pr * wr - pi * wi, pr * wi + pi * wr)

    def leave(s, m, i, gr, gi):
        pr = patch[s, 0, span(i, SECOND)].astype(F32)
        pi = patch[s, 1, span(i, SECOND)].astype(F32)
        put(m, i, pr * gr + pi * gi, pr * gi - pi * gr)
        wr = inc[s, m, 0, span(i, SECOND)].astype(F32)
        wi = inc[s, m, 1, span(i, SECOND)].astype(F32)
        tr = wr * gr + wi * gi
        ti = wr * gi - wi * gr
        if m == 0:
            term[0, span(i, SECOND)] = tr
            term[1, span(i, SECOND)] = ti
        else:
            outv[s, 0, span(i, SECOND)] = (term[0, span(i, SECOND)] + tr).astype(BF)
            outv[s, 1, span(i, SECOND)] = (term[1, span(i, SECOND)] + ti).astype(BF)

    count = n // SECOND

    def uses(m, use):
        return [functools.partial(lambda i: use(m, i, *pop(m, i)), i) for i in range(count)]

    def run(tasks):
        for task in tasks:
            task()

    def step(s, side, use, after=None):
        second(0, s, side, turn(1))
        second(1, s, side, uses(0, use))
        if after is None:
            run(uses(1, use))
        else:
            first(0, *after, uses(1, use))
            first(1, *after, turn(0))

    @pl.when(plan[HANDLER] == 1)
    def _():
        target_copy = pltpu.make_async_copy(wanted, target, gsem)
        target_copy.start()
        for s in range(slices):
            table_copy(s).start()
            for r in range(4):
                @pl.when(plan[REL + s] == r)
                def _():
                    pltpu.make_async_copy(ins[r].at[plan[ENTRY + s]], patch.at[s], psem.at[s]).start()
        table_copy(slices).start()
        patch_wait(0)
        table_copy(0).wait()
        for m in range(2):
            for i in range(count):
                enter(0, m, i, wave[m, 0, span(i, SECOND)].astype(F32), wave[m, 1, span(i, SECOND)].astype(F32))
            first(m, 0, 0)
        run(turn(0))

        def forward(s, carry):
            table_copy(s + 1).wait()
            patch_wait(s + 1)
            step(s, 1, lambda m, i, re, im: enter(s + 1, m, i, re, im), (s + 1, 0))
            return carry

        lax.fori_loop(0, slices - 1, forward, 0)
        table_copy(slices).wait()
        step(slices - 1, 1, put, (slices, 0))
        target_copy.wait()
        second(0, slices, 1, turn(1))
        second(1, slices, 1)
        for i in range(count):
            ar, ai = pop(0, i)
            br, bi = pop(1, i)
            resid = (ar * ar + ai * ai) + (br * br + bi * bi) - target[span(i, SECOND)]
            put(0, i, resid * ar, resid * ai)
            put(1, i, resid * br, resid * bi)
        first(0, slices, 1)
        first(1, slices, 1, turn(0))
        step(slices, 0, put, (slices - 1, 1))

        def send(s):
            for r in range(4):
                @pl.when(plan[REL + s] == r)
                def _():
                    for h, group in enumerate((near_out, far_out)):
                        pltpu.make_async_copy(outv.at[s, :, pl.ds(h * half, half)], group[r].at[plan[ENTRY + s]], osem.at[h, s]).start()

        def backward(back, carry):
            s = slices - 1 - back
            step(s, 0, lambda m, i, re, im: leave(s, m, i, re, im), (s - 1, 1))
            send(s)
            return carry

        lax.fori_loop(0, slices - 1, backward, 0)
        step(0, 0, lambda m, i, re, im: leave(0, m, i, re, im))
        send(0)
        for s in range(slices):
            for h in range(2):
                pltpu.make_async_copy(outv.at[s, :, pl.ds(h * half, half)], near_out[0].at[0], osem.at[h, s]).wait()


def chain(plan, wave, wanted, messages, tables):
    n = wave.shape[-1]
    slices = tables.shape[0] - 1
    piece = jax.ShapeDtypeStruct((slices // 4, 2, n // 2, n), BF)
    return pl.pallas_call(
        functools.partial(chain_kernel, n=n, slices=slices),
        out_shape=(piece,) * 8,
        in_specs=[SMEM, VMEM] + [ANY] * 6,
        out_specs=(ANY,) * 8,
        scratch_shapes=[
            pltpu.VMEM((slices, 2, n, n), BF),
            pltpu.VMEM((slices + 1, 2, 2 * n, 2 * n), BF),
            pltpu.VMEM((slices, 2, 2, n, n), BF),
            pltpu.VMEM((2 * n, n), BF),
            pltpu.VMEM((2 * n, n), BF),
            pltpu.VMEM((n, 2 * n), BF),
            pltpu.VMEM((n, 2 * n), BF),
            pltpu.VMEM((slices, 2, n, n), BF),
            pltpu.VMEM((n, n), F32),
            pltpu.VMEM((2, n, n), F32),
            pltpu.SemaphoreType.DMA((slices,)),
            pltpu.SemaphoreType.DMA((slices + 1,)),
            pltpu.SemaphoreType.DMA((2, slices)),
            pltpu.SemaphoreType.DMA,
        ],
        compiler_params=pltpu.CompilerParams(vmem_limit_bytes=58 << 20),
    )(plan, wave, wanted, *messages[::-1], tables)


def window(ref, lead, offset, n):
    width = ref.shape[-1]
    start = pl.multiple_of((offset // n) * n, n)
    after = pl.multiple_of(jnp.minimum(start + n, width - n), n)
    lane = lax.broadcasted_iota(jnp.int32, (ref.shape[-2], n), 1)
    first = ref[lead, :, pl.ds(start, n)].astype(F32)
    second = ref[lead, :, pl.ds(after, n)].astype(F32)
    return jnp.where(lane >= offset % n, first, second)


def own_windows_kernel(places, tile, wins, *, n):
    for p in range(places.shape[0]):
        for c in range(2):
            wins[p, c] = window(tile, c, places[p, 1], n).astype(BF)


def own_windows(places, tile, n):
    return pl.pallas_call(
        functools.partial(own_windows_kernel, n=n),
        out_shape=jax.ShapeDtypeStruct((places.shape[0], 2, tile.shape[1], n), BF),
        in_specs=[SMEM, VMEM],
        out_specs=VMEM,
        compiler_params=pltpu.CompilerParams(vmem_limit_bytes=40 << 20),
    )(places, tile)


def roll_kernel(plan, places, probe, out, *, rows, n):
    row_shift = lax.rem(places[plan[POSITION], 0], rows)
    col_shift = lax.rem(places[plan[POSITION], 1], n)
    for m in range(probe.shape[0]):
        for c in range(2):
            x = pltpu.roll(probe[m, c], row_shift, 0)
            out[m, c] = pltpu.roll(x, col_shift, 1).astype(BF)


def roll_probe(plan, places, probe, rows):
    return pl.pallas_call(
        functools.partial(roll_kernel, rows=rows, n=probe.shape[-1]),
        out_shape=jax.ShapeDtypeStruct(probe.shape, BF),
        in_specs=[SMEM, SMEM, VMEM],
        out_specs=VMEM,
        compiler_params=pltpu.CompilerParams(vmem_limit_bytes=40 << 20),
    )(plan, places, probe)


def merge_kernel(plan, places, behind, tile, ahead, *outs, n):
    rows = tile.shape[1]
    row = lax.broadcasted_iota(jnp.int32, (rows, n), 0)
    for k in range(4):
        p = plan[ORDER + k]
        for c in range(2):
            far = window(ahead, c, places[p, 1], n)
            near = behind[p, c].astype(F32)
            outs[k][c, 0:rows] = jnp.where(row >= places[p, 0] % rows, near, far).astype(BF)
            outs[k][c, rows:2 * rows] = window(tile, c, places[p, 1], n).astype(BF)


def merge(plan, places, behind, tile, ahead, n):
    return pl.pallas_call(
        functools.partial(merge_kernel, n=n),
        out_shape=(jax.ShapeDtypeStruct((2, 2 * tile.shape[1], n), BF),) * 4,
        in_specs=[SMEM, SMEM, VMEM, VMEM, VMEM],
        out_specs=(VMEM,) * 4,
        compiler_params=pltpu.CompilerParams(vmem_limit_bytes=40 << 20),
    )(plan, places, behind, tile, ahead)


def add_window(out, places, p, c, term, n):
    width = out.shape[-1]
    offset = places[p, 1]
    start = pl.multiple_of((offset // n) * n, n)
    after = pl.multiple_of(jnp.minimum(start + n, width - n), n)
    here = lax.broadcasted_iota(jnp.int32, term.shape, 1) >= offset % n
    out[c, :, pl.ds(start, n)] += jnp.where(here, term, 0.0)
    out[c, :, pl.ds(after, n)] += jnp.where(here, 0.0, term)


def halo_terms_kernel(plan, own_places, far_places, from_own, from_far, out, *, n):
    rows = out.shape[1]
    row = lax.broadcasted_iota(jnp.int32, (rows, n), 0)
    out[...] = jnp.zeros_like(out)
    for k in range(4):
        p = plan[OTHER + k]
        for c in range(2):
            term = jnp.where(row >= own_places[p, 0] % rows, from_own[k, c].astype(F32), 0.0)
            add_window(out, own_places, p, c, term, n)
            term = jnp.where(row < far_places[p, 0] % rows, from_far[k, c].astype(F32), 0.0)
            add_window(out, far_places, p, c, term, n)


def halo_terms(plan, own_places, far_places, from_own, from_far, width):
    _, _, rows, n = from_own.shape
    return pl.pallas_call(
        functools.partial(halo_terms_kernel, n=n),
        out_shape=jax.ShapeDtypeStruct((2, rows, width), F32),
        in_specs=[SMEM] * 3 + [VMEM] * 2,
        out_specs=VMEM,
        compiler_params=pltpu.CompilerParams(vmem_limit_bytes=40 << 20),
    )(plan, own_places, far_places, from_own, from_far)


def own_terms_kernel(plan, places, total, m0, m1, m2, m3, out_hbm, out, sems, *, n):
    out[...] = total[...]
    for c in range(2):
        for k, ref in enumerate((m0, m1, m2, m3)):
            add_window(out, places, plan[ORDER + k], c, ref[c].astype(F32), n)
        pltpu.make_async_copy(out.at[c], out_hbm.at[c], sems.at[c]).start()
    for c in range(2):
        pltpu.make_async_copy(out.at[c], out_hbm.at[c], sems.at[c]).wait()


def own_terms(plan, places, total, mids):
    return pl.pallas_call(
        functools.partial(own_terms_kernel, n=mids[0].shape[-1]),
        out_shape=jax.ShapeDtypeStruct(total.shape, F32),
        in_specs=[SMEM] * 2 + [VMEM] * 5,
        out_specs=ANY,
        scratch_shapes=[pltpu.VMEM(total.shape, F32), pltpu.SemaphoreType.DMA((2,))],
        compiler_params=pltpu.CompilerParams(vmem_limit_bytes=40 << 20),
    )(plan, places, total, *mids)


def shifted(block, distance):
    size = lax.axis_size("lat")
    return lax.ppermute(block, "lat", [(i, (i + distance) % size) for i in range(size)])


HANDLER, POSITION, SOURCE, ORDER, OTHER, REL, ENTRY = 0, 1, 2, 3, 7, 11, 27
GOAL = (((0, 0), (1, 1), (2, 0), (3, 1)), ((1, 2), (0, 3), (3, 2), (2, 3)))


def meet(c, team, j):
    goal, inner = GOAL[c][j]
    flip = inner ^ 2
    if c == 0:
        return inner if (team - goal) % 4 in (0, 1) else flip
    return inner if (team - goal) % 4 in (0, 3) else flip


def place_of(c, d):
    v = (d + 2 * c) % 16
    return v // 4, v % 4


def position_at(c, team, inner):
    found = [j for j in range(4) if meet(c, team, j) == inner]
    assert len(found) == 1
    return found[0]


def device_of(c, team, inner):
    return (4 * team + inner - 2 * c) % 16


@functools.lru_cache
def make_plan():
    out = np.zeros((2, 16, 48), np.int32)
    for c in range(2):
        for d in range(16):
            team, inner = place_of(c, d)
            j = position_at(c, team, inner)
            row = out[c, d]
            row[HANDLER] = GOAL[c][j] == (team, inner)
            row[POSITION] = j
            row[SOURCE] = (team - GOAL[c][j][0]) % 4
            other = place_of(1 - c, d)
            for k in range(4):
                row[ORDER + k] = position_at(c, team, inner ^ k)
                row[OTHER + k] = position_at(1 - c, other[0], other[1] ^ k)
            for s in range(16):
                there, at = place_of(c, s)
                row[REL + s] = (there - team) % 4
                row[ENTRY + s] = at ^ meet(c, there, j)
    return out


def permute(block, route):
    depth, lat = lax.axis_size("depth"), lax.axis_size("lat")
    pairs = []
    for d in range(depth):
        for m in range(lat):
            to = route(m % 2, *place_of(m % 2, d))
            if to is not None:
                pairs.append((d * lat + m, device_of(m % 2, *to) * lat + m))
    return lax.ppermute(block, ("depth", "lat"), pairs)


def within(block, k):
    return permute(block, lambda c, team, inner: (team, inner ^ k))


def towards(block, k):
    def route(c, team, inner):
        goal = GOAL[c][position_at(c, team, inner)]
        return goal if (team - goal[0]) % 4 == k else None
    return permute(block, route)


def away(block, k):
    def route(c, team, inner):
        j = position_at(c, team, inner)
        there = (team + k) % 4
        return (there, meet(c, there, j)) if GOAL[c][j] == (team, inner) else None
    return permute(block, route)


def on_device(object_slices, probe, positions, measured):
    n = probe.shape[-1]
    rows, width = object_slices.shape[2:]
    depth_size = lax.axis_size("depth")
    d = lax.axis_index("depth")
    m = lax.axis_index("lat")
    plan = lax.dynamic_slice(jnp.asarray(make_plan()), (m % 2, d, 0), (1, 1, 48)).reshape(48)
    tile = object_slices[0]

    tile_bf = tile.astype(BF)
    ahead = shifted(tile_bf, -1)
    mine = own_windows(positions, tile_bf, n)
    behind = shifted(mine, 1)
    mid_places = shifted(positions, 1)
    mid_places, ahead, behind = lax.optimization_barrier((mid_places, ahead, behind))
    parts = merge(plan, mid_places, behind, tile_bf, ahead, n)

    measured, late_positions, parts = lax.optimization_barrier((measured, positions, parts))
    far_places = shifted(late_positions, 2)
    target = shifted(lax.dynamic_index_in_dim(measured, plan[OTHER], 0, False), 1)

    message = jnp.stack([parts[0]] + [within(parts[k], k) for k in (1, 2, 3)])
    messages = [message] + [towards(message, k) for k in (1, 2, 3)]
    tables = make_tables(n, depth_size)
    wave = roll_probe(plan, mid_places, probe, rows)
    wave, source, far_places = lax.optimization_barrier((wave, [plan[SOURCE] == k for k in (1, 2, 3)], far_places))
    terms = tuple(chain(plan, wave, target, messages, tables))

    def home(pieces):
        block = pieces[0]
        for k in (2, 1, 3):
            block = jnp.where(source[k - 1], away(pieces[k], k), block)
        return block

    near_block = home(terms[:4])
    far_block = home(terms[4:])
    mixed = jnp.stack([near_block[0]] + [within(near_block[k], k) for k in (1, 2, 3)])
    mids = [far_block[0]] + [within(far_block[k], k) for k in (1, 2, 3)]
    from_own = shifted(mixed, -1)
    from_far = shifted(mixed, 1)
    total = halo_terms(plan, positions, far_places, from_own, from_far, width)
    return own_terms(plan, mid_places, total, mids)[None]


def solution(mesh):
    return jax.shard_map(
        on_device,
        mesh=mesh,
        in_specs=(P("depth", None, "lat", None), P(), P("lat", None), P("lat", None, None)),
        out_specs=P("depth", None, "lat", None),
        check_vma=False,
    )
```
